128 devices in a mesh: gx: 16 (over z, y), gy: 8 (over x, core).
Axes of the slice: x: 4, y: 4, z: 4, core: 2. Of those that a mesh axis runs over, the one named last changes fastest.
Arguments:
- features: bfloat16 [16, 8, 64, 2048], P('gx', 'gy'), may hold values from -6 to 6
- counts: int32 [16, 8], P('gx', 'gy'), may hold values from 1 to 4, as said below
- sub_rows: int32 [16, 8, 27, 2048], P('gx', 'gy'), may hold values from 0 to 2047, as said below
- sub_from: int32 [16, 8, 27, 2048], P('gx', 'gy'), may hold values from 0 to 9, as said below
- down_map: int32 [16, 8, 2, 2048], P('gx', 'gy'), may hold values from 0 to 1088, as said below
- w_sub: bfloat16 [27, 64, 64], replicated, may hold values from -0.15625 to 0.15625
- w_down: bfloat16 [8, 64, 64], replicated, may hold values from -0.75 to 0.75
- cotangent: bfloat16 [16, 8, 64, 512], P('gx', 'gy'), may hold values from -6 to 6
Outputs:
- coarse_out: bfloat16 [16, 8, 64, 512], P('gx', 'gy')
- grad_features: bfloat16 [16, 8, 64, 2048], P('gx', 'gy')
- grad_w_sub: float32 [27, 64, 64], replicated
- grad_w_down: float32 [8, 64, 64], replicated
The draws below stay inside these ranges and needn't reach their ends.
Inputs may be any that keep to these rules, and one draw needn't show every extreme that they name: Active voxel blocks of a tile; the first 512 * counts rows of a tile are live, the others padded. `sub_from`: offset k stands for the step (k // 9 - 1, k // 3 % 3 - 1, k % 3 - 1). Value d < 9 names the tile d // 3 - 1 steps along gx and d % 3 - 1 along gy, which exists; d is 4 (the same tile) or 3 * (k // 9) + k // 3 % 3, and differs from 4 only for output rows below 512. 9 means no source. Padded rows have no source; a live row is its own source at offset 13. `sub_rows`: the source voxel's row in the tile named by sub_from: where that tile is the same one, a row of the same block of 512 rows as the output row; where it is another one, a row below 512; 0 where there is no source. `down_map`: row 0: below 512 a coarse row of the same tile, and then for the fine row r one of the coarse rows (r // 512) * 128 to (r // 512 + 1) * 128 - 1; 512 + d * 64 + j (d not 4, j below 64) coarse row j of the tile d // 3 - 1 steps along gx and d % 3 - 1 along gy, which exists, used only by fine rows below 512; 1088 exactly on padded rows. Row 1: the kernel offset of the stride-2 convolution, 0 on padded rows.
All inputs are finite; a program needn't handle non-finite values.
Results may differ from the reference program's by a relative error of at most 0.0052.
Values may be sent and summed in bfloat16 or wider, within the bound.
No kernel may reach another device: no remote copies, remote signals or barrier semaphores. Data moves between devices by JAX's collectives and lax.ppermute only.
A program may use at most 64 MiB of HBM per device.

```python
import jax
import jax.numpy as jnp
from jax import lax

C = 64
VB = 512
BLK_DEV = 4
TX = 16
TY = 8
ROWS = 2048
BND_BLK = 1
BND = 512
CROWS = 512
CB = 64


def tile_counts(key):
    spread = BLK_DEV - BND_BLK
    first_key, second_key, third_key = jax.random.split(jax.random.fold_in(key, 11), 3)
    factor_one = jax.random.randint(first_key, (TX * TY,), 0, spread + 1)
    factor_two = jax.random.randint(second_key, (TX * TY,), 0, spread + 1)
    values = BND_BLK + factor_one * factor_two // spread
    chosen = jax.random.randint(third_key, (), 0, TX * TY)
    places = jnp.arange(TX * TY)
    values = jnp.where(places == chosen, BLK_DEV, values)
    values = jnp.where(places == (chosen + 1) % (TX * TY), BND_BLK, values)
    return values.reshape(TX, TY).astype(jnp.int32)


def kernel_lists(key):
    tile_count = tile_counts(key)
    live_rows = (tile_count * VB)[:, :, None, None]
    row_ids = jnp.arange(ROWS)[None, None, None, :]
    offsets = jnp.arange(27)[None, None, :, None]
    step_x = offsets // 9 - 1
    step_y = offsets // 3 % 3 - 1
    tile_x = jnp.arange(TX)[:, None, None, None]
    tile_y = jnp.arange(TY)[None, :, None, None]
    exists = (tile_x + step_x >= 0) & (tile_x + step_x < TX) & (tile_y + step_y >= 0) & (tile_y + step_y < TY)
    exists = exists & ((step_x != 0) | (step_y != 0))
    key_list = jax.random.split(jax.random.fold_in(key, 23), 4)
    full_shape = (TX, TY, 27, ROWS)
    local_row = row_ids // VB * VB + jax.random.randint(key_list[0], full_shape, 0, VB)
    present = jax.random.randint(key_list[1], full_shape, 0, 10) < 6
    remote = (jax.random.randint(key_list[2], full_shape, 0, 2) == 0) & exists & (row_ids < BND)
    border_row = jax.random.randint(key_list[3], full_shape, 0, BND)
    centre = offsets == 13
    direction = (step_x + 1) * 3 + (step_y + 1)
    is_live = row_ids < live_rows
    has_source = (present | centre) & is_live
    rows_out = jnp.where(centre, row_ids + 0 * local_row, jnp.where(remote, border_row, local_row))
    from_out = jnp.where(remote & jnp.logical_not(centre), direction + 0 * local_row, 4)
    rows_out = jnp.where(has_source, rows_out, 0)
    from_out = jnp.where(has_source, from_out, 9)
    return (rows_out.astype(jnp.int32), from_out.astype(jnp.int32))


def draw_counts(key, part):
    return tile_counts(key)


def draw_sub_rows(key, part):
    return kernel_lists(key)[0]


def draw_sub_from(key, part):
    return kernel_lists(key)[1]


def draw_down_map(key, part):
    tile_count = tile_counts(key)
    live_rows = (tile_count * VB)[:, :, None]
    row_ids = jnp.arange(ROWS)[None, None, :]
    key_list = jax.random.split(jax.random.fold_in(key, 37), 5)
    full_shape = (TX, TY, ROWS)
    kernel_off = jax.random.randint(key_list[0], full_shape, 0, 8)
    local_slot = row_ids // VB * (VB // 4) + jax.random.randint(key_list[1], full_shape, 0, VB // 4)
    direction = jax.random.randint(key_list[2], full_shape, 0, 8)
    direction = direction + (direction >= 4).astype(jnp.int32)
    step_x = direction // 3 - 1
    step_y = direction % 3 - 1
    tile_x = jnp.arange(TX)[:, None, None]
    tile_y = jnp.arange(TY)[None, :, None]
    exists = (tile_x + step_x >= 0) & (tile_x + step_x < TX) & (tile_y + step_y >= 0) & (tile_y + step_y < TY)
    crossing = (jax.random.randint(key_list[3], full_shape, 0, 5) < 2) & exists & (row_ids < BND)
    border_slot = jax.random.randint(key_list[4], full_shape, 0, CB)
    target = jnp.where(crossing, CROWS + direction * CB + border_slot, local_slot)
    is_live = row_ids < live_rows
    target = jnp.where(is_live, target, CROWS + 9 * CB)
    kernel_off = jnp.where(is_live, kernel_off, 0)
    return jnp.stack([target, kernel_off], axis=2).astype(jnp.int32)


def block_scale(own_key, dims, cuts, smallest, high):
    def one(dim, blocks):
        heights = jax.random.uniform(jax.random.fold_in(jax.random.fold_in(own_key, 6), dim), (blocks,), jnp.float32, smallest / len(cuts), high / len(cuts))
        return jnp.repeat(jnp.exp(heights), dims[dim] // blocks).reshape((-1,) + (1,) * (len(dims) - dim - 1))

    level = one(*cuts[0])
    for cut in cuts[1:]:
        level = level * one(*cut)
    return level


def noise(stream_key, extent, scale, bound, cuts=(), held_as=jnp.bfloat16):
    values = jax.random.normal(stream_key, extent, jnp.float32) * scale
    if len(cuts) > 0:
        values = block_scale(stream_key, extent, cuts, -0.22, 0.18) * values
    return jnp.clip(values, min=-bound, max=bound).astype(held_as)


def setup_inputs(seed: int = 0) -> dict:
    seeds = jax.random.split(jax.random.key(seed), 9)
    return {
        "features": noise(seeds[0], (TX, TY, C, ROWS), 1.0, 6.0, ((0, 16), (1, 8))),
        "counts": draw_counts(jax.random.fold_in(seeds[8], 71), 0),
        "sub_rows": draw_sub_rows(jax.random.fold_in(seeds[8], 71), 0),
        "sub_from": draw_sub_from(jax.random.fold_in(seeds[8], 71), 0),
        "down_map": draw_down_map(jax.random.fold_in(seeds[8], 71), 0),
        "w_sub": noise(seeds[5], (27, C, C), (27 * C) ** -0.5, 0.15625),
        "w_down": noise(seeds[6], (8, C, C), C ** -0.5, 0.75),
        "cotangent": noise(seeds[7], (TX, TY, C, CROWS), 1.0, 6.0, ((0, 16), (1, 8))),
    }


def gather_slabs(border):
    padded = jnp.pad(border, ((1, 1), (1, 1), (0, 0), (0, 0)))
    pieces = [padded[first:first + TX, second:second + TY] for first in range(3) for second in range(3)]
    return jnp.concatenate(pieces, axis=3)


def return_slabs(slabs, width):
    rounded = lax.optimization_barrier(slabs.astype(jnp.bfloat16)).astype(jnp.float32)
    shaped = rounded.reshape(TX, TY, C, 3, 3, width)
    padded = jnp.pad(shaped, ((1, 1), (1, 1), (0, 0), (0, 0), (0, 0), (0, 0)))
    total = jnp.zeros((TX, TY, C, width), jnp.float32)
    for first in range(3):
        for second in range(3):
            total = total + padded[2 - first:2 - first + TX, 2 - second:2 - second + TY, :, first, second, :]
    return total


def source_index(rows_map, from_map):
    absent_index = ROWS + 9 * BND
    halo_index = ROWS + from_map * BND + rows_map
    merged = jnp.where(from_map == 4, rows_map, jnp.where(from_map == 9, absent_index, halo_index))
    return merged.astype(jnp.int32)


def tile_work(tile_inputs, w_sub, w_down):
    feat_tile, feat_halo, grad_tile, grad_halo, tile_count, rows_map, from_map, coarse_map = tile_inputs
    padding = jnp.zeros((C, 128), jnp.bfloat16)
    feat_table = jnp.concatenate([feat_tile, feat_halo, padding], axis=1)
    grad_table = jnp.concatenate([grad_tile, grad_halo, padding], axis=1)
    live_mask = (jnp.arange(ROWS) < tile_count * VB).astype(jnp.float32)
    indices = source_index(rows_map, from_map)
    pre_act = jnp.zeros((C, ROWS), jnp.float32)
    for offset in range(27):
        source = jnp.take(feat_table, indices[offset], axis=1)
        pre_act = pre_act + jnp.dot(w_sub[offset], source, preferred_element_type=jnp.float32)
    sigmoid_v = jax.nn.sigmoid(pre_act)
    hidden = (pre_act * sigmoid_v * live_mask).astype(jnp.bfloat16)
    target = coarse_map[0].astype(jnp.int32)
    kernel_off = coarse_map[1]
    upstream = jnp.take(grad_table, target, axis=1)
    contrib = jnp.zeros((C, ROWS), jnp.float32)
    grad_hidden = jnp.zeros((C, ROWS), jnp.float32)
    grad_down = []
    for offset in range(8):
        chosen = (kernel_off == offset)[None, :]
        picked_h = jnp.where(chosen, hidden, jnp.zeros((), jnp.bfloat16))
        picked_g = jnp.where(chosen, upstream, jnp.zeros((), jnp.bfloat16))
        contrib = contrib + jnp.dot(w_down[offset], picked_h, preferred_element_type=jnp.float32)
        grad_hidden = grad_hidden + jnp.dot(w_down[offset].T, picked_g, preferred_element_type=jnp.float32)
        grad_down.append(jnp.dot(picked_g, hidden.T, preferred_element_type=jnp.float32))
    coarse_acc = jnp.zeros((C, CROWS + 9 * CB + 1), jnp.float32).at[:, target].add(contrib)
    grad_pre = (grad_hidden * sigmoid_v * (1.0 + pre_act * (1.0 - sigmoid_v)) * live_mask).astype(jnp.bfloat16)
    feat_acc = jnp.zeros((C, ROWS + 9 * BND + 1), jnp.float32)
    grad_sub = []
    for offset in range(27):
        source = jnp.take(feat_table, indices[offset], axis=1)
        grad_sub.append(jnp.dot(grad_pre, source.T, preferred_element_type=jnp.float32))
        spread = jnp.dot(w_sub[offset].T, grad_pre, preferred_element_type=jnp.float32)
        feat_acc = feat_acc.at[:, indices[offset]].add(spread)
    return coarse_acc[:, :CROWS + 9 * CB], feat_acc[:, :ROWS + 9 * BND], jnp.stack(grad_sub), jnp.stack(grad_down)


def reference(features, counts, sub_rows, sub_from, down_map, w_sub, w_down, cotangent):
    feat_halo = gather_slabs(features[:, :, :, :BND])
    grad_halo = gather_slabs(cotangent[:, :, :, :CB])
    tiles = TX * TY

    def by_tile(array):
        return array.reshape((tiles,) + array.shape[2:])

    inputs = (by_tile(features), by_tile(feat_halo), by_tile(cotangent), by_tile(grad_halo),
              counts.reshape(tiles), by_tile(sub_rows), by_tile(sub_from), by_tile(down_map))
    coarse_acc, feat_acc, grad_sub, grad_down = lax.map(lambda tile_inputs: tile_work(tile_inputs, w_sub, w_down), inputs)
    scale = float(ROWS * TX * TY) ** -0.5
    grad_w_sub = jnp.sum(grad_sub, axis=0) * scale
    grad_w_down = jnp.sum(grad_down, axis=0) * scale
    coarse_acc = coarse_acc.reshape(TX, TY, C, CROWS + 9 * CB)
    incoming = return_slabs(coarse_acc[..., CROWS:], CB)
    coarse_out = coarse_acc[..., :CROWS].at[..., :CB].add(incoming).astype(jnp.bfloat16)
    feat_acc = feat_acc.reshape(TX, TY, C, ROWS + 9 * BND)
    incoming_feat = return_slabs(feat_acc[..., ROWS:], BND)
    grad_local = feat_acc[..., :ROWS].at[..., :BND].add(incoming_feat)
    live_mask = (jnp.arange(ROWS)[None, None, None, :] < (counts * VB)[:, :, None, None]).astype(jnp.float32)
    grad_features = (grad_local * live_mask).astype(jnp.bfloat16)
    return (coarse_out, grad_features, grad_w_sub, grad_w_down)
```

```python
import functools
import jax
import jax.numpy as jnp
from jax import lax
from jax.experimental import pallas as pl
from jax.sharding import PartitionSpec as P
from jax.experimental.pallas import tpu as pltpu

VB = 512
ROWS = 2048
CROWS = 512
CB = 64
C = 64
K = 27
KC = K * C
L = 256
H = VB // L
CQ = 128
EDGE = 640
WIDE = VB + 2 * CB
HALF = (KC + 8 * C) // 2
PIECE = 16
BF = jnp.bfloat16
F32 = jnp.float32
DIRS = [3 * (k // 9) + k // 3 % 3 for k in range(K)]


def mm(a, b):
    return jnp.dot(a, b, preferred_element_type=F32)


def mm_nt(a, b):
    return lax.dot_general(a, b, (((1,), (1,)), ((), ())), preferred_element_type=F32)


def pick(cond):
    return jnp.where(cond, jnp.ones((), BF), jnp.zeros((), BF))


def block_work(remote, first, base, refs):
    (feat, rows, frm, dmap, grad, halo, w_cat, w_t, wd_cat, wd_t, hot, source, spread) = refs
    slots = 2 * H if remote else H
    row_v = rows[...]
    frm_v = frm[...]
    if remote:
        joint = jnp.where(frm_v == 4, row_v, jnp.where(frm_v == 9, -1, row_v + VB))
    else:
        joint = jnp.where(frm_v == 4, row_v - base, -1)
    high = joint >> (L.bit_length() - 1)
    low = (joint & (L - 1)).astype(F32).astype(BF)
    low_ids = lax.broadcasted_iota(jnp.int32, (L, VB), 0).astype(F32).astype(BF)
    local = jnp.concatenate([feat[:, i * L:(i + 1) * L] for i in range(H)], axis=0)
    for k in range(K):
        one_hot = pick(low[k:k + 1, :] == low_ids)
        hot[k] = one_hot
        parts = [mm(local, one_hot)]
        if remote and DIRS[k] != 4:
            slab = halo[DIRS[k] % 3][DIRS[k] // 3, :, 0:VB]
            slab = jnp.concatenate([slab[:, i * L:(i + 1) * L] for i in range(H)], axis=0)
            parts.append(mm(slab, one_hot))
        high_k = high[k:k + 1, :]
        got = jnp.zeros((C, VB), F32)
        for j, part in enumerate(parts):
            for i in range(H):
                got = jnp.where(high_k == j * H + i, part[i * C:(i + 1) * C, :], got)
        source[k * C:(k + 1) * C, :] = got.astype(BF)
    pre = mm(w_cat[...], source[...])
    sig = jax.nn.sigmoid(pre)
    hidden = (pre * sig).astype(BF)
    target = dmap[0:1, :]
    kind = dmap[1:2, :]
    coarse_rel = jnp.where(target < CROWS, target - base // 4, -1)
    pick_own = pick(coarse_rel == lax.broadcasted_iota(jnp.int32, (CQ, VB), 0))
    zero = jnp.zeros((), BF)
    kinds = [kind == i for i in range(8)]
    picked_h = jnp.concatenate([jnp.where(m, hidden, zero) for m in kinds], axis=0)
    contrib = mm(wd_cat[...], picked_h)
    c_hi = contrib.astype(BF)
    c_lo = (contrib - c_hi.astype(F32)).astype(BF)
    split = jnp.concatenate([c_hi, c_lo], axis=0)
    own = mm_nt(split, pick_own)
    coarse = own[:C] + own[C:]
    up = mm(grad[...], pick_own)
    edge = None
    if remote:
        edge_ids = lax.broadcasted_iota(jnp.int32, (EDGE, VB), 0)
        pick_edge = pick((target - CROWS) == edge_ids)
        edge_grad = jnp.concatenate([halo[d % 3][d // 3, :, VB:VB + CB] for d in range(9)] + [jnp.zeros((C, EDGE - 9 * CB), BF)], axis=1)
        edge_grad = jnp.where(lax.broadcasted_iota(jnp.int32, (C, EDGE), 1) < 9 * CB, edge_grad, zero)
        up = up + mm(edge_grad, pick_edge)
        both = mm_nt(split, pick_edge)
        edge = both[:C] + both[C:]
    up = up.astype(BF)
    picked_g = jnp.concatenate([jnp.where(m, up, zero) for m in kinds], axis=0)
    grad_hidden = mm(wd_t[...], picked_g)
    grad_down = mm_nt(picked_g, hidden)
    grad_pre = (grad_hidden * sig * (1.0 + pre * (1.0 - sig))).astype(BF)
    grad_sub = mm_nt(source[...], grad_pre)
    for k in range(K):
        high_k = high[k:k + 1, :]
        count = slots if (remote and DIRS[k] != 4) else H
        masked = jnp.concatenate([jnp.where(high_k == i, grad_pre, zero) for i in range(count)], axis=0)
        out = mm_nt(masked, hot[k]).astype(BF)
        for i in range(count):
            spread[k * C:(k + 1) * C, i * L:(i + 1) * L] = out[i * C:(i + 1) * C, :]
    gfeat = mm(w_t[...], spread[:, 0:VB])
    outward = []
    if remote:
        for d in range(9):
            ks = [k for k in range(K) if DIRS[k] == d]
            if d == 4:
                outward.append(jnp.zeros((C, VB), F32))
            else:
                a, b = ks[0] * C, (ks[-1] + 1) * C
                outward.append(mm(w_t[:, a:b], spread[a:b, VB:2 * VB]))
    return coarse, gfeat, grad_sub, grad_down, edge, outward


def local_kernel(counts, feat, rows, frm, dmap, grad, w_sub, w_down,
                 coarse_o, gfeat_o, gsub_o, gdown_o, w_cat, w_t, wd_cat, wd_t, hot, source, spread):
    i = pl.program_id(0)

    @pl.when(i == 0)
    def _():
        w_cat[...] = jnp.concatenate([w_sub[k] for k in range(K)], axis=1)
        w_t[...] = w_sub[...].reshape(KC, C).T
        wd_cat[...] = jnp.concatenate([w_down[k] for k in range(8)], axis=1)
        wd_t[...] = w_down[...].reshape(8 * C, C).T
        gsub_o[...] = jnp.zeros_like(gsub_o)
        gdown_o[...] = jnp.zeros_like(gdown_o)

    @pl.when(i + 1 < counts[0])
    def _():
        refs = (feat, rows, frm, dmap, grad, None, w_cat, w_t, wd_cat, wd_t, hot, source, spread)
        coarse, gfeat, gsub, gdown, _, _ = block_work(False, False, (i + 1) * VB, refs)
        coarse_o[...] = coarse.astype(BF)
        gfeat_o[...] = gfeat.astype(BF)
        gsub_o[...] += gsub
        gdown_o[...] += gdown

    @pl.when(i + 1 >= counts[0])
    def _():
        coarse_o[...] = jnp.zeros_like(coarse_o)
        gfeat_o[...] = jnp.zeros_like(gfeat_o)


def full(shape):
    return pl.BlockSpec(shape, lambda i: (0,) * len(shape))


def local_call(counts, feat, rows, frm, dmap, grad, w_sub, w_down):
    sd = jax.ShapeDtypeStruct
    return pl.pallas_call(
        local_kernel,
        grid=(3,),
        in_specs=[
            pl.BlockSpec(memory_space=pltpu.SMEM),
            pl.BlockSpec((C, VB), lambda i: (0, i + 1)),
            pl.BlockSpec((K, VB), lambda i: (0, i + 1)),
            pl.BlockSpec((K, VB), lambda i: (0, i + 1)),
            pl.BlockSpec((2, VB), lambda i: (0, i + 1)),
            pl.BlockSpec((C, CQ), lambda i: (0, i + 1)),
            full((K, C, C)),
            full((8, C, C)),
        ],
        out_specs=[
            pl.BlockSpec((C, CQ), lambda i: (0, i + 1)),
            pl.BlockSpec((C, VB), lambda i: (0, i + 1)),
            full((KC, C)),
            full((8 * C, C)),
            full((C, KC)),
            full((C, KC)),
            full((C, 8 * C)),
            full((C, 8 * C)),
        ],
        out_shape=[
            sd((C, CROWS), BF), sd((C, ROWS), BF), sd((KC, C), F32), sd((8 * C, C), F32),
            sd((C, KC), BF), sd((C, KC), BF), sd((C, 8 * C), BF), sd((C, 8 * C), BF),
        ],
        scratch_shapes=[
            pltpu.VMEM((K, L, VB), BF),
            pltpu.VMEM((KC, VB), BF),
            pltpu.VMEM((KC, VB), BF),
        ],
        compiler_params=pltpu.CompilerParams(vmem_limit_bytes=48 << 20),
        name="local_blocks",
    )(counts, feat, rows, frm, dmap, grad, w_sub, w_down)


def border_kernel(feat, rows, frm, dmap, grad, below, column, above, w_cat, w_t, wd_cat, wd_t, gsub, gdown,
                  coarse_o, gfeat_o, packed_o, mid_o, down_o, up_o, hot, source, spread):
    refs = (feat, rows, frm, dmap, grad, (below, column, above), w_cat, w_t, wd_cat, wd_t, hot, source, spread)
    coarse, gfeat, dsub, ddown, edge, outward = block_work(True, True, 0, refs)
    coarse_o[...] = coarse
    gfeat_o[...] = gfeat
    whole = jnp.concatenate([gsub[...] + dsub, gdown[...] + ddown], axis=0)
    packed_o[0:HALF, :] = jnp.concatenate([whole[:HALF], whole[HALF:]], axis=1).astype(BF)
    packed_o[HALF:, :] = jnp.zeros((packed_o.shape[0] - HALF, 2 * C), BF)
    for d in range(9):
        out = (down_o, mid_o, up_o)[d % 3]
        out[d // 3, :, 0:VB] = outward[d].astype(out.dtype)
        tail = jnp.concatenate([edge[:, d * CB:(d + 1) * CB], jnp.zeros((C, CB), F32)], axis=1)
        out[d // 3, :, VB:] = tail.astype(out.dtype)


def border_call(feat, rows, frm, dmap, grad, below, column, above, w_cat, w_t, wd_cat, wd_t, gsub, gdown):
    sd = jax.ShapeDtypeStruct
    count = lax.axis_size("gx") * lax.axis_size("gy")
    return pl.pallas_call(
        border_kernel,
        grid=(1,),
        in_specs=[
            pl.BlockSpec((C, VB), lambda i: (0, 0)),
            pl.BlockSpec((K, VB), lambda i: (0, 0)),
            pl.BlockSpec((K, VB), lambda i: (0, 0)),
            pl.BlockSpec((2, VB), lambda i: (0, 0)),
            pl.BlockSpec((C, CQ), lambda i: (0, 0)),
            full((3, C, WIDE)), full((3, C, WIDE)), full((3, C, WIDE)),
            full((C, KC)), full((C, KC)), full((C, 8 * C)), full((C, 8 * C)),
            full((KC, C)), full((8 * C, C)),
        ],
        out_specs=[
            full((C, CQ)), full((C, VB)), full((count * PIECE, 2 * C)),
            full((3, C, WIDE)), full((3, C, WIDE)), full((3, C, WIDE)),
        ],
        out_shape=[
            sd((C, CQ), F32), sd((C, VB), F32), sd((count * PIECE, 2 * C), BF),
            sd((3, C, WIDE), F32), sd((3, C, WIDE), BF), sd((3, C, WIDE), BF),
        ],
        scratch_shapes=[
            pltpu.VMEM((K, L, VB), BF),
            pltpu.VMEM((KC, VB), BF),
            pltpu.VMEM((KC, 2 * VB), BF),
        ],
        compiler_params=pltpu.CompilerParams(vmem_limit_bytes=48 << 20),
        name="border_block",
    )(feat, rows, frm, dmap, grad, below, column, above, w_cat, w_t, wd_cat, wd_t, gsub, gdown)


def finish_kernel(coarse_i, gfeat_i, coarse, gfeat, total, left, right, coarse_o, gfeat_o):
    inc = total[...] + left[...].astype(F32) + right[...].astype(F32)
    gfeat_o[...] = (gfeat[...] + inc[:, 0:VB]).astype(BF)
    coarse_o[:, 0:CB] = (coarse[:, 0:CB] + inc[:, VB:VB + CB]).astype(BF)
    coarse_o[:, CB:] = coarse[:, CB:].astype(BF)


def finish_call(coarse_all, gfeat_all, coarse, gfeat, total, left, right):
    sd = jax.ShapeDtypeStruct
    return pl.pallas_call(
        finish_kernel,
        grid=(1,),
        in_specs=[
            pl.BlockSpec(memory_space=pl.ANY),
            pl.BlockSpec(memory_space=pl.ANY),
            full((C, CQ)), full((C, VB)), full((C, WIDE)), full((C, WIDE)), full((C, WIDE)),
        ],
        out_specs=[pl.BlockSpec((C, CQ), lambda i: (0, 0)), pl.BlockSpec((C, VB), lambda i: (0, 0))],
        out_shape=[sd((C, CROWS), BF), sd((C, ROWS), BF)],
        input_output_aliases={0: 0, 1: 1},
        name="add_incoming",
    )(coarse_all, gfeat_all, coarse, gfeat, total, left, right)


def weights_kernel(scale, packed, gsub_o, gdown_o):
    whole = packed[...].astype(F32) * scale
    for k in range(K):
        r = k * C
        part = whole[r:r + C, 0:C] if r + C <= HALF else None
        if part is None:
            if r >= HALF:
                part = whole[r - HALF:r - HALF + C, C:2 * C]
            else:
                part = jnp.concatenate([whole[r:HALF, 0:C], whole[0:r + C - HALF, C:2 * C]], axis=0)
        gsub_o[k] = part.T
    for k in range(8):
        r = KC + k * C - HALF
        gdown_o[k] = whole[r:r + C, C:2 * C]


def weights_call(scale, packed):
    sd = jax.ShapeDtypeStruct
    return pl.pallas_call(
        functools.partial(weights_kernel, scale),
        grid=(1,),
        in_specs=[pl.BlockSpec((HALF, 2 * C), lambda i: (0, 0))],
        out_specs=[full((K, C, C)), full((8, C, C))],
        out_shape=[sd((K, C, C), F32), sd((8, C, C), F32)],
        name="unpack_weights",
    )(packed)


def ring(block, axis, step):
    n = lax.axis_size(axis)
    return lax.ppermute(block, axis, [(i, (i + step) % n) for i in range(n)])


def shards(features, counts, sub_rows, sub_from, down_map, w_sub, w_down, cotangent):
    feat = features[0, 0]
    grad = cotangent[0, 0]
    rows, frm, dmap = sub_rows[0, 0], sub_from[0, 0], down_map[0, 0]
    nx, ny = lax.axis_size("gx"), lax.axis_size("gy")
    count = nx * ny
    border = jnp.concatenate([feat[:, :VB], grad[:, :CB], jnp.zeros((C, CB), BF)], axis=1)
    column = jnp.stack([ring(border, "gx", 1), border, ring(border, "gx", -1)])
    below, above = ring(column, "gy", 1), ring(column, "gy", -1)
    coarse_all, gfeat_all, gsub, gdown, w_cat, w_t, wd_cat, wd_t = local_call(
        counts.reshape(1), feat, rows, frm, dmap, grad, w_sub, w_down)
    coarse, gfeat, packed, mid, down, up = border_call(
        feat, rows, frm, dmap, grad, below, column, above, w_cat, w_t, wd_cat, wd_t, gsub, gdown)
    from_up, from_down = ring(down, "gy", -1), ring(up, "gy", 1)
    total = mid + from_up.astype(F32) + from_down.astype(F32)
    from_right = ring(total[0].astype(BF), "gx", -1)
    from_left = ring(total[2].astype(BF), "gx", 1)
    pieces = lax.all_to_all(packed.reshape(count, -1, 2 * C), ("gx", "gy"), 0, 0, tiled=True)
    summed = jnp.sum(pieces.astype(F32), axis=0).astype(BF)
    spread = jnp.broadcast_to(summed[None], pieces.shape)
    gathered = lax.all_to_all(spread, ("gx", "gy"), 0, 0, tiled=True).reshape(-1, 2 * C)
    grad_w_sub, grad_w_down = weights_call(float(ROWS * count) ** -0.5, gathered)
    coarse_out, grad_features = finish_call(coarse_all, gfeat_all, coarse, gfeat, total[1], from_left, from_right)
    return coarse_out[None, None], grad_features[None, None], grad_w_sub, grad_w_down


def solution(mesh):
    tile = P("gx", "gy", None, None)
    return jax.shard_map(
        shards,
        mesh=mesh,
        in_specs=(tile, P("gx", "gy"), tile, tile, tile, P(), P(), tile),
        out_specs=(tile, tile, P(), P()),
        check_vma=False,
    )
```

```python
import functools
import jax
import jax.numpy as jnp
from jax import lax
from jax.experimental import pallas as pl
from jax.sharding import PartitionSpec as P
from jax.experimental.pallas import tpu as pltpu

VB = 512
ROWS = 2048
CROWS = 512
CB = 64
C = 64
K = 27
KC = K * C
L = 256
H = VB // L
CQ = 128
EDGE = 640
WIDE = VB + 2 * CB
HALF = (KC + 8 * C) // 2
PAIRS = 5
PIECE = 2 * PAIRS
BF = jnp.bfloat16
F32 = jnp.float32
DIRS = [3 * (k // 9) + k // 3 % 3 for k in range(K)]


def mm(a, b):
    return jnp.dot(a, b, preferred_element_type=F32)


def mm_nt(a, b):
    return lax.dot_general(a, b, (((1,), (1,)), ((), ())), preferred_element_type=F32)


def pick(cond):
    return jnp.where(cond, jnp.ones((), BF), jnp.zeros((), BF))


def block_work(remote, base, refs):
    (feat, rows, frm, dmap, grad, halo, w_cat, w_t, wd_cat, wd_t, hot, source, spread) = refs
    slots = 2 * H if remote else H
    row_v = rows[...]
    frm_v = frm[...]
    if remote:
        joint = jnp.where(frm_v == 4, row_v, jnp.where(frm_v == 9, -1, row_v + VB))
    else:
        joint = jnp.where(frm_v == 4, row_v - base, -1)
    high = joint >> (L.bit_length() - 1)
    low = (joint & (L - 1)).astype(F32).astype(BF)
    low_ids = lax.broadcasted_iota(jnp.int32, (L, VB), 0).astype(F32).astype(BF)
    local = jnp.concatenate([feat[:, i * L:(i + 1) * L] for i in range(H)], axis=0)
    for k in range(K):
        one_hot = pick(low[k:k + 1, :] == low_ids)
        hot[k] = one_hot
        parts = [mm(local, one_hot)]
        if remote and DIRS[k] != 4:
            slab = halo[DIRS[k] % 3][DIRS[k] // 3, :, 0:VB]
            slab = jnp.concatenate([slab[:, i * L:(i + 1) * L] for i in range(H)], axis=0)
            parts.append(mm(slab, one_hot))
        high_k = high[k:k + 1, :]
        got = jnp.zeros((C, VB), F32)
        for j, part in enumerate(parts):
            for i in range(H):
                got = jnp.where(high_k == j * H + i, part[i * C:(i + 1) * C, :], got)
        source[k * C:(k + 1) * C, :] = got.astype(BF)
    pre = mm(w_cat[...], source[...])
    sig = jax.nn.sigmoid(pre)
    hidden = (pre * sig).astype(BF)
    target = dmap[0:1, :]
    kind = dmap[1:2, :]
    coarse_rel = jnp.where(target < CROWS, target - base // 4, -1)
    pick_own = pick(coarse_rel == lax.broadcasted_iota(jnp.int32, (CQ, VB), 0))
    zero = jnp.zeros((), BF)
    kinds = [kind == i for i in range(8)]
    picked_h = jnp.concatenate([jnp.where(m, hidden, zero) for m in kinds], axis=0)
    contrib = mm(wd_cat[...], picked_h)
    c_hi = contrib.astype(BF)
    c_lo = (contrib - c_hi.astype(F32)).astype(BF)
    split = jnp.concatenate([c_hi, c_lo], axis=0)
    own = mm_nt(split, pick_own)
    coarse = own[:C] + own[C:]
    up = mm(grad[...], pick_own)
    edge = None
    if remote:
        edge_ids = lax.broadcasted_iota(jnp.int32, (EDGE, VB), 0)
        pick_edge = pick((target - CROWS) == edge_ids)
        edge_grad = jnp.concatenate([halo[d % 3][d // 3, :, VB:VB + CB] for d in range(9)] + [jnp.zeros((C, EDGE - 9 * CB), BF)], axis=1)
        edge_grad = jnp.where(lax.broadcasted_iota(jnp.int32, (C, EDGE), 1) < 9 * CB, edge_grad, zero)
        up = up + mm(edge_grad, pick_edge)
        both = mm_nt(split, pick_edge)
        edge = both[:C] + both[C:]
    up = up.astype(BF)
    picked_g = jnp.concatenate([jnp.where(m, up, zero) for m in kinds], axis=0)
    grad_hidden = mm(wd_t[...], picked_g)
    grad_down = mm_nt(picked_g, hidden)
    grad_pre = (grad_hidden * sig * (1.0 + pre * (1.0 - sig))).astype(BF)
    grad_sub = mm_nt(source[...], grad_pre)
    for k in range(K):
        high_k = high[k:k + 1, :]
        count = slots if (remote and DIRS[k] != 4) else H
        masked = jnp.concatenate([jnp.where(high_k == i, grad_pre, zero) for i in range(count)], axis=0)
        out = mm_nt(masked, hot[k]).astype(BF)
        for i in range(count):
            spread[k * C:(k + 1) * C, i * L:(i + 1) * L] = out[i * C:(i + 1) * C, :]
    gfeat = mm(w_t[...], spread[:, 0:VB])
    outward = []
    if remote:
        for d in range(9):
            ks = [k for k in range(K) if DIRS[k] == d]
            if d == 4:
                outward.append(jnp.zeros((C, VB), F32))
            else:
                a, b = ks[0] * C, (ks[-1] + 1) * C
                outward.append(mm(w_t[:, a:b], spread[a:b, VB:2 * VB]))
    return coarse, gfeat, grad_sub, grad_down, edge, outward


def prepare_weights(w_sub, w_down, w_cat, w_t, wd_cat, wd_t):
    w_cat[...] = jnp.concatenate([w_sub[k] for k in range(K)], axis=1)
    w_t[...] = w_sub[...].reshape(KC, C).T
    wd_cat[...] = jnp.concatenate([w_down[k] for k in range(8)], axis=1)
    wd_t[...] = w_down[...].reshape(8 * C, C).T


def one_local(block, counts, feat, rows, frm, dmap, grad, weights, outs, scratch):
    coarse_o, gfeat_o, gsub_o, gdown_o = outs

    @pl.when(block < counts[0])
    def _():
        refs = (feat, rows, frm, dmap, grad, None) + weights + scratch
        coarse, gfeat, gsub, gdown, _, _ = block_work(False, block * VB, refs)
        coarse_o[...] = coarse.astype(BF)
        gfeat_o[...] = gfeat.astype(BF)
        gsub_o[...] += gsub
        gdown_o[...] += gdown

    @pl.when(block >= counts[0])
    def _():
        coarse_o[...] = jnp.zeros_like(coarse_o)
        gfeat_o[...] = jnp.zeros_like(gfeat_o)


def first_kernel(counts, feat, rows, frm, dmap, grad, w_sub, w_down,
                 coarse_o, gfeat_o, gsub_o, gdown_o, w_cat, w_t, wd_cat, wd_t, hot, source, spread):
    prepare_weights(w_sub, w_down, w_cat, w_t, wd_cat, wd_t)
    gsub_o[...] = jnp.zeros_like(gsub_o)
    gdown_o[...] = jnp.zeros_like(gdown_o)
    one_local(1, counts, feat, rows, frm, dmap, grad, (w_cat, w_t, wd_cat, wd_t),
              (coarse_o, gfeat_o, gsub_o, gdown_o), (hot, source, spread))


def rest_kernel(counts, feat, rows, frm, dmap, grad, w_cat, w_t, wd_cat, wd_t, gsub, gdown, coarse_a, gfeat_a,
                coarse_o, gfeat_o, gsub_o, gdown_o, hot, source, spread):
    i = pl.program_id(0)

    @pl.when(i == 0)
    def _():
        gsub_o[...] = gsub[...]
        gdown_o[...] = gdown[...]

    one_local(i + 2, counts, feat, rows, frm, dmap, grad, (w_cat, w_t, wd_cat, wd_t),
              (coarse_o, gfeat_o, gsub_o, gdown_o), (hot, source, spread))


def full(shape):
    return pl.BlockSpec(shape, lambda i: (0,) * len(shape))


def columns(shape, first):
    return pl.BlockSpec(shape, lambda i: (0, i + first))


def table_specs(first):
    return [columns((C, VB), first), columns((K, VB), first), columns((K, VB), first),
            columns((2, VB), first), columns((C, CQ), first)]


def work_scratch(width):
    return [pltpu.VMEM((K, L, VB), BF), pltpu.VMEM((KC, VB), BF), pltpu.VMEM((KC, width), BF)]


WEIGHTS = [(C, KC), (C, KC), (C, 8 * C), (C, 8 * C)]
LIMIT = pltpu.CompilerParams(vmem_limit_bytes=26 << 20)
SMALL = pltpu.CompilerParams(vmem_limit_bytes=8 << 20)


def first_call(counts, feat, rows, frm, dmap, grad, w_sub, w_down):
    sd = jax.ShapeDtypeStruct
    return pl.pallas_call(
        first_kernel,
        grid=(1,),
        in_specs=[pl.BlockSpec(memory_space=pltpu.SMEM)] + table_specs(1) + [full((K, C, C)), full((8, C, C))],
        out_specs=[columns((C, CQ), 1), columns((C, VB), 1), full((KC, C)), full((8 * C, C))]
        + [full(w) for w in WEIGHTS],
        out_shape=[sd((C, CROWS), BF), sd((C, ROWS), BF), sd((KC, C), F32), sd((8 * C, C), F32)]
        + [sd(w, BF) for w in WEIGHTS],
        scratch_shapes=work_scratch(VB),
        compiler_params=LIMIT,
        name="first_local_block",
    )(counts, feat, rows, frm, dmap, grad, w_sub, w_down)


def rest_call(counts, feat, rows, frm, dmap, grad, weights, gsub, gdown, coarse_all, gfeat_all):
    sd = jax.ShapeDtypeStruct
    return pl.pallas_call(
        rest_kernel,
        grid=(2,),
        in_specs=[pl.BlockSpec(memory_space=pltpu.SMEM)] + table_specs(2) + [full(w) for w in WEIGHTS]
        + [full((KC, C)), full((8 * C, C)), pl.BlockSpec(memory_space=pl.ANY), pl.BlockSpec(memory_space=pl.ANY)],
        out_specs=[columns((C, CQ), 2), columns((C, VB), 2), full((KC, C)), full((8 * C, C))],
        out_shape=[sd((C, CROWS), BF), sd((C, ROWS), BF), sd((KC, C), F32), sd((8 * C, C), F32)],
        scratch_shapes=work_scratch(VB),
        input_output_aliases={12: 0, 13: 1},
        compiler_params=LIMIT,
        name="other_local_blocks",
    )(counts, feat, rows, frm, dmap, grad, *weights, gsub, gdown, coarse_all, gfeat_all)


def border_pack_kernel(feat, grad, out, sems):
    a = pltpu.make_async_copy(feat.at[:, 0:VB], out.at[:, 0:VB], sems.at[0])
    b = pltpu.make_async_copy(grad.at[:, 0:CQ], out.at[:, VB:], sems.at[1])
    a.start()
    b.start()
    a.wait()
    b.wait()


def border_pack(feat, grad):
    return pl.pallas_call(
        border_pack_kernel,
        in_specs=[pl.BlockSpec(memory_space=pltpu.HBM), pl.BlockSpec(memory_space=pltpu.HBM)],
        out_specs=pl.BlockSpec(memory_space=pltpu.VMEM),
        out_shape=jax.ShapeDtypeStruct((C, WIDE), BF),
        scratch_shapes=[pltpu.SemaphoreType.DMA((2,))],
        compiler_params=SMALL,
        name="pack_border",
    )(feat, grad)


def sum_kernel(pieces, out):
    rows = pieces.shape[0]
    span = 4 * PIECE
    total = jnp.sum(pieces[...].astype(F32).reshape(rows // span, span, 2 * C), axis=0)
    mine = total[0:PIECE]
    for i in range(1, 4):
        mine = mine + total[i * PIECE:(i + 1) * PIECE]
    tiled = jnp.concatenate([mine] * 8, axis=0).astype(BF)
    for i in range(rows // (8 * PIECE)):
        out[i * 8 * PIECE:(i + 1) * 8 * PIECE, :] = tiled


def sum_call(pieces):
    return pl.pallas_call(
        sum_kernel,
        grid=(1,),
        in_specs=[full(pieces.shape)],
        out_specs=full(pieces.shape),
        out_shape=jax.ShapeDtypeStruct(pieces.shape, BF),
        compiler_params=SMALL,
        name="sum_pieces",
    )(pieces)


def border_kernel(feat, rows, frm, dmap, grad, below, column, above, w_cat, w_t, wd_cat, wd_t, gsub, gdown,
                  coarse_o, gfeat_o, packed_o, mid_o, down_o, up_o, hot, source, spread):
    refs = (feat, rows, frm, dmap, grad, (below, column, above), w_cat, w_t, wd_cat, wd_t, hot, source, spread)
    coarse, gfeat, dsub, ddown, edge, outward = block_work(True, 0, refs)
    coarse_o[...] = coarse
    gfeat_o[...] = gfeat
    whole = jnp.concatenate([gsub[...] + dsub, gdown[...] + ddown], axis=0)
    packed_o[0:HALF, :] = jnp.concatenate([whole[:HALF], whole[HALF:]], axis=1).astype(BF)
    packed_o[HALF:, :] = jnp.zeros((packed_o.shape[0] - HALF, 2 * C), BF)
    for d in range(9):
        out = (down_o, mid_o, up_o)[d % 3]
        out[d // 3, :, 0:VB] = outward[d].astype(out.dtype)
        tail = jnp.concatenate([edge[:, d * CB:(d + 1) * CB], jnp.zeros((C, CB), F32)], axis=1)
        out[d // 3, :, VB:] = tail.astype(out.dtype)


def border_call(feat, rows, frm, dmap, grad, below, column, above, w_cat, w_t, wd_cat, wd_t, gsub, gdown):
    sd = jax.ShapeDtypeStruct
    count = lax.axis_size("gx") * lax.axis_size("gy")
    return pl.pallas_call(
        border_kernel,
        grid=(1,),
        in_specs=[
            pl.BlockSpec((C, VB), lambda i: (0, 0)),
            pl.BlockSpec((K, VB), lambda i: (0, 0)),
            pl.BlockSpec((K, VB), lambda i: (0, 0)),
            pl.BlockSpec((2, VB), lambda i: (0, 0)),
            pl.BlockSpec((C, CQ), lambda i: (0, 0)),
            full((3, C, WIDE)), full((3, C, WIDE)), full((3, C, WIDE)),
            full((C, KC)), full((C, KC)), full((C, 8 * C)), full((C, 8 * C)),
            full((KC, C)), full((8 * C, C)),
        ],
        out_specs=[
            full((C, CQ)), full((C, VB)), full((count * PIECE, 2 * C)),
            full((3, C, WIDE)), full((3, C, WIDE)), full((3, C, WIDE)),
        ],
        out_shape=[
            sd((C, CQ), F32), sd((C, VB), F32), sd((count * PIECE, 2 * C), BF),
            sd((3, C, WIDE), F32), sd((3, C, WIDE), BF), sd((3, C, WIDE), BF),
        ],
        scratch_shapes=[
            pltpu.VMEM((K, L, VB), BF),
            pltpu.VMEM((KC, VB), BF),
            pltpu.VMEM((KC, 2 * VB), BF),
        ],
        compiler_params=pltpu.CompilerParams(vmem_limit_bytes=26 << 20),
        name="border_block",
    )(feat, rows, frm, dmap, grad, below, column, above, w_cat, w_t, wd_cat, wd_t, gsub, gdown)


def finish_kernel(coarse_i, gfeat_i, coarse, gfeat, total, left, right, coarse_o, gfeat_o):
    inc = total[...] + left[...].astype(F32) + right[...].astype(F32)
    gfeat_o[...] = (gfeat[...] + inc[:, 0:VB]).astype(BF)
    coarse_o[:, 0:CB] = (coarse[:, 0:CB] + inc[:, VB:VB + CB]).astype(BF)
    coarse_o[:, CB:] = coarse[:, CB:].astype(BF)


def finish_call(coarse_all, gfeat_all, coarse, gfeat, total, left, right):
    sd = jax.ShapeDtypeStruct
    return pl.pallas_call(
        finish_kernel,
        grid=(1,),
        in_specs=[
            pl.BlockSpec(memory_space=pl.ANY),
            pl.BlockSpec(memory_space=pl.ANY),
            full((C, CQ)), full((C, VB)), full((C, WIDE)), full((C, WIDE)), full((C, WIDE)),
        ],
        out_specs=[pl.BlockSpec((C, CQ), lambda i: (0, 0)), pl.BlockSpec((C, VB), lambda i: (0, 0))],
        out_shape=[sd((C, CROWS), BF), sd((C, ROWS), BF)],
        input_output_aliases={0: 0, 1: 1},
        compiler_params=SMALL,
        name="add_incoming",
    )(coarse_all, gfeat_all, coarse, gfeat, total, left, right)


def weights_kernel(scale, packed, gsub_o, gdown_o):
    whole = packed[...].astype(F32) * scale
    for k in range(K):
        r = k * C
        part = whole[r:r + C, 0:C] if r + C <= HALF else None
        if part is None:
            if r >= HALF:
                part = whole[r - HALF:r - HALF + C, C:2 * C]
            else:
                part = jnp.concatenate([whole[r:HALF, 0:C], whole[0:r + C - HALF, C:2 * C]], axis=0)
        gsub_o[k] = part.T
    for k in range(8):
        r = KC + k * C - HALF
        gdown_o[k] = whole[r:r + C, C:2 * C]


def weights_call(scale, packed):
    sd = jax.ShapeDtypeStruct
    return pl.pallas_call(
        functools.partial(weights_kernel, scale),
        grid=(1,),
        in_specs=[pl.BlockSpec((HALF, 2 * C), lambda i: (0, 0))],
        out_specs=[full((K, C, C)), full((8, C, C))],
        out_shape=[sd((K, C, C), F32), sd((8, C, C), F32)],
        compiler_params=SMALL,
        name="unpack_weights",
    )(packed)


def ring(block, axis, step):
    n = lax.axis_size(axis)
    return lax.ppermute(block, axis, [(i, (i + step) % n) for i in range(n)])


def shards(features, counts, sub_rows, sub_from, down_map, w_sub, w_down, cotangent):
    feat = features[0, 0]
    grad = cotangent[0, 0]
    rows, frm, dmap = sub_rows[0, 0], sub_from[0, 0], down_map[0, 0]
    nx, ny = lax.axis_size("gx"), lax.axis_size("gy")
    count = nx * ny
    border = border_pack(feat, grad)
    from_before, from_after = ring(border, "gx", 1), ring(border, "gx", -1)
    counts = counts.reshape(1)
    coarse_all, gfeat_all, gsub, gdown, *weights = first_call(counts, feat, rows, frm, dmap, grad, w_sub, w_down)
    from_before, from_after, gsub = lax.optimization_barrier((from_before, from_after, gsub))
    column = jnp.stack([from_before, border, from_after])
    below, above = ring(column, "gy", 1), ring(column, "gy", -1)
    coarse_all, gfeat_all, gsub, gdown = rest_call(
        counts, feat, rows, frm, dmap, grad, weights, gsub, gdown, coarse_all, gfeat_all)
    coarse, gfeat, packed, mid, down, up = border_call(
        feat, rows, frm, dmap, grad, below, column, above, *weights, gsub, gdown)
    pieces = lax.all_to_all(packed.reshape(count, PAIRS, 2, 2 * C), ("gx", "gy"), 0, 0, tiled=True)
    from_up, from_down = ring(down, "gy", -1), ring(up, "gy", 1)
    total = mid + from_up.astype(F32) + from_down.astype(F32)
    from_right = ring(total[0].astype(BF), "gx", -1)
    from_left = ring(total[2].astype(BF), "gx", 1)
    pieces, from_right, from_left = lax.optimization_barrier((pieces, from_right, from_left))
    shape = pieces.shape
    spread = sum_call(pieces.reshape(count * PIECE, 2 * C))
    gathered = lax.all_to_all(spread.reshape(shape), ("gx", "gy"), 0, 0, tiled=True).reshape(-1, 2 * C)
    coarse_out, grad_features = finish_call(coarse_all, gfeat_all, coarse, gfeat, total[1], from_left, from_right)
    grad_w_sub, grad_w_down = weights_call(float(ROWS * count) ** -0.5, gathered)
    return coarse_out[None, None], grad_features[None, None], grad_w_sub, grad_w_down


def solution(mesh):
    tile = P("gx", "gy", None, None)
    return jax.shard_map(
        shards,
        mesh=mesh,
        in_specs=(tile, P("gx", "gy"), tile, tile, tile, P(), P(), tile),
        out_specs=(tile, tile, P(), P()),
        check_vma=False,
    )
```

```python
import functools
import jax
import jax.numpy as jnp
from jax import lax
from jax.experimental import pallas as pl
from jax.sharding import PartitionSpec as P
from jax.experimental.pallas import tpu as pltpu

VB = 512
ROWS = 2048
CROWS = 512
CB = 64
C = 64
K = 27
KC = K * C
L = 256
H = VB // L
CQ = 128
EDGE = 640
WIDE = VB + 2 * CB
SUB_ROWS = (K + 1) // 2 * C
USED = SUB_ROWS + 4 * C
PAIRS = 5
PIECE = 2 * PAIRS
BF = jnp.bfloat16
F32 = jnp.float32
DIRS = [3 * (k // 9) + k // 3 % 3 for k in range(K)]


def mm(a, b):
    return jnp.dot(a, b, preferred_element_type=F32)


def mm_nt(a, b):
    return lax.dot_general(a, b, (((1,), (1,)), ((), ())), preferred_element_type=F32)


def pick(cond):
    return jnp.where(cond, jnp.ones((), BF), jnp.zeros((), BF))


def table(remote, base, rows, frm):
    row_v = rows[:, 0, :]
    frm_v = frm[:, 0, :]
    if remote:
        joint = jnp.where(frm_v == 4, row_v, jnp.where(frm_v == 9, -1, row_v + VB))
    else:
        joint = jnp.where(frm_v == 4, row_v - base, -1)
    high = joint >> (L.bit_length() - 1)
    low = jnp.where(joint < 0, -1, joint & (L - 1)).astype(F32)
    return high, low


def forward_work(remote, base, feat, rows, frm, dmap, grad, halo, w_cat, wd_cat, wd_t, source):
    high, low = table(remote, base, rows, frm)
    low = low.astype(BF)
    low_ids = lax.broadcasted_iota(jnp.int32, (L, VB), 0).astype(F32).astype(BF)
    local = jnp.concatenate([feat[:, i * L:(i + 1) * L] for i in range(H)], axis=0)
    for k in range(K):
        one_hot = pick(low[k:k + 1, :] == low_ids)
        parts = [mm(local, one_hot)]
        if remote and DIRS[k] != 4:
            slab = halo[DIRS[k] % 3][DIRS[k] // 3, :, 0:VB]
            slab = jnp.concatenate([slab[:, i * L:(i + 1) * L] for i in range(H)], axis=0)
            parts.append(mm(slab, one_hot))
        high_k = high[k:k + 1, :]
        pieces = [part[i * C:(i + 1) * C, :] for part in parts for i in range(H)]
        got = pieces[0]
        for i in range(1, len(pieces)):
            got = jnp.where(high_k == i, pieces[i], got)
        source[k * C:(k + 1) * C, :] = got.astype(BF)
    pre = mm(w_cat[...], source[...])
    sig = jax.nn.sigmoid(pre)
    hidden = (pre * sig).astype(BF)
    target = dmap[0:1, :]
    kind = dmap[1:2, :]
    coarse_rel = jnp.where(target < CROWS, target - base // 4, -1)
    pick_own = pick(coarse_rel == lax.broadcasted_iota(jnp.int32, (CQ, VB), 0))
    zero = jnp.zeros((), BF)
    kinds = [kind == i for i in range(8)]
    up = mm(grad[...], pick_own)
    if remote:
        edge_grad = [halo[d % 3][d // 3, :, VB:VB + CB] for d in range(9)] + [jnp.zeros((C, EDGE - 9 * CB), BF)]
        up = up + mm(jnp.concatenate(edge_grad, axis=1), pick_edges(target))
    up = up.astype(BF)
    picked_g = jnp.concatenate([jnp.where(m, up, zero) for m in kinds], axis=0)
    grad_hidden = mm(wd_t[...], picked_g)
    grad_pre = (grad_hidden * sig * (1.0 + pre * (1.0 - sig))).astype(BF)
    grad_sub = mm_nt(grad_pre, source[...])
    grad_down = mm_nt(picked_g, hidden)
    picked_h = jnp.concatenate([jnp.where(m, hidden, zero) for m in kinds], axis=0)
    contrib = mm(wd_cat[...], picked_h)
    c_hi = contrib.astype(BF)
    c_lo = (contrib - c_hi.astype(F32)).astype(BF)
    split = jnp.concatenate([c_hi, c_lo], axis=0)
    own = mm_nt(split, pick_own)
    return own[:C] + own[C:], grad_pre, grad_sub, grad_down, split


def pick_edges(target):
    return pick((target - CROWS) == lax.broadcasted_iota(jnp.int32, (EDGE, VB), 0))


def scatter_work(remote, base, rows, frm, grad_pre, w_t, spread):
    high, low = table(remote, base, rows, frm)
    low_t = jnp.concatenate([low, jnp.zeros((32 - K, VB), F32)], axis=0).T.astype(BF)
    lane_ids = lax.broadcasted_iota(jnp.int32, (VB, L), 1).astype(F32).astype(BF)
    zero = jnp.zeros((), BF)
    for k in range(K):
        high_k = high[k:k + 1, :]
        count = 2 * H if (remote and DIRS[k] != 4) else H
        masked = jnp.concatenate([jnp.where(high_k == i, grad_pre, zero) for i in range(count)], axis=0)
        out = mm(masked, pick(low_t[:, k:k + 1] == lane_ids)).astype(BF)
        for i in range(count):
            spread[k * C:(k + 1) * C, i * L:(i + 1) * L] = out[i * C:(i + 1) * C, :]
    return mm(w_t[...], spread[:, 0:VB])


def prepare_weights(w_sub, w_down, w_cat, w_t, wd_cat, wd_t):
    w_cat[...] = jnp.concatenate([w_sub[k] for k in range(K)], axis=1)
    w_t[...] = w_sub[...].reshape(KC, C).T
    wd_cat[...] = jnp.concatenate([w_down[k] for k in range(8)], axis=1)
    wd_t[...] = w_down[...].reshape(8 * C, C).T


def one_local(block, counts, feat, rows, frm, dmap, grad, w_cat, wd_cat, wd_t, outs, source):
    coarse_o, gpre_o, gsub_o, gdown_o = outs

    @pl.when(block < counts[0])
    def _():
        coarse, gpre, gsub, gdown, _ = forward_work(
            False, block * VB, feat, rows, frm, dmap, grad, None, w_cat, wd_cat, wd_t, source)
        coarse_o[...] = coarse.astype(BF)
        gpre_o[...] = gpre
        gsub_o[...] += gsub
        gdown_o[...] += gdown

    @pl.when(block >= counts[0])
    def _():
        coarse_o[...] = jnp.zeros_like(coarse_o)


def first_kernel(counts, feat, rows, frm, dmap, grad, w_sub, w_down,
                 coarse_o, gpre_o, gsub_o, gdown_o, w_cat, w_t, wd_cat, wd_t, source):
    prepare_weights(w_sub, w_down, w_cat, w_t, wd_cat, wd_t)
    gsub_o[...] = jnp.zeros_like(gsub_o)
    gdown_o[...] = jnp.zeros_like(gdown_o)
    one_local(1, counts, feat, rows, frm, dmap, grad, w_cat, wd_cat, wd_t,
              (coarse_o, gpre_o, gsub_o, gdown_o), source)


def rest_kernel(counts, feat, rows, frm, dmap, grad, w_cat, wd_cat, wd_t, gsub, gdown, coarse_a, gpre_a,
                coarse_o, gpre_o, gsub_o, gdown_o, source):
    i = pl.program_id(0)

    @pl.when(i == 0)
    def _():
        gsub_o[...] = gsub[...]
        gdown_o[...] = gdown[...]

    one_local(i + 2, counts, feat, rows, frm, dmap, grad, w_cat, wd_cat, wd_t,
              (coarse_o, gpre_o, gsub_o, gdown_o), source)


def local_scatter_kernel(counts, rows, frm, gpre, w_t, gfeat_o, spread):
    block = pl.program_id(0) + 1

    @pl.when(block < counts[0])
    def _():
        gfeat_o[...] = scatter_work(False, block * VB, rows, frm, gpre[...], w_t, spread).astype(BF)

    @pl.when(block >= counts[0])
    def _():
        gfeat_o[...] = jnp.zeros_like(gfeat_o)


def full(shape):
    return pl.BlockSpec(shape, lambda i: (0,) * len(shape))


def columns(shape, first):
    return pl.BlockSpec(shape, lambda i: (0, i + first))


def index_columns(first):
    return pl.BlockSpec((K, 1, VB), lambda i: (0, 0, i + first))


def table_specs(first):
    return [columns((C, VB), first), index_columns(first), index_columns(first),
            columns((2, VB), first), columns((C, CQ), first)]


LIMIT = pltpu.CompilerParams(vmem_limit_bytes=20 << 20)
SMALL = pltpu.CompilerParams(vmem_limit_bytes=8 << 20)
SOURCE = pltpu.VMEM((KC, VB), BF)


def sd(shape, dtype):
    return jax.ShapeDtypeStruct(shape, dtype)


def first_call(counts, feat, rows, frm, dmap, grad, w_sub, w_down):
    weights = [(C, KC), (C, KC), (C, 8 * C), (C, 8 * C)]
    return pl.pallas_call(
        first_kernel,
        grid=(1,),
        in_specs=[pl.BlockSpec(memory_space=pltpu.SMEM)] + table_specs(1) + [full((K, C, C)), full((8, C, C))],
        out_specs=[columns((C, CQ), 1), columns((C, VB), 1), full((C, KC)), full((8 * C, C))]
        + [full(w) for w in weights],
        out_shape=[sd((C, CROWS), BF), sd((C, ROWS), BF), sd((C, KC), F32), sd((8 * C, C), F32)]
        + [sd(w, BF) for w in weights],
        scratch_shapes=[SOURCE],
        compiler_params=LIMIT,
        name="first_local_block",
    )(counts, feat, rows, frm, dmap, grad, w_sub, w_down)


def rest_call(counts, feat, rows, frm, dmap, grad, w_cat, wd_cat, wd_t, gsub, gdown, coarse_all, gpre_all):
    return pl.pallas_call(
        rest_kernel,
        grid=(2,),
        in_specs=[pl.BlockSpec(memory_space=pltpu.SMEM)] + table_specs(2)
        + [full((C, KC)), full((C, 8 * C)), full((C, 8 * C)), full((C, KC)), full((8 * C, C)),
           pl.BlockSpec(memory_space=pl.ANY), pl.BlockSpec(memory_space=pl.ANY)],
        out_specs=[columns((C, CQ), 2), columns((C, VB), 2), full((C, KC)), full((8 * C, C))],
        out_shape=[sd((C, CROWS), BF), sd((C, ROWS), BF), sd((C, KC), F32), sd((8 * C, C), F32)],
        scratch_shapes=[SOURCE],
        input_output_aliases={11: 0, 12: 1},
        compiler_params=LIMIT,
        name="other_local_blocks",
    )(counts, feat, rows, frm, dmap, grad, w_cat, wd_cat, wd_t, gsub, gdown, coarse_all, gpre_all)


def local_scatter_call(counts, rows, frm, gpre_all, w_t):
    return pl.pallas_call(
        local_scatter_kernel,
        grid=(3,),
        in_specs=[pl.BlockSpec(memory_space=pltpu.SMEM), index_columns(1), index_columns(1),
                  columns((C, VB), 1), full((C, KC))],
        out_specs=columns((C, VB), 1),
        out_shape=sd((C, ROWS), BF),
        scratch_shapes=[SOURCE],
        compiler_params=LIMIT,
        name="local_scatter_blocks",
    )(counts, rows, frm, gpre_all, w_t)


def border_pack_kernel(feat, grad, out, sems):
    a = pltpu.make_async_copy(feat.at[:, 0:VB], out.at[:, 0:VB], sems.at[0])
    b = pltpu.make_async_copy(grad.at[:, 0:CQ], out.at[:, VB:], sems.at[1])
    a.start()
    b.start()
    a.wait()
    b.wait()


def border_pack(feat, grad):
    return pl.pallas_call(
        border_pack_kernel,
        in_specs=[pl.BlockSpec(memory_space=pltpu.HBM), pl.BlockSpec(memory_space=pltpu.HBM)],
        out_specs=pl.BlockSpec(memory_space=pltpu.VMEM),
        out_shape=jax.ShapeDtypeStruct((C, WIDE), BF),
        scratch_shapes=[pltpu.SemaphoreType.DMA((2,))],
        compiler_params=SMALL,
        name="pack_border",
    )(pltpu.with_memory_space_constraint(feat, pltpu.HBM), pltpu.with_memory_space_constraint(grad, pltpu.HBM))


def sum_kernel(pieces, out):
    rows = pieces.shape[0]
    span = 4 * PIECE
    total = jnp.sum(pieces[...].astype(F32).reshape(rows // span, span, 2 * C), axis=0)
    mine = total[0:PIECE]
    for i in range(1, 4):
        mine = mine + total[i * PIECE:(i + 1) * PIECE]
    tiled = jnp.concatenate([mine] * 8, axis=0).astype(BF)
    for i in range(rows // (8 * PIECE)):
        out[i * 8 * PIECE:(i + 1) * 8 * PIECE, :] = tiled


def sum_call(pieces):
    return pl.pallas_call(
        sum_kernel,
        grid=(1,),
        in_specs=[full(pieces.shape)],
        out_specs=full(pieces.shape),
        out_shape=jax.ShapeDtypeStruct(pieces.shape, BF),
        compiler_params=SMALL,
        name="sum_pieces",
    )(pieces)


def border_kernel(feat, rows, frm, dmap, grad, below, column, above, w_cat, wd_cat, wd_t, gsub, gdown,
                  coarse_o, packed_o, gpre_o, split_o, source):
    coarse, gpre, dsub, ddown, split = forward_work(
        True, 0, feat, rows, frm, dmap, grad, (below, column, above), w_cat, wd_cat, wd_t, source)
    coarse_o[...] = coarse
    gpre_o[...] = gpre
    split_o[...] = split
    total = gsub[...] + dsub
    for t in range(K // 2):
        packed_o[t * C:(t + 1) * C, :] = total[:, t * 2 * C:(t + 1) * 2 * C].astype(BF)
    last = jnp.concatenate([total[:, KC - C:], jnp.zeros((C, C), F32)], axis=1)
    packed_o[K // 2 * C:SUB_ROWS, :] = last.astype(BF)
    down = gdown[...] + ddown
    packed_o[SUB_ROWS:USED, :] = jnp.concatenate([down[:4 * C], down[4 * C:]], axis=1).astype(BF)
    packed_o[USED:, :] = jnp.zeros((packed_o.shape[0] - USED, 2 * C), BF)


def border_call(count, feat, rows, frm, dmap, grad, below, column, above, w_cat, wd_cat, wd_t, gsub, gdown):
    slab = full((3, C, WIDE))
    return pl.pallas_call(
        border_kernel,
        grid=(1,),
        in_specs=table_specs(0) + [slab, slab, slab, full((C, KC)), full((C, 8 * C)), full((C, 8 * C)),
                                   full((C, KC)), full((8 * C, C))],
        out_specs=[full((C, CQ)), full((count * PIECE, 2 * C)), full((C, VB)), full((2 * C, VB))],
        out_shape=[sd((C, CQ), F32), sd((count * PIECE, 2 * C), BF), sd((C, VB), BF), sd((2 * C, VB), BF)],
        scratch_shapes=[SOURCE],
        compiler_params=LIMIT,
        name="border_block",
    )(feat, rows, frm, dmap, grad, below, column, above, w_cat, wd_cat, wd_t, gsub, gdown)


def border_scatter_kernel(rows, frm, dmap, gpre, split, w_t, gfeat_o, mid_o, down_o, up_o, spread):
    gfeat_o[...] = scatter_work(True, 0, rows, frm, gpre[...], w_t, spread)
    both = mm_nt(split[...], pick_edges(dmap[0:1, :]))
    edge = both[:C] + both[C:]
    for d in range(9):
        out = (down_o, mid_o, up_o)[d % 3]
        ks = [k for k in range(K) if DIRS[k] == d]
        a, b = ks[0] * C, (ks[-1] + 1) * C
        outward = jnp.zeros((C, VB), F32) if d == 4 else mm(w_t[:, a:b], spread[a:b, VB:2 * VB])
        out[d // 3, :, 0:VB] = outward.astype(out.dtype)
        tail = jnp.concatenate([edge[:, d * CB:(d + 1) * CB], jnp.zeros((C, CB), F32)], axis=1)
        out[d // 3, :, VB:] = tail.astype(out.dtype)


def border_scatter_call(rows, frm, dmap, gpre, split, w_t):
    slab = (3, C, WIDE)
    return pl.pallas_call(
        border_scatter_kernel,
        grid=(1,),
        in_specs=[index_columns(0), index_columns(0), columns((2, VB), 0), full((C, VB)), full((2 * C, VB)),
                  full((C, KC))],
        out_specs=[full((C, VB)), full(slab), full(slab), full(slab)],
        out_shape=[sd((C, VB), F32), sd(slab, F32), sd(slab, BF), sd(slab, BF)],
        scratch_shapes=[pltpu.VMEM((KC, 2 * VB), BF)],
        compiler_params=LIMIT,
        name="border_scatter_block",
    )(rows, frm, dmap, gpre, split, w_t)


def finish_kernel(coarse_i, gfeat_i, coarse, gfeat, total, left, right, coarse_o, gfeat_o):
    inc = total[...] + left[...].astype(F32) + right[...].astype(F32)
    gfeat_o[...] = (gfeat[...] + inc[:, 0:VB]).astype(BF)
    coarse_o[:, 0:CB] = (coarse[:, 0:CB] + inc[:, VB:VB + CB]).astype(BF)
    coarse_o[:, CB:] = coarse[:, CB:].astype(BF)


def finish_call(coarse_all, gfeat_all, coarse, gfeat, total, left, right):
    return pl.pallas_call(
        finish_kernel,
        grid=(1,),
        in_specs=[
            pl.BlockSpec(memory_space=pl.ANY),
            pl.BlockSpec(memory_space=pl.ANY),
            full((C, CQ)), full((C, VB)), full((C, WIDE)), full((C, WIDE)), full((C, WIDE)),
        ],
        out_specs=[pl.BlockSpec((C, CQ), lambda i: (0, 0)), pl.BlockSpec((C, VB), lambda i: (0, 0))],
        out_shape=[sd((C, CROWS), BF), sd((C, ROWS), BF)],
        input_output_aliases={0: 0, 1: 1},
        compiler_params=SMALL,
        name="add_incoming",
    )(coarse_all, gfeat_all, coarse, gfeat, total, left, right)


def weights_kernel(scale, packed, gsub_o, gdown_o):
    for k in range(K):
        r, c = k // 2 * C, k % 2 * C
        gsub_o[k] = packed[r:r + C, c:c + C].astype(F32) * scale
    for k in range(8):
        r, c = SUB_ROWS + k % 4 * C, k // 4 * C
        gdown_o[k] = packed[r:r + C, c:c + C].astype(F32) * scale


def weights_call(scale, packed):
    return pl.pallas_call(
        functools.partial(weights_kernel, scale),
        grid=(1,),
        in_specs=[full(packed.shape)],
        out_specs=[full((K, C, C)), full((8, C, C))],
        out_shape=[sd((K, C, C), F32), sd((8, C, C), F32)],
        compiler_params=SMALL,
        name="unpack_weights",
    )(packed)


def shifted(block, axis, step):
    n = lax.axis_size(axis)
    return lax.ppermute(block, axis, [(i, i + step) for i in range(n) if 0 <= i + step < n])


def shards(features, counts, sub_rows, sub_from, down_map, w_sub, w_down, cotangent):
    feat = features[0, 0]
    grad = cotangent[0, 0]
    rows, frm, dmap = sub_rows.reshape(K, 1, ROWS), sub_from.reshape(K, 1, ROWS), down_map[0, 0]
    nx, ny = lax.axis_size("gx"), lax.axis_size("gy")
    count = nx * ny
    border = border_pack(feat, grad)
    from_before, from_after = shifted(border, "gx", 1), shifted(border, "gx", -1)
    counts = counts.reshape(1)
    coarse_all, gpre_all, gsub, gdown, w_cat, w_t, wd_cat, wd_t = first_call(
        counts, feat, rows, frm, dmap, grad, w_sub, w_down)
    from_before, from_after, gsub = lax.optimization_barrier((from_before, from_after, gsub))
    column = jnp.stack([from_before, border, from_after])
    below, above = shifted(column, "gy", 1), shifted(column, "gy", -1)
    coarse_all, gpre_all, gsub, gdown = rest_call(
        counts, feat, rows, frm, dmap, grad, w_cat, wd_cat, wd_t, gsub, gdown, coarse_all, gpre_all)
    coarse, packed, gpre, split = border_call(
        count, feat, rows, frm, dmap, grad, below, column, above, w_cat, wd_cat, wd_t, gsub, gdown)
    pieces = lax.all_to_all(packed.reshape(count, PAIRS, 2, 2 * C), ("gx", "gy"), 0, 0, tiled=True)
    gfeat, mid, down, up = border_scatter_call(rows, frm, dmap, gpre, split, w_t)
    from_up, from_down = shifted(down, "gy", -1), shifted(up, "gy", 1)
    pieces, from_up, from_down = lax.optimization_barrier((pieces, from_up, from_down))
    total = mid + from_up.astype(F32) + from_down.astype(F32)
    from_right = shifted(total[0].astype(BF), "gx", -1)
    from_left = shifted(total[2].astype(BF), "gx", 1)
    shape = pieces.shape
    spread = sum_call(pieces.reshape(count * PIECE, 2 * C))
    spread, gpre_all = lax.optimization_barrier((spread, gpre_all))
    gathered = lax.all_to_all(spread.reshape(shape), ("gx", "gy"), 0, 0, tiled=True).reshape(-1, 2 * C)
    gfeat_all = local_scatter_call(counts, rows, frm, gpre_all, w_t)
    coarse_out, grad_features = finish_call(coarse_all, gfeat_all, coarse, gfeat, total[1], from_left, from_right)
    grad_w_sub, grad_w_down = weights_call(float(ROWS * count) ** -0.5, gathered)
    return coarse_out[None, None], grad_features[None, None], grad_w_sub, grad_w_down


def solution(mesh):
    tile = P("gx", "gy", None, None)
    return jax.shard_map(
        shards,
        mesh=mesh,
        in_specs=(tile, P("gx", "gy"), tile, tile, tile, P(), P(), tile),
        out_specs=(tile, tile, P(), P()),
        check_vma=False,
    )
```

```python
import functools
import jax
import jax.numpy as jnp
from jax import lax
from jax.experimental import pallas as pl
from jax.sharding import PartitionSpec as P
from jax.experimental.pallas import tpu as pltpu

VB = 512
ROWS = 2048
CROWS = 512
CB = 64
C = 64
K = 27
KC = K * C
L = 256
H = VB // L
CQ = 128
EDGE = 640
WIDE = VB + 2 * CB
SUB_ROWS = (K + 1) // 2 * C
USED = SUB_ROWS + 4 * C
PAIRS = 5
PIECE = 2 * PAIRS
BF = jnp.bfloat16
F32 = jnp.float32
DIRS = [3 * (k // 9) + k // 3 % 3 for k in range(K)]


def mm(a, b):
    return jnp.dot(a, b, preferred_element_type=F32)


def mm_nt(a, b):
    return lax.dot_general(a, b, (((1,), (1,)), ((), ())), preferred_element_type=F32)


def pick(cond):
    return jnp.where(cond, jnp.ones((), BF), jnp.zeros((), BF))


def table(remote, base, rows, frm):
    row_v = rows[:, 0, :]
    frm_v = frm[:, 0, :]
    if remote:
        joint = jnp.where(frm_v == 4, row_v, jnp.where(frm_v == 9, -1, row_v + VB))
    else:
        joint = jnp.where(frm_v == 4, row_v - base, -1)
    high = joint >> (L.bit_length() - 1)
    low = jnp.where(joint < 0, -1, joint & (L - 1)).astype(F32)
    return high, low


def forward_work(remote, base, feat, rows, frm, dmap, grad, halo, w_cat, wd_cat, wd_t, source):
    high, low = table(remote, base, rows, frm)
    low = low.astype(BF)
    low_ids = lax.broadcasted_iota(jnp.int32, (L, VB), 0).astype(F32).astype(BF)
    local = jnp.concatenate([feat[:, i * L:(i + 1) * L] for i in range(H)], axis=0)
    for k in range(K):
        one_hot = pick(low[k:k + 1, :] == low_ids)
        parts = [mm(local, one_hot)]
        if remote and DIRS[k] != 4:
            slab = halo[DIRS[k] % 3][DIRS[k] // 3, :, 0:VB]
            slab = jnp.concatenate([slab[:, i * L:(i + 1) * L] for i in range(H)], axis=0)
            parts.append(mm(slab, one_hot))
        high_k = high[k:k + 1, :]
        pieces = [part[i * C:(i + 1) * C, :] for part in parts for i in range(H)]
        got = pieces[0]
        for i in range(1, len(pieces)):
            got = jnp.where(high_k == i, pieces[i], got)
        source[k * C:(k + 1) * C, :] = got.astype(BF)
    pre = mm(w_cat[...], source[...])
    sig = jax.nn.sigmoid(pre)
    hidden = (pre * sig).astype(BF)
    target = dmap[0:1, :]
    kind = dmap[1:2, :]
    coarse_rel = jnp.where(target < CROWS, target - base // 4, -1)
    pick_own = pick(coarse_rel == lax.broadcasted_iota(jnp.int32, (CQ, VB), 0))
    zero = jnp.zeros((), BF)
    kinds = [kind == i for i in range(8)]
    up = mm(grad[...], pick_own)
    if remote:
        edge_grad = [halo[d % 3][d // 3, :, VB:VB + CB] for d in range(9)] + [jnp.zeros((C, EDGE - 9 * CB), BF)]
        up = up + mm(jnp.concatenate(edge_grad, axis=1), pick_edges(target))
    up = up.astype(BF)
    picked_g = jnp.concatenate([jnp.where(m, up, zero) for m in kinds], axis=0)
    grad_hidden = mm(wd_t[...], picked_g)
    grad_pre = (grad_hidden * sig * (1.0 + pre * (1.0 - sig))).astype(BF)
    grad_sub = mm_nt(grad_pre, source[...])
    grad_down = mm_nt(picked_g, hidden)
    picked_h = jnp.concatenate([jnp.where(m, hidden, zero) for m in kinds], axis=0)
    contrib = mm(wd_cat[...], picked_h)
    c_hi = contrib.astype(BF)
    c_lo = (contrib - c_hi.astype(F32)).astype(BF)
    split = jnp.concatenate([c_hi, c_lo], axis=0)
    own = mm_nt(split, pick_own)
    return own[:C] + own[C:], grad_pre, grad_sub, grad_down, split


def pick_edges(target):
    return pick((target - CROWS) == lax.broadcasted_iota(jnp.int32, (EDGE, VB), 0))


def scatter_work(remote, base, rows, frm, grad_pre, w_t, spread):
    high, low = table(remote, base, rows, frm)
    low_t = jnp.concatenate([low, jnp.zeros((32 - K, VB), F32)], axis=0).T.astype(BF)
    lane_ids = lax.broadcasted_iota(jnp.int32, (VB, L), 1).astype(F32).astype(BF)
    zero = jnp.zeros((), BF)
    for k in range(K):
        high_k = high[k:k + 1, :]
        count = 2 * H if (remote and DIRS[k] != 4) else H
        masked = jnp.concatenate([jnp.where(high_k == i, grad_pre, zero) for i in range(count)], axis=0)
        out = mm(masked, pick(low_t[:, k:k + 1] == lane_ids)).astype(BF)
        for i in range(count):
            spread[k * C:(k + 1) * C, i * L:(i + 1) * L] = out[i * C:(i + 1) * C, :]
    return mm(w_t[...], spread[:, 0:VB])


def prepare_weights(w_sub, w_down, w_cat, w_t, wd_cat, wd_t):
    w_cat[...] = jnp.concatenate([w_sub[k] for k in range(K)], axis=1)
    w_t[...] = w_sub[...].reshape(KC, C).T
    wd_cat[...] = jnp.concatenate([w_down[k] for k in range(8)], axis=1)
    wd_t[...] = w_down[...].reshape(8 * C, C).T


def one_local(block, counts, feat, rows, frm, dmap, grad, w_cat, wd_cat, wd_t, outs, source):
    coarse_o, gpre_o, gsub_o, gdown_o = outs

    @pl.when(block < counts[0])
    def _():
        coarse, gpre, gsub, gdown, _ = forward_work(
            False, block * VB, feat, rows, frm, dmap, grad, None, w_cat, wd_cat, wd_t, source)
        coarse_o[...] = coarse.astype(BF)
        gpre_o[...] = gpre
        gsub_o[...] += gsub
        gdown_o[...] += gdown

    @pl.when(block >= counts[0])
    def _():
        coarse_o[...] = jnp.zeros_like(coarse_o)


def first_kernel(counts, feat, rows, frm, dmap, grad, w_sub, w_down,
                 coarse_o, gpre_o, gsub_o, gdown_o, w_cat, w_t, wd_cat, wd_t, source):
    prepare_weights(w_sub, w_down, w_cat, w_t, wd_cat, wd_t)
    gsub_o[...] = jnp.zeros_like(gsub_o)
    gdown_o[...] = jnp.zeros_like(gdown_o)
    one_local(1, counts, feat, rows, frm, dmap, grad, w_cat, wd_cat, wd_t,
              (coarse_o, gpre_o, gsub_o, gdown_o), source)


def rest_kernel(counts, feat, rows, frm, dmap, grad, w_cat, wd_cat, wd_t, gsub, gdown, coarse_a, gpre_a,
                coarse_o, gpre_o, gsub_o, gdown_o, source):
    i = pl.program_id(0)

    @pl.when(i == 0)
    def _():
        gsub_o[...] = gsub[...]
        gdown_o[...] = gdown[...]

    one_local(i + 2, counts, feat, rows, frm, dmap, grad, w_cat, wd_cat, wd_t,
              (coarse_o, gpre_o, gsub_o, gdown_o), source)


def local_scatter_kernel(counts, rows, frm, gpre, w_t, gfeat_o, spread):
    block = pl.program_id(0) + 1

    @pl.when(block < counts[0])
    def _():
        gfeat_o[...] = scatter_work(False, block * VB, rows, frm, gpre[...], w_t, spread).astype(BF)

    @pl.when(block >= counts[0])
    def _():
        gfeat_o[...] = jnp.zeros_like(gfeat_o)


def full(shape):
    return pl.BlockSpec(shape, lambda i: (0,) * len(shape))


def columns(shape, first):
    return pl.BlockSpec(shape, lambda i: (0, i + first))


def index_columns(first):
    return pl.BlockSpec((K, 1, VB), lambda i: (0, 0, i + first))


def table_specs(first):
    return [columns((C, VB), first), index_columns(first), index_columns(first),
            columns((2, VB), first), columns((C, CQ), first)]


LIMIT = pltpu.CompilerParams(vmem_limit_bytes=20 << 20)
SMALL = pltpu.CompilerParams(vmem_limit_bytes=8 << 20)
SOURCE = pltpu.VMEM((KC, VB), BF)


def sd(shape, dtype):
    return jax.ShapeDtypeStruct(shape, dtype)


def first_call(counts, feat, rows, frm, dmap, grad, w_sub, w_down):
    weights = [(C, KC), (C, KC), (C, 8 * C), (C, 8 * C)]
    return pl.pallas_call(
        first_kernel,
        grid=(1,),
        in_specs=[pl.BlockSpec(memory_space=pltpu.SMEM)] + table_specs(1) + [full((K, C, C)), full((8, C, C))],
        out_specs=[columns((C, CQ), 1), columns((C, VB), 1), full((C, KC)), full((8 * C, C))]
        + [full(w) for w in weights],
        out_shape=[sd((C, CROWS), BF), sd((C, ROWS), BF), sd((C, KC), F32), sd((8 * C, C), F32)]
        + [sd(w, BF) for w in weights],
        scratch_shapes=[SOURCE],
        compiler_params=LIMIT,
        name="first_local_block",
    )(counts, feat, rows, frm, dmap, grad, w_sub, w_down)


def rest_call(counts, feat, rows, frm, dmap, grad, w_cat, wd_cat, wd_t, gsub, gdown, coarse_all, gpre_all):
    return pl.pallas_call(
        rest_kernel,
        grid=(2,),
        in_specs=[pl.BlockSpec(memory_space=pltpu.SMEM)] + table_specs(2)
        + [full((C, KC)), full((C, 8 * C)), full((C, 8 * C)), full((C, KC)), full((8 * C, C)),
           pl.BlockSpec(memory_space=pl.ANY), pl.BlockSpec(memory_space=pl.ANY)],
        out_specs=[columns((C, CQ), 2), columns((C, VB), 2), full((C, KC)), full((8 * C, C))],
        out_shape=[sd((C, CROWS), BF), sd((C, ROWS), BF), sd((C, KC), F32), sd((8 * C, C), F32)],
        scratch_shapes=[SOURCE],
        input_output_aliases={11: 0, 12: 1},
        compiler_params=LIMIT,
        name="other_local_blocks",
    )(counts, feat, rows, frm, dmap, grad, w_cat, wd_cat, wd_t, gsub, gdown, coarse_all, gpre_all)


def local_scatter_call(counts, rows, frm, gpre_all, w_t):
    return pl.pallas_call(
        local_scatter_kernel,
        grid=(3,),
        in_specs=[pl.BlockSpec(memory_space=pltpu.SMEM), index_columns(1), index_columns(1),
                  columns((C, VB), 1), full((C, KC))],
        out_specs=columns((C, VB), 1),
        out_shape=sd((C, ROWS), BF),
        scratch_shapes=[SOURCE],
        compiler_params=LIMIT,
        name="local_scatter_blocks",
    )(counts, rows, frm, gpre_all, w_t)


def border_pack_kernel(feat, grad, out, sems):
    a = pltpu.make_async_copy(feat.at[:, 0:VB], out.at[:, 0:VB], sems.at[0])
    b = pltpu.make_async_copy(grad.at[:, 0:CQ], out.at[:, VB:], sems.at[1])
    a.start()
    b.start()
    a.wait()
    b.wait()


def border_pack(feat, grad):
    return pl.pallas_call(
        border_pack_kernel,
        in_specs=[pl.BlockSpec(memory_space=pltpu.HBM), pl.BlockSpec(memory_space=pltpu.HBM)],
        out_specs=pl.BlockSpec(memory_space=pltpu.VMEM),
        out_shape=jax.ShapeDtypeStruct((C, WIDE), BF),
        scratch_shapes=[pltpu.SemaphoreType.DMA((2,))],
        compiler_params=SMALL,
        name="pack_border",
    )(pltpu.with_memory_space_constraint(feat, pltpu.HBM), pltpu.with_memory_space_constraint(grad, pltpu.HBM))


def sum_kernel(pieces, out):
    rows = pieces.shape[0]
    span = 4 * PIECE
    total = jnp.sum(pieces[...].astype(F32).reshape(rows // span, span, 2 * C), axis=0)
    mine = total[0:PIECE]
    for i in range(1, 4):
        mine = mine + total[i * PIECE:(i + 1) * PIECE]
    tiled = jnp.concatenate([mine] * 8, axis=0).astype(BF)
    for i in range(rows // (8 * PIECE)):
        out[i * 8 * PIECE:(i + 1) * 8 * PIECE, :] = tiled


def sum_call(pieces):
    return pl.pallas_call(
        sum_kernel,
        grid=(1,),
        in_specs=[full(pieces.shape)],
        out_specs=full(pieces.shape),
        out_shape=jax.ShapeDtypeStruct(pieces.shape, BF),
        compiler_params=SMALL,
        name="sum_pieces",
    )(pieces)


def border_kernel(side, feat, rows, frm, dmap, grad, near, column, far, w_cat, wd_cat, wd_t, gsub, gdown,
                  coarse_o, packed_o, gpre_o, split_o, source, below, above):
    even = side[0] == 1
    below[...] = jnp.where(even, far[...], near[...])
    above[...] = jnp.where(even, near[...], far[...])
    coarse, gpre, dsub, ddown, split = forward_work(
        True, 0, feat, rows, frm, dmap, grad, (below, column, above), w_cat, wd_cat, wd_t, source)
    coarse_o[...] = coarse
    gpre_o[...] = gpre
    split_o[...] = split
    total = gsub[...] + dsub
    for t in range(K // 2):
        packed_o[t * C:(t + 1) * C, :] = total[:, t * 2 * C:(t + 1) * 2 * C].astype(BF)
    last = jnp.concatenate([total[:, KC - C:], jnp.zeros((C, C), F32)], axis=1)
    packed_o[K // 2 * C:SUB_ROWS, :] = last.astype(BF)
    down = gdown[...] + ddown
    packed_o[SUB_ROWS:USED, :] = jnp.concatenate([down[:4 * C], down[4 * C:]], axis=1).astype(BF)
    packed_o[USED:, :] = jnp.zeros((packed_o.shape[0] - USED, 2 * C), BF)


def border_call(count, side, feat, rows, frm, dmap, grad, near, column, far, w_cat, wd_cat, wd_t, gsub, gdown):
    slab = full((3, C, WIDE))
    return pl.pallas_call(
        border_kernel,
        grid=(1,),
        in_specs=[pl.BlockSpec(memory_space=pltpu.SMEM)] + table_specs(0) + [slab, slab, slab, full((C, KC)), full((C, 8 * C)), full((C, 8 * C)),
                                   full((C, KC)), full((8 * C, C))],
        out_specs=[full((C, CQ)), full((count * PIECE, 2 * C)), full((C, VB)), full((2 * C, VB))],
        out_shape=[sd((C, CQ), F32), sd((count * PIECE, 2 * C), BF), sd((C, VB), BF), sd((2 * C, VB), BF)],
        scratch_shapes=[SOURCE, pltpu.VMEM((3, C, WIDE), BF), pltpu.VMEM((3, C, WIDE), BF)],
        compiler_params=LIMIT,
        name="border_block",
    )(side, feat, rows, frm, dmap, grad, near, column, far, w_cat, wd_cat, wd_t, gsub, gdown)


def border_scatter_kernel(side, rows, frm, dmap, gpre, split, w_t, gfeat_o, mid_o, near_o, far_o, spread):
    gfeat_o[...] = scatter_work(True, 0, rows, frm, gpre[...], w_t, spread)
    both = mm_nt(split[...], pick_edges(dmap[0:1, :]))
    edge = both[:C] + both[C:]
    even = side[0] == 1

    def slab(d):
        a = 9 * (d // 3) + 3 * (d % 3)
        a, b = a * C, (a + 3) * C
        outward = jnp.zeros((C, VB), F32) if d == 4 else mm(w_t[:, a:b], spread[a:b, VB:2 * VB])
        return jnp.concatenate([outward, edge[:, d * CB:(d + 1) * CB], jnp.zeros((C, CB), F32)], axis=1)

    for x in range(3):
        down, up = slab(3 * x).astype(BF), slab(3 * x + 2).astype(BF)
        mid_o[x] = slab(3 * x + 1)
        near_o[x] = jnp.where(even, up, down)
        far_o[x] = jnp.where(even, down, up)


def border_scatter_call(side, rows, frm, dmap, gpre, split, w_t):
    slab = (3, C, WIDE)
    return pl.pallas_call(
        border_scatter_kernel,
        grid=(1,),
        in_specs=[pl.BlockSpec(memory_space=pltpu.SMEM), index_columns(0), index_columns(0), columns((2, VB), 0),
                  full((C, VB)), full((2 * C, VB)),
                  full((C, KC))],
        out_specs=[full((C, VB)), full(slab), full(slab), full(slab)],
        out_shape=[sd((C, VB), F32), sd(slab, F32), sd(slab, BF), sd(slab, BF)],
        scratch_shapes=[pltpu.VMEM((KC, 2 * VB), BF)],
        compiler_params=LIMIT,
        name="border_scatter_block",
    )(side, rows, frm, dmap, gpre, split, w_t)


def finish_kernel(coarse_i, gfeat_i, coarse, gfeat, total, left, right, coarse_o, gfeat_o):
    inc = total[...] + left[...].astype(F32) + right[...].astype(F32)
    gfeat_o[...] = (gfeat[...] + inc[:, 0:VB]).astype(BF)
    coarse_o[:, 0:CB] = (coarse[:, 0:CB] + inc[:, VB:VB + CB]).astype(BF)
    coarse_o[:, CB:] = coarse[:, CB:].astype(BF)


def finish_call(coarse_all, gfeat_all, coarse, gfeat, total, left, right):
    return pl.pallas_call(
        finish_kernel,
        grid=(1,),
        in_specs=[
            pl.BlockSpec(memory_space=pl.ANY),
            pl.BlockSpec(memory_space=pl.ANY),
            full((C, CQ)), full((C, VB)), full((C, WIDE)), full((C, WIDE)), full((C, WIDE)),
        ],
        out_specs=[pl.BlockSpec((C, CQ), lambda i: (0, 0)), pl.BlockSpec((C, VB), lambda i: (0, 0))],
        out_shape=[sd((C, CROWS), BF), sd((C, ROWS), BF)],
        input_output_aliases={0: 0, 1: 1},
        compiler_params=SMALL,
        name="add_incoming",
    )(coarse_all, gfeat_all, coarse, gfeat, total, left, right)


def weights_kernel(scale, packed, gsub_o, gdown_o):
    for k in range(K):
        r, c = k // 2 * C, k % 2 * C
        gsub_o[k] = packed[r:r + C, c:c + C].astype(F32) * scale
    for k in range(8):
        r, c = SUB_ROWS + k % 4 * C, k // 4 * C
        gdown_o[k] = packed[r:r + C, c:c + C].astype(F32) * scale


def weights_call(scale, packed):
    return pl.pallas_call(
        functools.partial(weights_kernel, scale),
        grid=(1,),
        in_specs=[full(packed.shape)],
        out_specs=[full((K, C, C)), full((8, C, C))],
        out_shape=[sd((K, C, C), F32), sd((8, C, C), F32)],
        compiler_params=SMALL,
        name="unpack_weights",
    )(packed)


def swapped(block, axis, first):
    n = lax.axis_size(axis)
    pairs = [(i, i + 1) for i in range(0 if first else 1, n - 1, 2)]
    return lax.ppermute(block, axis, pairs + [(b, a) for a, b in pairs])


def shards(features, counts, sub_rows, sub_from, down_map, w_sub, w_down, cotangent):
    feat = features[0, 0]
    grad = cotangent[0, 0]
    rows, frm, dmap = sub_rows.reshape(K, 1, ROWS), sub_from.reshape(K, 1, ROWS), down_map[0, 0]
    nx, ny = lax.axis_size("gx"), lax.axis_size("gy")
    count = nx * ny
    border = border_pack(feat, grad)
    even_x, even_y = lax.axis_index("gx") % 2 == 0, lax.axis_index("gy") % 2 == 0
    side = even_y.astype(jnp.int32).reshape(1)
    near, far = swapped(border, "gx", True), swapped(border, "gx", False)
    counts = counts.reshape(1)
    coarse_all, gpre_all, gsub, gdown, w_cat, w_t, wd_cat, wd_t = first_call(
        counts, *[pltpu.with_memory_space_constraint(a, pltpu.HBM) for a in (feat, rows, frm, dmap, grad, w_sub, w_down)])
    near, far, gsub = lax.optimization_barrier((near, far, gsub))
    column = jnp.stack([jnp.where(even_x, far, near), border, jnp.where(even_x, near, far)])
    near, far = swapped(column, "gy", True), swapped(column, "gy", False)
    coarse_all, gpre_all, gsub, gdown = rest_call(
        counts, feat, rows, frm, dmap, grad, w_cat, wd_cat, wd_t, gsub, gdown, coarse_all, gpre_all)
    coarse, packed, gpre, split = border_call(
        count, side, feat, rows, frm, dmap, grad, near, column, far, w_cat, wd_cat, wd_t, gsub, gdown)
    pieces = lax.all_to_all(packed.reshape(count, PAIRS, 2, 2 * C), ("gx", "gy"), 0, 0, tiled=True)
    gfeat, mid, out_near, out_far = border_scatter_call(side, rows, frm, dmap, gpre, split, w_t)
    near, far = swapped(out_near, "gy", True), swapped(out_far, "gy", False)
    pieces, near, far = lax.optimization_barrier((pieces, near, far))
    total = mid + near.astype(F32) + far.astype(F32)
    near = swapped(jnp.where(even_x, total[2], total[0]).astype(BF), "gx", True)
    far = swapped(jnp.where(even_x, total[0], total[2]).astype(BF), "gx", False)
    shape = pieces.shape
    spread = sum_call(pieces.reshape(count * PIECE, 2 * C))
    spread, gpre_all = lax.optimization_barrier((spread, gpre_all))
    gathered = lax.all_to_all(spread.reshape(shape), ("gx", "gy"), 0, 0, tiled=True).reshape(-1, 2 * C)
    gfeat_all = local_scatter_call(counts, rows, frm, gpre_all, w_t)
    coarse_out, grad_features = finish_call(coarse_all, gfeat_all, coarse, gfeat, total[1], near, far)
    grad_w_sub, grad_w_down = weights_call(float(ROWS * count) ** -0.5, gathered)
    return coarse_out[None, None], grad_features[None, None], grad_w_sub, grad_w_down


def solution(mesh):
    tile = P("gx", "gy", None, None)
    return jax.shard_map(
        shards,
        mesh=mesh,
        in_specs=(tile, P("gx", "gy"), tile, tile, tile, P(), P(), tile),
        out_specs=(tile, tile, P(), P()),
        check_vma=False,
    )
```

```python
import functools
import jax
import jax.numpy as jnp
from jax import lax
from jax.experimental import pallas as pl
from jax.sharding import PartitionSpec as P
from jax.experimental.pallas import tpu as pltpu

VB = 512
ROWS = 2048
CROWS = 512
CB = 64
C = 64
K = 27
KC = K * C
L = 256
H = VB // L
CQ = 128
EDGE = 640
WIDE = VB + 2 * CB
SUB_ROWS = (K + 1) // 2 * C
USED = SUB_ROWS + 4 * C
PAIRS = 5
PIECE = 2 * PAIRS
BF = jnp.bfloat16
F32 = jnp.float32
DIRS = [3 * (k // 9) + k // 3 % 3 for k in range(K)]


def mm(a, b):
    return jnp.dot(a, b, preferred_element_type=F32)


def mm_nt(a, b):
    return lax.dot_general(a, b, (((1,), (1,)), ((), ())), preferred_element_type=F32)


def pick(cond):
    return jnp.where(cond, jnp.ones((), BF), jnp.zeros((), BF))


def table(remote, base, rows, frm):
    row_v = rows[:, 0, :]
    frm_v = frm[:, 0, :]
    if remote:
        joint = jnp.where(frm_v == 4, row_v, jnp.where(frm_v == 9, -1, row_v + VB))
    else:
        joint = jnp.where(frm_v == 4, row_v - base, -1)
    high = joint >> (L.bit_length() - 1)
    low = jnp.where(joint < 0, -1, joint & (L - 1)).astype(F32)
    return high, low


def forward_work(remote, base, feat, rows, frm, dmap, grad, halo, w_cat, wd_cat, wd_t, source):
    high, low = table(remote, base, rows, frm)
    low = low.astype(BF)
    low_ids = lax.broadcasted_iota(jnp.int32, (L, VB), 0).astype(F32).astype(BF)
    local = jnp.concatenate([feat[:, i * L:(i + 1) * L] for i in range(H)], axis=0)
    slabs = {}
    for k in range(K):
        one_hot = pick(low[k:k + 1, :] == low_ids)
        parts = [mm(local, one_hot)]
        if remote and DIRS[k] != 4:
            if DIRS[k] not in slabs:
                slab = halo[DIRS[k] % 3][DIRS[k] // 3, :, 0:VB]
                slabs[DIRS[k]] = jnp.concatenate([slab[:, i * L:(i + 1) * L] for i in range(H)], axis=0)
            parts.append(mm(slabs[DIRS[k]], one_hot))
        high_k = high[k:k + 1, :]
        pieces = [part[i * C:(i + 1) * C, :] for part in parts for i in range(H)]
        got = pieces[0]
        for i in range(1, len(pieces)):
            got = jnp.where(high_k == i, pieces[i], got)
        source[k * C:(k + 1) * C, :] = got.astype(BF)
    pre = mm(w_cat[...], source[...])
    sig = jax.nn.sigmoid(pre)
    hidden = (pre * sig).astype(BF)
    target = dmap[0:1, :]
    kind = dmap[1:2, :]
    coarse_rel = jnp.where(target < CROWS, target - base // 4, -1)
    pick_own = pick(coarse_rel == lax.broadcasted_iota(jnp.int32, (CQ, VB), 0))
    zero = jnp.zeros((), BF)
    kinds = [kind == i for i in range(8)]
    up = mm(grad[...], pick_own)
    if remote:
        edge_grad = [halo[d % 3][d // 3, :, VB:VB + CB] for d in range(9)] + [jnp.zeros((C, EDGE - 9 * CB), BF)]
        up = up + mm(jnp.concatenate(edge_grad, axis=1), pick_edges(target))
    up = up.astype(BF)
    picked_g = jnp.concatenate([jnp.where(m, up, zero) for m in kinds], axis=0)
    grad_hidden = mm(wd_t[...], picked_g)
    grad_pre = (grad_hidden * sig * (1.0 + pre * (1.0 - sig))).astype(BF)
    grad_sub = mm_nt(grad_pre, source[...])
    grad_down = mm_nt(picked_g, hidden)
    picked_h = jnp.concatenate([jnp.where(m, hidden, zero) for m in kinds], axis=0)
    contrib = mm(wd_cat[...], picked_h)
    c_hi = contrib.astype(BF)
    c_lo = (contrib - c_hi.astype(F32)).astype(BF)
    split = jnp.concatenate([c_hi, c_lo], axis=0)
    own = mm_nt(split, pick_own)
    return own[:C] + own[C:], grad_pre, grad_sub, grad_down, split


def pick_edges(target):
    return pick((target - CROWS) == lax.broadcasted_iota(jnp.int32, (EDGE, VB), 0))


def scatter_work(remote, base, rows, frm, grad_pre, w_t, spread):
    high, low = table(remote, base, rows, frm)
    low_t = jnp.concatenate([low, jnp.zeros((32 - K, VB), F32)], axis=0).T.astype(BF)
    lane_ids = lax.broadcasted_iota(jnp.int32, (VB, L), 1).astype(F32).astype(BF)
    zero = jnp.zeros((), BF)
    for k in range(K):
        high_k = high[k:k + 1, :]
        count = 2 * H if (remote and DIRS[k] != 4) else H
        masked = jnp.concatenate([jnp.where(high_k == i, grad_pre, zero) for i in range(count)], axis=0)
        out = mm(masked, pick(low_t[:, k:k + 1] == lane_ids)).astype(BF)
        for i in range(count):
            spread[k * C:(k + 1) * C, i * L:(i + 1) * L] = out[i * C:(i + 1) * C, :]
    return mm(w_t[...], spread[:, 0:VB])


def prepare_weights(w_sub, w_down, w_cat, w_t, wd_cat, wd_t):
    w_cat[...] = jnp.concatenate([w_sub[k] for k in range(K)], axis=1)
    w_t[...] = w_sub[...].reshape(KC, C).T
    wd_cat[...] = jnp.concatenate([w_down[k] for k in range(8)], axis=1)
    wd_t[...] = w_down[...].reshape(8 * C, C).T


def one_local(block, counts, feat, rows, frm, dmap, grad, w_cat, wd_cat, wd_t, outs, source):
    coarse_o, gpre_o, gsub_o, gdown_o = outs

    @pl.when(block < counts[0])
    def _():
        coarse, gpre, gsub, gdown, _ = forward_work(
            False, block * VB, feat, rows, frm, dmap, grad, None, w_cat, wd_cat, wd_t, source)
        coarse_o[...] = coarse.astype(BF)
        gpre_o[...] = gpre
        gsub_o[...] += gsub
        gdown_o[...] += gdown

    @pl.when(block >= counts[0])
    def _():
        coarse_o[...] = jnp.zeros_like(coarse_o)


def first_kernel(counts, feat, rows, frm, dmap, grad, w_sub, w_down,
                 coarse_o, gpre_o, gsub_o, gdown_o, w_cat, w_t, wd_cat, wd_t, source):
    prepare_weights(w_sub, w_down, w_cat, w_t, wd_cat, wd_t)
    gsub_o[...] = jnp.zeros_like(gsub_o)
    gdown_o[...] = jnp.zeros_like(gdown_o)
    one_local(1, counts, feat, rows, frm, dmap, grad, w_cat, wd_cat, wd_t,
              (coarse_o, gpre_o, gsub_o, gdown_o), source)


def rest_kernel(counts, feat, rows, frm, dmap, grad, w_cat, wd_cat, wd_t, gsub, gdown, coarse_a, gpre_a,
                coarse_o, gpre_o, gsub_o, gdown_o, source):
    i = pl.program_id(0)

    @pl.when(i == 0)
    def _():
        gsub_o[...] = gsub[...]
        gdown_o[...] = gdown[...]

    one_local(i + 2, counts, feat, rows, frm, dmap, grad, w_cat, wd_cat, wd_t,
              (coarse_o, gpre_o, gsub_o, gdown_o), source)


def local_scatter_kernel(counts, rows, frm, gpre, w_t, gfeat_o, spread):
    block = pl.program_id(0) + 1

    @pl.when(block < counts[0])
    def _():
        gfeat_o[...] = scatter_work(False, block * VB, rows, frm, gpre[...], w_t, spread).astype(BF)

    @pl.when(block >= counts[0])
    def _():
        gfeat_o[...] = jnp.zeros_like(gfeat_o)


def full(shape):
    return pl.BlockSpec(shape, lambda i: (0,) * len(shape))


def columns(shape, first):
    return pl.BlockSpec(shape, lambda i: (0, i + first))


def index_columns(first):
    return pl.BlockSpec((K, 1, VB), lambda i: (0, 0, i + first))


def table_specs(first):
    return [columns((C, VB), first), index_columns(first), index_columns(first),
            columns((2, VB), first), columns((C, CQ), first)]


LIMIT = pltpu.CompilerParams(vmem_limit_bytes=20 << 20)
SMALL = pltpu.CompilerParams(vmem_limit_bytes=8 << 20)
SOURCE = pltpu.VMEM((KC, VB), BF)


def sd(shape, dtype):
    return jax.ShapeDtypeStruct(shape, dtype)


def first_call(counts, feat, rows, frm, dmap, grad, w_sub, w_down):
    weights = [(C, KC), (C, KC), (C, 8 * C), (C, 8 * C)]
    return pl.pallas_call(
        first_kernel,
        grid=(1,),
        in_specs=[pl.BlockSpec(memory_space=pltpu.SMEM)] + table_specs(1) + [full((K, C, C)), full((8, C, C))],
        out_specs=[columns((C, CQ), 1), columns((C, VB), 1), full((C, KC)), full((8 * C, C))]
        + [full(w) for w in weights],
        out_shape=[sd((C, CROWS), BF), sd((C, ROWS), BF), sd((C, KC), F32), sd((8 * C, C), F32)]
        + [sd(w, BF) for w in weights],
        scratch_shapes=[SOURCE],
        compiler_params=LIMIT,
        name="first_local_block",
    )(counts, feat, rows, frm, dmap, grad, w_sub, w_down)


def rest_call(counts, feat, rows, frm, dmap, grad, w_cat, wd_cat, wd_t, gsub, gdown, coarse_all, gpre_all):
    return pl.pallas_call(
        rest_kernel,
        grid=(2,),
        in_specs=[pl.BlockSpec(memory_space=pltpu.SMEM)] + table_specs(2)
        + [full((C, KC)), full((C, 8 * C)), full((C, 8 * C)), full((C, KC)), full((8 * C, C)),
           pl.BlockSpec(memory_space=pl.ANY), pl.BlockSpec(memory_space=pl.ANY)],
        out_specs=[columns((C, CQ), 2), columns((C, VB), 2), full((C, KC)), full((8 * C, C))],
        out_shape=[sd((C, CROWS), BF), sd((C, ROWS), BF), sd((C, KC), F32), sd((8 * C, C), F32)],
        scratch_shapes=[SOURCE],
        input_output_aliases={11: 0, 12: 1},
        compiler_params=LIMIT,
        name="other_local_blocks",
    )(counts, feat, rows, frm, dmap, grad, w_cat, wd_cat, wd_t, gsub, gdown, coarse_all, gpre_all)


def local_scatter_call(counts, rows, frm, gpre_all, w_t):
    return pl.pallas_call(
        local_scatter_kernel,
        grid=(3,),
        in_specs=[pl.BlockSpec(memory_space=pltpu.SMEM), index_columns(1), index_columns(1),
                  columns((C, VB), 1), full((C, KC))],
        out_specs=columns((C, VB), 1),
        out_shape=sd((C, ROWS), BF),
        scratch_shapes=[SOURCE],
        compiler_params=LIMIT,
        name="local_scatter_blocks",
    )(counts, rows, frm, gpre_all, w_t)


def in_hbm(array):
    return pltpu.with_memory_space_constraint(array, pltpu.HBM)


def border_pack_kernel(feat, grad, out, sems):
    a = pltpu.make_async_copy(feat.at[:, 0:VB], out.at[:, 0:VB], sems.at[0])
    b = pltpu.make_async_copy(grad.at[:, 0:CQ], out.at[:, VB:], sems.at[1])
    a.start()
    b.start()
    a.wait()
    b.wait()


def border_pack(feat, grad):
    return pl.pallas_call(
        border_pack_kernel,
        in_specs=[pl.BlockSpec(memory_space=pltpu.HBM), pl.BlockSpec(memory_space=pltpu.HBM)],
        out_specs=pl.BlockSpec(memory_space=pltpu.VMEM),
        out_shape=jax.ShapeDtypeStruct((C, WIDE), BF),
        scratch_shapes=[pltpu.SemaphoreType.DMA((2,))],
        compiler_params=SMALL,
        name="pack_border",
    )(in_hbm(feat), in_hbm(grad))


def sum_kernel(pieces, out):
    rows = pieces.shape[0]
    span = 4 * PIECE
    total = jnp.sum(pieces[...].astype(F32).reshape(rows // span, span, 2 * C), axis=0)
    mine = total[0:PIECE]
    for i in range(1, 4):
        mine = mine + total[i * PIECE:(i + 1) * PIECE]
    tiled = jnp.concatenate([mine] * 8, axis=0).astype(BF)
    for i in range(rows // (8 * PIECE)):
        out[i * 8 * PIECE:(i + 1) * 8 * PIECE, :] = tiled


def sum_call(pieces):
    return pl.pallas_call(
        sum_kernel,
        grid=(1,),
        in_specs=[full(pieces.shape)],
        out_specs=full(pieces.shape),
        out_shape=jax.ShapeDtypeStruct(pieces.shape, BF),
        compiler_params=SMALL,
        name="sum_pieces",
    )(pieces)


def border_kernel(side, feat, rows, frm, dmap, grad, near, column, far, w_cat, wd_cat, wd_t, gsub, gdown,
                  coarse_o, packed_o, gpre_o, split_o, source, below, above):
    even = side[0] == 1
    below[...] = jnp.where(even, far[...], near[...])
    above[...] = jnp.where(even, near[...], far[...])
    coarse, gpre, dsub, ddown, split = forward_work(
        True, 0, feat, rows, frm, dmap, grad, (below, column, above), w_cat, wd_cat, wd_t, source)
    coarse_o[...] = coarse
    gpre_o[...] = gpre
    split_o[...] = split
    total = gsub[...] + dsub
    for t in range(K // 2):
        packed_o[t * C:(t + 1) * C, :] = total[:, t * 2 * C:(t + 1) * 2 * C].astype(BF)
    last = jnp.concatenate([total[:, KC - C:], jnp.zeros((C, C), F32)], axis=1)
    packed_o[K // 2 * C:SUB_ROWS, :] = last.astype(BF)
    down = gdown[...] + ddown
    packed_o[SUB_ROWS:USED, :] = jnp.concatenate([down[:4 * C], down[4 * C:]], axis=1).astype(BF)
    packed_o[USED:, :] = jnp.zeros((packed_o.shape[0] - USED, 2 * C), BF)


def border_call(count, side, feat, rows, frm, dmap, grad, near, column, far, w_cat, wd_cat, wd_t, gsub, gdown):
    slab = full((3, C, WIDE))
    return pl.pallas_call(
        border_kernel,
        grid=(1,),
        in_specs=[pl.BlockSpec(memory_space=pltpu.SMEM)] + table_specs(0) + [slab, slab, slab, full((C, KC)), full((C, 8 * C)), full((C, 8 * C)),
                                   full((C, KC)), full((8 * C, C))],
        out_specs=[full((C, CQ)), full((count * PIECE, 2 * C)), full((C, VB)), full((2 * C, VB))],
        out_shape=[sd((C, CQ), F32), sd((count * PIECE, 2 * C), BF), sd((C, VB), BF), sd((2 * C, VB), BF)],
        scratch_shapes=[SOURCE, pltpu.VMEM((3, C, WIDE), BF), pltpu.VMEM((3, C, WIDE), BF)],
        compiler_params=LIMIT,
        name="border_block",
    )(side, feat, rows, frm, dmap, grad, near, column, far, w_cat, wd_cat, wd_t, gsub, gdown)


def border_scatter_kernel(side, rows, frm, dmap, gpre, split, w_t, gfeat_o, mid_o, near_o, far_o, spread):
    gfeat_o[...] = scatter_work(True, 0, rows, frm, gpre[...], w_t, spread)
    both = mm_nt(split[...], pick_edges(dmap[0:1, :]))
    edge = both[:C] + both[C:]
    even = side[0] == 1

    def slab(d):
        a = 9 * (d // 3) + 3 * (d % 3)
        a, b = a * C, (a + 3) * C
        outward = jnp.zeros((C, VB), F32) if d == 4 else mm(w_t[:, a:b], spread[a:b, VB:2 * VB])
        return jnp.concatenate([outward, edge[:, d * CB:(d + 1) * CB], jnp.zeros((C, CB), F32)], axis=1)

    for x in range(3):
        down, up = slab(3 * x).astype(BF), slab(3 * x + 2).astype(BF)
        mid_o[x] = slab(3 * x + 1)
        near_o[x] = jnp.where(even, up, down)
        far_o[x] = jnp.where(even, down, up)


def border_scatter_call(side, rows, frm, dmap, gpre, split, w_t):
    slab = (3, C, WIDE)
    return pl.pallas_call(
        border_scatter_kernel,
        grid=(1,),
        in_specs=[pl.BlockSpec(memory_space=pltpu.SMEM), index_columns(0), index_columns(0), columns((2, VB), 0),
                  full((C, VB)), full((2 * C, VB)),
                  full((C, KC))],
        out_specs=[full((C, VB)), full(slab), full(slab), full(slab)],
        out_shape=[sd((C, VB), F32), sd(slab, F32), sd(slab, BF), sd(slab, BF)],
        scratch_shapes=[pltpu.VMEM((KC, 2 * VB), BF)],
        compiler_params=LIMIT,
        name="border_scatter_block",
    )(side, rows, frm, dmap, gpre, split, w_t)


def finish_kernel(coarse_i, gfeat_i, coarse, gfeat, total, left, right, coarse_o, gfeat_o):
    inc = total[...] + left[...].astype(F32) + right[...].astype(F32)
    gfeat_o[...] = (gfeat[...] + inc[:, 0:VB]).astype(BF)
    coarse_o[:, 0:CB] = (coarse[:, 0:CB] + inc[:, VB:VB + CB]).astype(BF)
    coarse_o[:, CB:] = coarse[:, CB:].astype(BF)


def finish_call(coarse_all, gfeat_all, coarse, gfeat, total, left, right):
    return pl.pallas_call(
        finish_kernel,
        grid=(1,),
        in_specs=[
            pl.BlockSpec(memory_space=pl.ANY),
            pl.BlockSpec(memory_space=pl.ANY),
            full((C, CQ)), full((C, VB)), full((C, WIDE)), full((C, WIDE)), full((C, WIDE)),
        ],
        out_specs=[pl.BlockSpec((C, CQ), lambda i: (0, 0)), pl.BlockSpec((C, VB), lambda i: (0, 0))],
        out_shape=[sd((C, CROWS), BF), sd((C, ROWS), BF)],
        input_output_aliases={0: 0, 1: 1},
        compiler_params=SMALL,
        name="add_incoming",
    )(coarse_all, gfeat_all, coarse, gfeat, total, left, right)


def weights_kernel(scale, packed, gsub_o, gdown_o):
    for k in range(K):
        r, c = k // 2 * C, k % 2 * C
        gsub_o[k] = packed[r:r + C, c:c + C].astype(F32) * scale
    for k in range(8):
        r, c = SUB_ROWS + k % 4 * C, k // 4 * C
        gdown_o[k] = packed[r:r + C, c:c + C].astype(F32) * scale


def weights_call(scale, packed):
    return pl.pallas_call(
        functools.partial(weights_kernel, scale),
        grid=(1,),
        in_specs=[full(packed.shape)],
        out_specs=[full((K, C, C)), full((8, C, C))],
        out_shape=[sd((K, C, C), F32), sd((8, C, C), F32)],
        compiler_params=SMALL,
        name="unpack_weights",
    )(packed)


def swapped(block, axis, first):
    n = lax.axis_size(axis)
    pairs = [(i, i + 1) for i in range(0 if first else 1, n - 1, 2)]
    return lax.ppermute(block, axis, pairs + [(b, a) for a, b in pairs])


def shards(features, counts, sub_rows, sub_from, down_map, w_sub, w_down, cotangent):
    feat = features[0, 0]
    grad = cotangent[0, 0]
    rows, frm, dmap = sub_rows.reshape(K, 1, ROWS), sub_from.reshape(K, 1, ROWS), down_map[0, 0]
    nx, ny = lax.axis_size("gx"), lax.axis_size("gy")
    count = nx * ny
    border = border_pack(feat, grad)
    even_x, even_y = lax.axis_index("gx") % 2 == 0, lax.axis_index("gy") % 2 == 0
    side = even_y.astype(jnp.int32).reshape(1)
    near, far = swapped(border, "gx", True), swapped(border, "gx", False)
    counts = counts.reshape(1)
    coarse_all, gpre_all, gsub, gdown, w_cat, w_t, wd_cat, wd_t = first_call(
        counts, *[in_hbm(a) for a in (feat, rows, frm, dmap, grad, w_sub, w_down)])
    near, far, gsub = lax.optimization_barrier((near, far, gsub))
    dmap = in_hbm(dmap)
    column = jnp.stack([jnp.where(even_x, far, near), border, jnp.where(even_x, near, far)])
    near, far = swapped(column, "gy", True), swapped(column, "gy", False)
    coarse_all, gpre_all, gsub, gdown = rest_call(
        counts, feat, rows, frm, dmap, grad, w_cat, wd_cat, wd_t, gsub, gdown, coarse_all, gpre_all)
    coarse, packed, gpre, split = border_call(
        count, side, feat, rows, frm, dmap, grad, near, column, far, w_cat, wd_cat, wd_t, gsub, gdown)
    pieces = lax.all_to_all(packed.reshape(count, PAIRS, 2, 2 * C), ("gx", "gy"), 0, 0, tiled=True)
    gfeat, mid, out_near, out_far = border_scatter_call(side, rows, frm, dmap, gpre, split, w_t)
    near, far = swapped(out_near, "gy", True), swapped(out_far, "gy", False)
    shape = pieces.shape
    spread = sum_call(pieces.reshape(count * PIECE, 2 * C))
    spread, gpre_all, mid = lax.optimization_barrier((spread, gpre_all, mid))
    total = mid + near.astype(F32) + far.astype(F32)
    near = swapped(jnp.where(even_x, total[2], total[0]).astype(BF), "gx", True)
    far = swapped(jnp.where(even_x, total[0], total[2]).astype(BF), "gx", False)
    gathered = lax.all_to_all(spread.reshape(shape), ("gx", "gy"), 0, 0, tiled=True).reshape(-1, 2 * C)
    gfeat_all = local_scatter_call(counts, rows, frm, gpre_all, w_t)
    coarse_out, grad_features = finish_call(coarse_all, gfeat_all, coarse, gfeat, total[1], near, far)
    grad_w_sub, grad_w_down = weights_call(float(ROWS * count) ** -0.5, gathered)
    return coarse_out[None, None], grad_features[None, None], grad_w_sub, grad_w_down


def solution(mesh):
    tile = P("gx", "gy", None, None)
    return jax.shard_map(
        shards,
        mesh=mesh,
        in_specs=(tile, P("gx", "gy"), tile, tile, tile, P(), P(), tile),
        out_specs=(tile, tile, P(), P()),
        check_vma=False,
    )
```

```python
import functools
import jax
import jax.numpy as jnp
from jax import lax
from jax.experimental import pallas as pl
from jax.sharding import PartitionSpec as P
from jax.experimental.pallas import tpu as pltpu

VB = 512
ROWS = 2048
CROWS = 512
CB = 64
C = 64
K = 27
KC = K * C
L = 256
H = VB // L
CQ = 128
EDGE = 640
WIDE = VB + 2 * CB
SUB_ROWS = (K + 1) // 2 * C
USED = SUB_ROWS + 4 * C
PAIRS = 5
PIECE = 2 * PAIRS
BF = jnp.bfloat16
F32 = jnp.float32
DIRS = [3 * (k // 9) + k // 3 % 3 for k in range(K)]


def mm(a, b):
    return jnp.dot(a, b, preferred_element_type=F32)


def mm_nt(a, b):
    return lax.dot_general(a, b, (((1,), (1,)), ((), ())), preferred_element_type=F32)


def pick(cond):
    return jnp.where(cond, jnp.ones((), BF), jnp.zeros((), BF))


def table(remote, base, rows, frm):
    row_v = rows[:, 0, :]
    frm_v = frm[:, 0, :]
    if remote:
        joint = jnp.where(frm_v == 4, row_v, jnp.where(frm_v == 9, -1, row_v + VB))
    else:
        joint = jnp.where(frm_v == 4, row_v - base, -1)
    high = joint >> (L.bit_length() - 1)
    low = jnp.where(joint < 0, -1, joint & (L - 1)).astype(F32)
    return high, low


def forward_work(remote, base, feat, rows, frm, dmap, grad, halo, w_cat, wd_cat, wd_t, source):
    high, low = table(remote, base, rows, frm)
    low = low.astype(BF)
    low_ids = lax.broadcasted_iota(jnp.int32, (L, VB), 0).astype(F32).astype(BF)
    local = jnp.concatenate([feat[:, i * L:(i + 1) * L] for i in range(H)], axis=0)
    slabs = {}
    for k in range(K):
        one_hot = pick(low[k:k + 1, :] == low_ids)
        parts = [mm(local, one_hot)]
        if remote and DIRS[k] != 4:
            if DIRS[k] not in slabs:
                slab = halo[DIRS[k] % 3][DIRS[k] // 3, :, 0:VB]
                slabs[DIRS[k]] = jnp.concatenate([slab[:, i * L:(i + 1) * L] for i in range(H)], axis=0)
            parts.append(mm(slabs[DIRS[k]], one_hot))
        high_k = high[k:k + 1, :]
        pieces = [part[i * C:(i + 1) * C, :] for part in parts for i in range(H)]
        got = pieces[0]
        for i in range(1, len(pieces)):
            got = jnp.where(high_k == i, pieces[i], got)
        source[k * C:(k + 1) * C, :] = got.astype(BF)
    pre = mm(w_cat[...], source[...])
    sig = jax.nn.sigmoid(pre)
    hidden = (pre * sig).astype(BF)
    target = dmap[0:1, :]
    kind = dmap[1:2, :]
    coarse_rel = jnp.where(target < CROWS, target - base // 4, -1)
    pick_own = pick(coarse_rel == lax.broadcasted_iota(jnp.int32, (CQ, VB), 0))
    zero = jnp.zeros((), BF)
    kinds = [kind == i for i in range(8)]
    up = mm(grad[...], pick_own)
    if remote:
        edge_grad = [halo[d % 3][d // 3, :, VB:VB + CB] for d in range(9)] + [jnp.zeros((C, EDGE - 9 * CB), BF)]
        up = up + mm(jnp.concatenate(edge_grad, axis=1), pick_edges(target))
    up = up.astype(BF)
    picked_g = jnp.concatenate([jnp.where(m, up, zero) for m in kinds], axis=0)
    grad_hidden = mm(wd_t[...], picked_g)
    grad_pre = (grad_hidden * sig * (1.0 + pre * (1.0 - sig))).astype(BF)
    grad_sub = mm_nt(grad_pre, source[...])
    grad_down = mm_nt(picked_g, hidden)
    picked_h = jnp.concatenate([jnp.where(m, hidden, zero) for m in kinds], axis=0)
    contrib = mm(wd_cat[...], picked_h)
    c_hi = contrib.astype(BF)
    c_lo = (contrib - c_hi.astype(F32)).astype(BF)
    split = jnp.concatenate([c_hi, c_lo], axis=0)
    own = mm_nt(split, pick_own)
    return own[:C] + own[C:], grad_pre, grad_sub, grad_down, split


def pick_edges(target):
    return pick((target - CROWS) == lax.broadcasted_iota(jnp.int32, (EDGE, VB), 0))


def scatter_work(remote, base, rows, frm, grad_pre, w_t, spread):
    high, low = table(remote, base, rows, frm)
    low_t = jnp.concatenate([low, jnp.zeros((32 - K, VB), F32)], axis=0).T.astype(BF)
    lane_ids = lax.broadcasted_iota(jnp.int32, (VB, L), 1).astype(F32).astype(BF)
    zero = jnp.zeros((), BF)
    for k in range(K):
        high_k = high[k:k + 1, :]
        count = 2 * H if (remote and DIRS[k] != 4) else H
        masked = jnp.concatenate([jnp.where(high_k == i, grad_pre, zero) for i in range(count)], axis=0)
        out = mm(masked, pick(low_t[:, k:k + 1] == lane_ids)).astype(BF)
        for i in range(count):
            spread[k * C:(k + 1) * C, i * L:(i + 1) * L] = out[i * C:(i + 1) * C, :]
    return mm(w_t[...], spread[:, 0:VB])


def prepare_weights(w_sub, w_down, w_cat, w_t, wd_cat, wd_t):
    w_cat[...] = jnp.concatenate([w_sub[k] for k in range(K)], axis=1)
    w_t[...] = w_sub[...].reshape(KC, C).T
    wd_cat[...] = jnp.concatenate([w_down[k] for k in range(8)], axis=1)
    wd_t[...] = w_down[...].reshape(8 * C, C).T


def one_local(block, counts, feat, rows, frm, dmap, grad, w_cat, wd_cat, wd_t, outs, source):
    coarse_o, gpre_o, gsub_o, gdown_o = outs

    @pl.when(block < counts[0, 0])
    def _():
        coarse, gpre, gsub, gdown, _ = forward_work(
            False, block * VB, feat, rows, frm, dmap, grad, None, w_cat, wd_cat, wd_t, source)
        coarse_o[...] = coarse.astype(BF)
        gpre_o[...] = gpre
        gsub_o[...] += gsub
        gdown_o[...] += gdown

    @pl.when(block >= counts[0, 0])
    def _():
        coarse_o[...] = jnp.zeros_like(coarse_o)


def first_kernel(counts, feat, rows, frm, dmap, grad, w_sub, w_down,
                 coarse_o, gpre_o, gsub_o, gdown_o, w_cat, w_t, wd_cat, wd_t, source):
    prepare_weights(w_sub, w_down, w_cat, w_t, wd_cat, wd_t)
    gsub_o[...] = jnp.zeros_like(gsub_o)
    gdown_o[...] = jnp.zeros_like(gdown_o)
    one_local(1, counts, feat, rows, frm, dmap, grad, w_cat, wd_cat, wd_t,
              (coarse_o, gpre_o, gsub_o, gdown_o), source)


def rest_kernel(counts, feat, rows, frm, dmap, grad, w_cat, wd_cat, wd_t, gsub, gdown, coarse_a, gpre_a,
                coarse_o, gpre_o, gsub_o, gdown_o, source):
    i = pl.program_id(0)

    @pl.when(i == 0)
    def _():
        gsub_o[...] = gsub[...]
        gdown_o[...] = gdown[...]

    one_local(i + 2, counts, feat, rows, frm, dmap, grad, w_cat, wd_cat, wd_t,
              (coarse_o, gpre_o, gsub_o, gdown_o), source)


def local_scatter_kernel(counts, rows, frm, gpre, w_t, gfeat_o, spread):
    block = pl.program_id(0) + 1

    @pl.when(block < counts[0, 0])
    def _():
        gfeat_o[...] = scatter_work(False, block * VB, rows, frm, gpre[...], w_t, spread).astype(BF)

    @pl.when(block >= counts[0, 0])
    def _():
        gfeat_o[...] = jnp.zeros_like(gfeat_o)


WHOLE = pl.BlockSpec(memory_space=pltpu.VMEM)


def full(shape):
    return WHOLE


def piped(shape):
    return pl.BlockSpec(shape, lambda i: (0,) * len(shape))


def columns(shape, first):
    return pl.BlockSpec(shape, lambda i: (0, i + first))


def index_columns(first):
    return pl.BlockSpec((K, 1, VB), lambda i: (0, 0, i + first))


def table_specs(first):
    return [columns((C, VB), first), index_columns(first), index_columns(first),
            columns((2, VB), first), columns((C, CQ), first)]


LIMIT = pltpu.CompilerParams(vmem_limit_bytes=20 << 20)
SMALL = pltpu.CompilerParams(vmem_limit_bytes=8 << 20)
SOURCE = pltpu.VMEM((KC, VB), BF)


def sd(shape, dtype):
    return jax.ShapeDtypeStruct(shape, dtype)


def first_call(counts, feat, rows, frm, dmap, grad, w_sub, w_down):
    weights = [(C, KC), (C, KC), (C, 8 * C), (C, 8 * C)]
    return pl.pallas_call(
        first_kernel,
        grid=(1,),
        in_specs=[pl.BlockSpec(memory_space=pltpu.SMEM)] + table_specs(1) + [piped((K, C, C)), piped((8, C, C))],
        out_specs=[columns((C, CQ), 1), columns((C, VB), 1), full((C, KC)), full((8 * C, C))]
        + [full(w) for w in weights],
        out_shape=[sd((C, CROWS), BF), sd((C, ROWS), BF), sd((C, KC), F32), sd((8 * C, C), F32)]
        + [sd(w, BF) for w in weights],
        scratch_shapes=[SOURCE],
        compiler_params=LIMIT,
        name="first_local_block",
    )(counts, feat, rows, frm, dmap, grad, w_sub, w_down)


def rest_call(counts, feat, rows, frm, dmap, grad, w_cat, wd_cat, wd_t, gsub, gdown, coarse_all, gpre_all):
    return pl.pallas_call(
        rest_kernel,
        grid=(2,),
        in_specs=[pl.BlockSpec(memory_space=pltpu.SMEM)] + table_specs(2)
        + [full((C, KC)), full((C, 8 * C)), full((C, 8 * C)), full((C, KC)), full((8 * C, C)),
           pl.BlockSpec(memory_space=pl.ANY), pl.BlockSpec(memory_space=pl.ANY)],
        out_specs=[columns((C, CQ), 2), columns((C, VB), 2), full((C, KC)), full((8 * C, C))],
        out_shape=[sd((C, CROWS), BF), sd((C, ROWS), BF), sd((C, KC), F32), sd((8 * C, C), F32)],
        scratch_shapes=[SOURCE],
        input_output_aliases={11: 0, 12: 1},
        compiler_params=LIMIT,
        name="other_local_blocks",
    )(counts, feat, rows, frm, dmap, grad, w_cat, wd_cat, wd_t, gsub, gdown, coarse_all, gpre_all)


def local_scatter_call(counts, rows, frm, gpre_all, w_t):
    return pl.pallas_call(
        local_scatter_kernel,
        grid=(3,),
        in_specs=[pl.BlockSpec(memory_space=pltpu.SMEM), index_columns(1), index_columns(1),
                  columns((C, VB), 1), full((C, KC))],
        out_specs=columns((C, VB), 1),
        out_shape=sd((C, ROWS), BF),
        scratch_shapes=[SOURCE],
        compiler_params=LIMIT,
        name="local_scatter_blocks",
    )(counts, rows, frm, gpre_all, w_t)


def in_hbm(array):
    return pltpu.with_memory_space_constraint(array, pltpu.HBM)


def border_pack_kernel(feat, grad, out, sems):
    a = pltpu.make_async_copy(feat.at[:, 0:VB], out.at[:, 0:VB], sems.at[0])
    b = pltpu.make_async_copy(grad.at[:, 0:CQ], out.at[:, VB:], sems.at[1])
    a.start()
    b.start()
    a.wait()
    b.wait()


def border_pack(feat, grad):
    return pl.pallas_call(
        border_pack_kernel,
        in_specs=[pl.BlockSpec(memory_space=pltpu.HBM)] * 2,
        out_specs=WHOLE,
        out_shape=sd((C, WIDE), BF),
        scratch_shapes=[pltpu.SemaphoreType.DMA((2,))],
        compiler_params=SMALL,
        name="pack_border",
    )(in_hbm(feat), in_hbm(grad))


def sum_kernel(pieces, out):
    rows = pieces.shape[0]
    span = 4 * PIECE
    total = jnp.sum(pieces[...].astype(F32).reshape(rows // span, span, 2 * C), axis=0)
    mine = total[0:PIECE]
    for i in range(1, 4):
        mine = mine + total[i * PIECE:(i + 1) * PIECE]
    tiled = jnp.concatenate([mine] * 8, axis=0).astype(BF)
    for i in range(rows // (8 * PIECE)):
        out[i * 8 * PIECE:(i + 1) * 8 * PIECE, :] = tiled


def sum_call(pieces):
    return pl.pallas_call(
        sum_kernel,
        grid=(1,),
        in_specs=[full(pieces.shape)],
        out_specs=piped(pieces.shape),
        out_shape=jax.ShapeDtypeStruct(pieces.shape, BF),
        compiler_params=SMALL,
        name="sum_pieces",
    )(pieces)


def border_kernel(side, feat, rows, frm, dmap, grad, near, column, far, w_cat, wd_cat, wd_t, gsub, gdown,
                  coarse_o, packed_o, gpre_o, split_o, source, below, above):
    even = side[0] == 1
    below[...] = jnp.where(even, far[...], near[...])
    above[...] = jnp.where(even, near[...], far[...])
    coarse, gpre, dsub, ddown, split = forward_work(
        True, 0, feat, rows, frm, dmap, grad, (below, column, above), w_cat, wd_cat, wd_t, source)
    coarse_o[...] = coarse
    gpre_o[...] = gpre
    split_o[...] = split
    total = gsub[...] + dsub
    for t in range(K // 2):
        packed_o[t * C:(t + 1) * C, :] = total[:, t * 2 * C:(t + 1) * 2 * C].astype(BF)
    last = jnp.concatenate([total[:, KC - C:], jnp.zeros((C, C), F32)], axis=1)
    packed_o[K // 2 * C:SUB_ROWS, :] = last.astype(BF)
    down = gdown[...] + ddown
    packed_o[SUB_ROWS:USED, :] = jnp.concatenate([down[:4 * C], down[4 * C:]], axis=1).astype(BF)
    packed_o[USED:, :] = jnp.zeros((packed_o.shape[0] - USED, 2 * C), BF)


def border_call(count, side, feat, rows, frm, dmap, grad, near, column, far, w_cat, wd_cat, wd_t, gsub, gdown):
    slab = full((3, C, WIDE))
    return pl.pallas_call(
        border_kernel,
        grid=(1,),
        in_specs=[pl.BlockSpec(memory_space=pltpu.SMEM)] + table_specs(0) + [slab, slab, slab, full((C, KC)), full((C, 8 * C)), full((C, 8 * C)),
                                   full((C, KC)), full((8 * C, C))],
        out_specs=[full((C, CQ)), piped((count * PIECE, 2 * C)), full((C, VB)), full((2 * C, VB))],
        out_shape=[sd((C, CQ), F32), sd((count * PIECE, 2 * C), BF), sd((C, VB), BF), sd((2 * C, VB), BF)],
        scratch_shapes=[SOURCE, pltpu.VMEM((3, C, WIDE), BF), pltpu.VMEM((3, C, WIDE), BF)],
        compiler_params=LIMIT,
        name="border_block",
    )(side, feat, rows, frm, dmap, grad, near, column, far, w_cat, wd_cat, wd_t, gsub, gdown)


def border_scatter_kernel(side, rows, frm, dmap, gpre, split, w_t, gfeat_o, mid_o, near_o, far_o, spread):
    gfeat_o[...] = scatter_work(True, 0, rows, frm, gpre[...], w_t, spread)
    both = mm_nt(split[...], pick_edges(dmap[0:1, :]))
    edge = both[:C] + both[C:]
    even = side[0] == 1

    def slab(d):
        a = 9 * (d // 3) + 3 * (d % 3)
        a, b = a * C, (a + 3) * C
        outward = jnp.zeros((C, VB), F32) if d == 4 else mm(w_t[:, a:b], spread[a:b, VB:2 * VB])
        return jnp.concatenate([outward, edge[:, d * CB:(d + 1) * CB], jnp.zeros((C, CB), F32)], axis=1)

    for x in range(3):
        down, up = slab(3 * x).astype(BF), slab(3 * x + 2).astype(BF)
        mid_o[x] = slab(3 * x + 1)
        near_o[x] = jnp.where(even, up, down)
        far_o[x] = jnp.where(even, down, up)


def border_scatter_call(side, rows, frm, dmap, gpre, split, w_t):
    slab = (3, C, WIDE)
    return pl.pallas_call(
        border_scatter_kernel,
        grid=(1,),
        in_specs=[pl.BlockSpec(memory_space=pltpu.SMEM), index_columns(0), index_columns(0), columns((2, VB), 0),
                  full((C, VB)), full((2 * C, VB)),
                  full((C, KC))],
        out_specs=[full((C, VB)), full(slab), full(slab), full(slab)],
        out_shape=[sd((C, VB), F32), sd(slab, F32), sd(slab, BF), sd(slab, BF)],
        scratch_shapes=[pltpu.VMEM((KC, 2 * VB), BF)],
        compiler_params=LIMIT,
        name="border_scatter_block",
    )(side, rows, frm, dmap, gpre, split, w_t)


def finish_kernel(coarse_i, gfeat_i, coarse, gfeat, total, left, right, coarse_o, gfeat_o):
    inc = total[...] + left[...].astype(F32) + right[...].astype(F32)
    gfeat_o[...] = (gfeat[...] + inc[:, 0:VB]).astype(BF)
    coarse_o[:, 0:CB] = (coarse[:, 0:CB] + inc[:, VB:VB + CB]).astype(BF)
    coarse_o[:, CB:] = coarse[:, CB:].astype(BF)


def finish_call(coarse_all, gfeat_all, coarse, gfeat, total, left, right):
    return pl.pallas_call(
        finish_kernel,
        grid=(1,),
        in_specs=[
            pl.BlockSpec(memory_space=pl.ANY),
            pl.BlockSpec(memory_space=pl.ANY),
            full((C, CQ)), full((C, VB)), full((C, WIDE)), full((C, WIDE)), full((C, WIDE)),
        ],
        out_specs=[pl.BlockSpec((C, CQ), lambda i: (0, 0)), pl.BlockSpec((C, VB), lambda i: (0, 0))],
        out_shape=[sd((C, CROWS), BF), sd((C, ROWS), BF)],
        input_output_aliases={0: 0, 1: 1},
        compiler_params=SMALL,
        name="add_incoming",
    )(coarse_all, gfeat_all, coarse, gfeat, total, left, right)


def weights_kernel(scale, packed, gsub_o, gdown_o):
    for k in range(K):
        r, c = k // 2 * C, k % 2 * C
        gsub_o[k] = packed[r:r + C, c:c + C].astype(F32) * scale
    for k in range(8):
        r, c = SUB_ROWS + k % 4 * C, k // 4 * C
        gdown_o[k] = packed[r:r + C, c:c + C].astype(F32) * scale


def weights_call(scale, packed):
    return pl.pallas_call(
        functools.partial(weights_kernel, scale),
        grid=(1,),
        in_specs=[full(packed.shape)],
        out_specs=[piped((K, C, C)), piped((8, C, C))],
        out_shape=[sd((K, C, C), F32), sd((8, C, C), F32)],
        compiler_params=SMALL,
        name="unpack_weights",
    )(packed)


def swapped(block, axis, first):
    n = lax.axis_size(axis)
    pairs = [(i, i + 1) for i in range(0 if first else 1, n - 1, 2)]
    return lax.ppermute(block, axis, pairs + [(b, a) for a, b in pairs])


def shards(features, counts, sub_rows, sub_from, down_map, w_sub, w_down, cotangent):
    feat = features[0, 0]
    grad = cotangent[0, 0]
    rows, frm, dmap = sub_rows.reshape(K, 1, ROWS), sub_from.reshape(K, 1, ROWS), down_map[0, 0]
    nx, ny = lax.axis_size("gx"), lax.axis_size("gy")
    count = nx * ny
    border = border_pack(feat, grad)
    even_x, even_y = lax.axis_index("gx") % 2 == 0, lax.axis_index("gy") % 2 == 0
    side = even_y.astype(jnp.int32).reshape(1)
    near, far = swapped(border, "gx", True), swapped(border, "gx", False)
    coarse_all, gpre_all, gsub, gdown, w_cat, w_t, wd_cat, wd_t = first_call(
        counts, *[in_hbm(a) for a in (feat, rows, frm)], dmap, *[in_hbm(a) for a in (grad, w_sub, w_down)])
    near, far, gsub = lax.optimization_barrier((near, far, gsub))
    column = jnp.stack([jnp.where(even_x, far, near), border, jnp.where(even_x, near, far)])
    near, far = swapped(column, "gy", True), swapped(column, "gy", False)
    coarse_all, gpre_all, gsub, gdown = rest_call(
        counts, feat, rows, frm, dmap, grad, w_cat, wd_cat, wd_t, gsub, gdown, coarse_all, gpre_all)
    coarse, packed, gpre, split = border_call(
        count, side, feat, rows, frm, dmap, grad, near, column, far, w_cat, wd_cat, wd_t, gsub, gdown)
    pieces = lax.all_to_all(packed.reshape(count, PAIRS, 2, 2 * C), ("gx", "gy"), 0, 0, tiled=True)
    gfeat, mid, out_near, out_far = border_scatter_call(side, rows, frm, dmap, gpre, split, w_t)
    near, far = swapped(out_near, "gy", True), swapped(out_far, "gy", False)
    shape = pieces.shape
    spread = sum_call(pieces.reshape(count * PIECE, 2 * C))
    spread, gpre_all, mid = lax.optimization_barrier((spread, gpre_all, mid))
    total = mid + near.astype(F32) + far.astype(F32)
    near = swapped(jnp.where(even_x, total[2], total[0]).astype(BF), "gx", True)
    far = swapped(jnp.where(even_x, total[0], total[2]).astype(BF), "gx", False)
    gathered = lax.all_to_all(spread.reshape(shape), ("gx", "gy"), 0, 0, tiled=True).reshape(-1, 2 * C)
    gfeat_all = local_scatter_call(counts, rows, frm, gpre_all, w_t)
    coarse_out, grad_features = finish_call(coarse_all, gfeat_all, coarse, gfeat, total[1], near, far)
    grad_w_sub, grad_w_down = weights_call(float(ROWS * count) ** -0.5, gathered)
    return coarse_out[None, None], grad_features[None, None], grad_w_sub, grad_w_down


def solution(mesh):
    tile = P("gx", "gy", None, None)
    return jax.shard_map(
        shards,
        mesh=mesh,
        in_specs=(tile, P("gx", "gy"), tile, tile, tile, P(), P(), tile),
        out_specs=(tile, tile, P(), P()),
        check_vma=False,
    )
```

```python
import functools
import jax
import jax.numpy as jnp
from jax import lax
from jax.experimental import pallas as pl
from jax.sharding import PartitionSpec as P
from jax.experimental.pallas import tpu as pltpu

VB = 512
ROWS = 2048
CROWS = 512
CB = 64
C = 64
K = 27
KC = K * C
L = 256
H = VB // L
CQ = 128
EDGE = 640
WIDE = VB + 2 * CB
SUB_ROWS = (K + 1) // 2 * C
USED = SUB_ROWS + 4 * C
PAIRS = 5
PIECE = 2 * PAIRS
BF = jnp.bfloat16
F32 = jnp.float32
DIRS = [3 * (k // 9) + k // 3 % 3 for k in range(K)]


def mm(a, b):
    return jnp.dot(a, b, preferred_element_type=F32)


def mm_nt(a, b):
    return lax.dot_general(a, b, (((1,), (1,)), ((), ())), preferred_element_type=F32)


def pick(cond):
    return jnp.where(cond, jnp.ones((), BF), jnp.zeros((), BF))


def table(remote, base, rows, frm):
    row_v = rows[:, 0, :]
    frm_v = frm[:, 0, :]
    if remote:
        joint = jnp.where(frm_v == 4, row_v, jnp.where(frm_v == 9, -1, row_v + VB))
    else:
        joint = jnp.where(frm_v == 4, row_v - base, -1)
    high = joint >> (L.bit_length() - 1)
    low = jnp.where(joint < 0, -1, joint & (L - 1)).astype(F32)
    return high, low


def forward_work(remote, base, feat, rows, frm, dmap, grad, halo, w_cat, wd_cat, wd_t, source):
    high, low = table(remote, base, rows, frm)
    low = low.astype(BF)
    low_ids = lax.broadcasted_iota(jnp.int32, (L, VB), 0).astype(F32).astype(BF)
    local = jnp.concatenate([feat[:, i * L:(i + 1) * L] for i in range(H)], axis=0)
    slabs = {}
    for k in range(K):
        one_hot = pick(low[k:k + 1, :] == low_ids)
        parts = [mm(local, one_hot)]
        if remote and DIRS[k] != 4:
            if DIRS[k] not in slabs:
                slab = halo[DIRS[k] % 3][DIRS[k] // 3, :, 0:VB]
                slabs[DIRS[k]] = jnp.concatenate([slab[:, i * L:(i + 1) * L] for i in range(H)], axis=0)
            parts.append(mm(slabs[DIRS[k]], one_hot))
        high_k = high[k:k + 1, :]
        pieces = [part[i * C:(i + 1) * C, :] for part in parts for i in range(H)]
        got = pieces[0]
        for i in range(1, len(pieces)):
            got = jnp.where(high_k == i, pieces[i], got)
        source[k * C:(k + 1) * C, :] = got.astype(BF)
    pre = mm(w_cat[...], source[...])
    sig = jax.nn.sigmoid(pre)
    hidden = (pre * sig).astype(BF)
    target = dmap[0:1, :]
    kind = dmap[1:2, :]
    coarse_rel = jnp.where(target < CROWS, target - base // 4, -1)
    pick_own = pick(coarse_rel == lax.broadcasted_iota(jnp.int32, (CQ, VB), 0))
    zero = jnp.zeros((), BF)
    kinds = [kind == i for i in range(8)]
    up = mm(grad[...], pick_own)
    if remote:
        edge_grad = [halo[d % 3][d // 3, :, VB:VB + CB] for d in range(9)] + [jnp.zeros((C, EDGE - 9 * CB), BF)]
        up = up + mm(jnp.concatenate(edge_grad, axis=1), pick_edges(target))
    up = up.astype(BF)
    picked_g = jnp.concatenate([jnp.where(m, up, zero) for m in kinds], axis=0)
    grad_hidden = mm(wd_t[...], picked_g)
    grad_pre = (grad_hidden * sig * (1.0 + pre * (1.0 - sig))).astype(BF)
    grad_sub = mm_nt(grad_pre, source[...])
    grad_down = mm_nt(picked_g, hidden)
    picked_h = jnp.concatenate([jnp.where(m, hidden, zero) for m in kinds], axis=0)
    contrib = mm(wd_cat[...], picked_h)
    c_hi = contrib.astype(BF)
    c_lo = (contrib - c_hi.astype(F32)).astype(BF)
    split = jnp.concatenate([c_hi, c_lo], axis=0)
    own = mm_nt(split, pick_own)
    return own[:C] + own[C:], grad_pre, grad_sub, grad_down, split


def pick_edges(target):
    return pick((target - CROWS) == lax.broadcasted_iota(jnp.int32, (EDGE, VB), 0))


def scatter_work(remote, base, rows, frm, grad_pre, w_t, spread):
    high, low = table(remote, base, rows, frm)
    low_t = jnp.concatenate([low, jnp.zeros((32 - K, VB), F32)], axis=0).T.astype(BF)
    lane_ids = lax.broadcasted_iota(jnp.int32, (VB, L), 1).astype(F32).astype(BF)
    zero = jnp.zeros((), BF)
    for k in range(K):
        high_k = high[k:k + 1, :]
        count = 2 * H if (remote and DIRS[k] != 4) else H
        masked = jnp.concatenate([jnp.where(high_k == i, grad_pre, zero) for i in range(count)], axis=0)
        out = mm(masked, pick(low_t[:, k:k + 1] == lane_ids)).astype(BF)
        for i in range(count):
            spread[k * C:(k + 1) * C, i * L:(i + 1) * L] = out[i * C:(i + 1) * C, :]
    return mm(w_t[...], spread[:, 0:VB])


def prepare_sub(w_sub, w_cat, w_t):
    w_cat[...] = jnp.concatenate([w_sub[k] for k in range(K)], axis=1)
    w_t[...] = w_sub[...].reshape(KC, C).T


def prepare_down(w_down, wd_cat, wd_t):
    wd_cat[...] = jnp.concatenate([w_down[k] for k in range(8)], axis=1)
    wd_t[...] = w_down[...].reshape(8 * C, C).T


def one_local(block, counts, feat, rows, frm, dmap, grad, w_cat, wd_cat, wd_t, outs, source):
    coarse_o, gpre_o, gsub_o, gdown_o = outs

    @pl.when(block < counts[0, 0])
    def _():
        coarse, gpre, gsub, gdown, _ = forward_work(
            False, block * VB, feat, rows, frm, dmap, grad, None, w_cat, wd_cat, wd_t, source)
        coarse_o[...] = coarse.astype(BF)
        gpre_o[...] = gpre
        gsub_o[...] += gsub
        gdown_o[...] += gdown

    @pl.when(block >= counts[0, 0])
    def _():
        coarse_o[...] = jnp.zeros_like(coarse_o)


def local_kernel(counts, feat, rows, frm, dmap, grad, w_sub, w_down_h,
                 coarse_o, gpre_o, gsub_o, gdown_o, w_cat, w_t, wd_cat, wd_t, source, w_down, sem):
    i = pl.program_id(0)

    @pl.when(i == 0)
    def _():
        copy = pltpu.make_async_copy(w_down_h, w_down, sem)
        copy.start()
        prepare_sub(w_sub, w_cat, w_t)
        copy.wait()
        prepare_down(w_down, wd_cat, wd_t)
        gsub_o[...] = jnp.zeros_like(gsub_o)
        gdown_o[...] = jnp.zeros_like(gdown_o)

    one_local(i + 1, counts, feat, rows, frm, dmap, grad, w_cat, wd_cat, wd_t,
              (coarse_o, gpre_o, gsub_o, gdown_o), source)


def local_scatter_kernel(counts, rows, frm, gpre, w_t, gfeat_o, spread):
    block = pl.program_id(0) + 1

    @pl.when(block < counts[0, 0])
    def _():
        gfeat_o[...] = scatter_work(False, block * VB, rows, frm, gpre[...], w_t, spread).astype(BF)

    @pl.when(block >= counts[0, 0])
    def _():
        gfeat_o[...] = jnp.zeros_like(gfeat_o)


WHOLE = pl.BlockSpec(memory_space=pltpu.VMEM)


def full(shape):
    return WHOLE


def piped(shape):
    return pl.BlockSpec(shape, lambda i: (0,) * len(shape))


def columns(shape, first):
    return pl.BlockSpec(shape, lambda i: (0, i + first))


def index_columns(first):
    return pl.BlockSpec((K, 1, VB), lambda i: (0, 0, i + first))


def table_specs(first):
    return [columns((C, VB), first), index_columns(first), index_columns(first),
            columns((2, VB), first), columns((C, CQ), first)]


LIMIT = pltpu.CompilerParams(vmem_limit_bytes=20 << 20)
SMALL = pltpu.CompilerParams(vmem_limit_bytes=8 << 20)
SOURCE = pltpu.VMEM((KC, VB), BF)


def sd(shape, dtype):
    return jax.ShapeDtypeStruct(shape, dtype)


def local_call(counts, feat, rows, frm, dmap, grad, w_sub, w_down):
    weights = [(C, KC), (C, KC), (C, 8 * C), (C, 8 * C)]
    return pl.pallas_call(
        local_kernel,
        grid=(3,),
        in_specs=[pl.BlockSpec(memory_space=pltpu.SMEM)] + table_specs(1)
        + [full((K, C, C)), pl.BlockSpec(memory_space=pltpu.HBM)],
        out_specs=[columns((C, CQ), 1), columns((C, VB), 1), full((C, KC)), full((8 * C, C))]
        + [full(w) for w in weights],
        out_shape=[sd((C, CROWS), BF), sd((C, ROWS), BF), sd((C, KC), F32), sd((8 * C, C), F32)]
        + [sd(w, BF) for w in weights],
        scratch_shapes=[SOURCE, pltpu.VMEM((8, C, C), BF), pltpu.SemaphoreType.DMA(())],
        compiler_params=LIMIT,
        name="local_blocks",
    )(counts, feat, rows, frm, dmap, grad, w_sub, in_hbm(w_down))


def local_scatter_call(counts, rows, frm, gpre_all, w_t):
    return pl.pallas_call(
        local_scatter_kernel,
        grid=(3,),
        in_specs=[pl.BlockSpec(memory_space=pltpu.SMEM), index_columns(1), index_columns(1),
                  columns((C, VB), 1), full((C, KC))],
        out_specs=columns((C, VB), 1),
        out_shape=sd((C, ROWS), BF),
        scratch_shapes=[SOURCE],
        compiler_params=LIMIT,
        name="local_scatter_blocks",
    )(counts, rows, frm, gpre_all, w_t)


def in_hbm(array):
    return pltpu.with_memory_space_constraint(array, pltpu.HBM)


def border_pack_kernel(feat, grad, out, sems):
    a = pltpu.make_async_copy(feat.at[:, 0:VB], out.at[:, 0:VB], sems.at[0])
    b = pltpu.make_async_copy(grad.at[:, 0:CQ], out.at[:, VB:], sems.at[1])
    a.start()
    b.start()
    a.wait()
    b.wait()


def border_pack(feat, grad):
    return pl.pallas_call(
        border_pack_kernel,
        in_specs=[pl.BlockSpec(memory_space=pltpu.HBM)] * 2,
        out_specs=WHOLE,
        out_shape=sd((C, WIDE), BF),
        scratch_shapes=[pltpu.SemaphoreType.DMA((2,))],
        compiler_params=SMALL,
        name="pack_border",
    )(in_hbm(feat), in_hbm(grad))


def sum_kernel(pieces, out):
    rows = pieces.shape[0]
    span = 4 * PIECE
    total = jnp.sum(pieces[...].astype(F32).reshape(rows // span, span, 2 * C), axis=0)
    mine = total[0:PIECE]
    for i in range(1, 4):
        mine = mine + total[i * PIECE:(i + 1) * PIECE]
    tiled = jnp.concatenate([mine] * 8, axis=0).astype(BF)
    for i in range(rows // (8 * PIECE)):
        out[i * 8 * PIECE:(i + 1) * 8 * PIECE, :] = tiled


def sum_call(pieces):
    return pl.pallas_call(
        sum_kernel,
        grid=(1,),
        in_specs=[full(pieces.shape)],
        out_specs=piped(pieces.shape),
        out_shape=jax.ShapeDtypeStruct(pieces.shape, BF),
        compiler_params=SMALL,
        name="sum_pieces",
    )(pieces)


def border_kernel(side, feat, rows, frm, dmap, grad, near, column, far, w_cat, wd_cat, wd_t, gsub, gdown,
                  coarse_o, packed_o, gpre_o, split_o, source, below, above):
    even = side[0] == 1
    below[...] = jnp.where(even, far[...], near[...])
    above[...] = jnp.where(even, near[...], far[...])
    coarse, gpre, dsub, ddown, split = forward_work(
        True, 0, feat, rows, frm, dmap, grad, (below, column, above), w_cat, wd_cat, wd_t, source)
    coarse_o[...] = coarse
    gpre_o[...] = gpre
    split_o[...] = split
    total = gsub[...] + dsub
    for t in range(K // 2):
        packed_o[t * C:(t + 1) * C, :] = total[:, t * 2 * C:(t + 1) * 2 * C].astype(BF)
    last = jnp.concatenate([total[:, KC - C:], jnp.zeros((C, C), F32)], axis=1)
    packed_o[K // 2 * C:SUB_ROWS, :] = last.astype(BF)
    down = gdown[...] + ddown
    packed_o[SUB_ROWS:USED, :] = jnp.concatenate([down[:4 * C], down[4 * C:]], axis=1).astype(BF)
    packed_o[USED:, :] = jnp.zeros((packed_o.shape[0] - USED, 2 * C), BF)


def border_call(count, side, feat, rows, frm, dmap, grad, near, column, far, w_cat, wd_cat, wd_t, gsub, gdown):
    slab = full((3, C, WIDE))
    return pl.pallas_call(
        border_kernel,
        grid=(1,),
        in_specs=[pl.BlockSpec(memory_space=pltpu.SMEM)] + table_specs(0) + [slab, slab, slab, full((C, KC)), full((C, 8 * C)), full((C, 8 * C)),
                                   full((C, KC)), full((8 * C, C))],
        out_specs=[full((C, CQ)), piped((count * PIECE, 2 * C)), full((C, VB)), full((2 * C, VB))],
        out_shape=[sd((C, CQ), F32), sd((count * PIECE, 2 * C), BF), sd((C, VB), BF), sd((2 * C, VB), BF)],
        scratch_shapes=[SOURCE, pltpu.VMEM((3, C, WIDE), BF), pltpu.VMEM((3, C, WIDE), BF)],
        compiler_params=LIMIT,
        name="border_block",
    )(side, feat, rows, frm, dmap, grad, near, column, far, w_cat, wd_cat, wd_t, gsub, gdown)


def border_scatter_kernel(side, rows, frm, dmap, gpre, split, w_t, gfeat_o, mid_o, near_o, far_o, spread):
    gfeat_o[...] = scatter_work(True, 0, rows, frm, gpre[...], w_t, spread)
    both = mm_nt(split[...], pick_edges(dmap[0:1, :]))
    edge = both[:C] + both[C:]
    even = side[0] == 1

    def slab(d):
        a = 9 * (d // 3) + 3 * (d % 3)
        a, b = a * C, (a + 3) * C
        outward = jnp.zeros((C, VB), F32) if d == 4 else mm(w_t[:, a:b], spread[a:b, VB:2 * VB])
        return jnp.concatenate([outward, edge[:, d * CB:(d + 1) * CB], jnp.zeros((C, CB), F32)], axis=1)

    for x in range(3):
        down, up = slab(3 * x).astype(BF), slab(3 * x + 2).astype(BF)
        mid_o[x] = slab(3 * x + 1)
        near_o[x] = jnp.where(even, up, down)
        far_o[x] = jnp.where(even, down, up)


def border_scatter_call(side, rows, frm, dmap, gpre, split, w_t):
    slab = (3, C, WIDE)
    return pl.pallas_call(
        border_scatter_kernel,
        grid=(1,),
        in_specs=[pl.BlockSpec(memory_space=pltpu.SMEM), index_columns(0), index_columns(0), columns((2, VB), 0),
                  full((C, VB)), full((2 * C, VB)),
                  full((C, KC))],
        out_specs=[full((C, VB)), full(slab), full(slab), full(slab)],
        out_shape=[sd((C, VB), F32), sd(slab, F32), sd(slab, BF), sd(slab, BF)],
        scratch_shapes=[pltpu.VMEM((KC, 2 * VB), BF)],
        compiler_params=LIMIT,
        name="border_scatter_block",
    )(side, rows, frm, dmap, gpre, split, w_t)


def finish_kernel(coarse_i, gfeat_i, coarse, gfeat, total, left, right, coarse_o, gfeat_o):
    inc = total[...] + left[...].astype(F32) + right[...].astype(F32)
    gfeat_o[...] = (gfeat[...] + inc[:, 0:VB]).astype(BF)
    coarse_o[:, 0:CB] = (coarse[:, 0:CB] + inc[:, VB:VB + CB]).astype(BF)
    coarse_o[:, CB:] = coarse[:, CB:].astype(BF)


def finish_call(coarse_all, gfeat_all, coarse, gfeat, total, left, right):
    return pl.pallas_call(
        finish_kernel,
        grid=(1,),
        in_specs=[
            pl.BlockSpec(memory_space=pl.ANY),
            pl.BlockSpec(memory_space=pl.ANY),
            full((C, CQ)), full((C, VB)), full((C, WIDE)), full((C, WIDE)), full((C, WIDE)),
        ],
        out_specs=[pl.BlockSpec((C, CQ), lambda i: (0, 0)), pl.BlockSpec((C, VB), lambda i: (0, 0))],
        out_shape=[sd((C, CROWS), BF), sd((C, ROWS), BF)],
        input_output_aliases={0: 0, 1: 1},
        compiler_params=SMALL,
        name="add_incoming",
    )(coarse_all, gfeat_all, coarse, gfeat, total, left, right)


def weights_kernel(scale, packed, gsub_o, gdown_o):
    for k in range(K):
        r, c = k // 2 * C, k % 2 * C
        gsub_o[k] = packed[r:r + C, c:c + C].astype(F32) * scale
    for k in range(8):
        r, c = SUB_ROWS + k % 4 * C, k // 4 * C
        gdown_o[k] = packed[r:r + C, c:c + C].astype(F32) * scale


def weights_call(scale, packed):
    return pl.pallas_call(
        functools.partial(weights_kernel, scale),
        grid=(1,),
        in_specs=[full(packed.shape)],
        out_specs=[piped((K, C, C)), piped((8, C, C))],
        out_shape=[sd((K, C, C), F32), sd((8, C, C), F32)],
        compiler_params=SMALL,
        name="unpack_weights",
    )(packed)


def swapped(block, axis, first):
    n = lax.axis_size(axis)
    pairs = [(i, i + 1) for i in range(0 if first else 1, n - 1, 2)]
    return lax.ppermute(block, axis, pairs + [(b, a) for a, b in pairs])


def shards(features, counts, sub_rows, sub_from, down_map, w_sub, w_down, cotangent):
    feat = features[0, 0]
    grad = cotangent[0, 0]
    rows, frm, dmap = sub_rows.reshape(K, 1, ROWS), sub_from.reshape(K, 1, ROWS), down_map[0, 0]
    nx, ny = lax.axis_size("gx"), lax.axis_size("gy")
    count = nx * ny
    border = border_pack(feat, grad)
    even_x, even_y = lax.axis_index("gx") % 2 == 0, lax.axis_index("gy") % 2 == 0
    side = even_y.astype(jnp.int32).reshape(1)
    near, far = swapped(border, "gx", True), swapped(border, "gx", False)
    column = jnp.stack([jnp.where(even_x, far, near), border, jnp.where(even_x, near, far)])
    near, far = swapped(column, "gy", True), swapped(column, "gy", False)
    coarse_all, gpre_all, gsub, gdown, w_cat, w_t, wd_cat, wd_t = local_call(
        counts, feat, rows, frm, dmap, grad, w_sub, w_down)
    coarse, packed, gpre, split = border_call(
        count, side, feat, rows, frm, dmap, grad, near, column, far, w_cat, wd_cat, wd_t, gsub, gdown)
    pieces = lax.all_to_all(packed.reshape(count, PAIRS, 2, 2 * C), ("gx", "gy"), 0, 0, tiled=True)
    gfeat, mid, out_near, out_far = border_scatter_call(side, rows, frm, dmap, gpre, split, w_t)
    near, far = swapped(out_near, "gy", True), swapped(out_far, "gy", False)
    shape = pieces.shape
    spread = sum_call(pieces.reshape(count * PIECE, 2 * C))
    spread, gpre_all, mid = lax.optimization_barrier((spread, gpre_all, mid))
    total = mid + near.astype(F32) + far.astype(F32)
    near = swapped(jnp.where(even_x, total[2], total[0]).astype(BF), "gx", True)
    far = swapped(jnp.where(even_x, total[0], total[2]).astype(BF), "gx", False)
    gathered = lax.all_to_all(spread.reshape(shape), ("gx", "gy"), 0, 0, tiled=True).reshape(-1, 2 * C)
    gfeat_all = local_scatter_call(counts, rows, frm, gpre_all, w_t)
    coarse_out, grad_features = finish_call(coarse_all, gfeat_all, coarse, gfeat, total[1], near, far)
    grad_w_sub, grad_w_down = weights_call(float(ROWS * count) ** -0.5, gathered)
    return coarse_out[None, None], grad_features[None, None], grad_w_sub, grad_w_down


def solution(mesh):
    tile = P("gx", "gy", None, None)
    return jax.shard_map(
        shards,
        mesh=mesh,
        in_specs=(tile, P("gx", "gy"), tile, tile, tile, P(), P(), tile),
        out_specs=(tile, tile, P(), P()),
        check_vma=False,
    )
```

```python
import functools
import jax
import jax.numpy as jnp
from jax import lax
from jax.experimental import pallas as pl
from jax.sharding import PartitionSpec as P
from jax.experimental.pallas import tpu as pltpu

VB = 512
ROWS = 2048
CROWS = 512
CB = 64
NOWHERE = CROWS + 9 * CB
C = 64
K = 27
KC = K * C
L = 256
H = VB // L
CQ = 128
EDGE = 640
WIDE = VB + 2 * CB
SUB_ROWS = (K + 1) // 2 * C
USED = SUB_ROWS + 4 * C
PAIRS = 5
PIECE = 2 * PAIRS
BF = jnp.bfloat16
F32 = jnp.float32
DIRS = [3 * (k // 9) + k // 3 % 3 for k in range(K)]


def mm(a, b):
    return jnp.dot(a, b, preferred_element_type=F32)


def mm_nt(a, b):
    return lax.dot_general(a, b, (((1,), (1,)), ((), ())), preferred_element_type=F32)


def pick(cond):
    return jnp.where(cond, jnp.ones((), BF), jnp.zeros((), BF))


def table(remote, base, rows, frm):
    row_v = rows[:, 0, :]
    frm_v = frm[:, 0, :]
    if remote:
        joint = jnp.where(frm_v == 4, row_v, jnp.where(frm_v == 9, -1, row_v + VB))
    else:
        joint = jnp.where(frm_v == 4, row_v - base, -1)
    high = joint >> (L.bit_length() - 1)
    low = jnp.where(joint < 0, -1, joint & (L - 1)).astype(F32)
    return high, low


def forward_work(remote, base, feat, rows, frm, dmap, grad, halo, w_cat, wd_cat, wd_t, source):
    high, low = table(remote, base, rows, frm)
    low = low.astype(BF)
    low_ids = lax.broadcasted_iota(jnp.int32, (L, VB), 0).astype(F32).astype(BF)
    local = jnp.concatenate([feat[:, i * L:(i + 1) * L] for i in range(H)], axis=0)
    slabs = {}
    for k in range(K):
        one_hot = pick(low[k:k + 1, :] == low_ids)
        parts = [mm(local, one_hot)]
        if remote and DIRS[k] != 4:
            if DIRS[k] not in slabs:
                slab = halo[DIRS[k] % 3][DIRS[k] // 3, :, 0:VB]
                slabs[DIRS[k]] = jnp.concatenate([slab[:, i * L:(i + 1) * L] for i in range(H)], axis=0)
            parts.append(mm(slabs[DIRS[k]], one_hot))
        high_k = high[k:k + 1, :]
        pieces = [part[i * C:(i + 1) * C, :] for part in parts for i in range(H)]
        got = pieces[0]
        for i in range(1, len(pieces)):
            got = jnp.where(high_k == i, pieces[i], got)
        source[k * C:(k + 1) * C, :] = got.astype(BF)
    pre = mm(w_cat[...], source[...])
    sig = jax.nn.sigmoid(pre)
    hidden = (pre * sig).astype(BF)
    target = dmap[0:1, :]
    kind = dmap[1:2, :]
    coarse_rel = jnp.where(target < CROWS, target - base // 4, -1)
    pick_own = pick(coarse_rel == lax.broadcasted_iota(jnp.int32, (CQ, VB), 0))
    zero = jnp.zeros((), BF)
    kinds = [kind == i for i in range(8)]
    up = mm(grad[...], pick_own)
    if remote:
        edge_grad = [halo[d % 3][d // 3, :, VB:VB + CB] for d in range(9)] + [jnp.zeros((C, EDGE - 9 * CB), BF)]
        up = up + mm(jnp.concatenate(edge_grad, axis=1), pick_edges(target))
    up = up.astype(BF)
    picked_g = jnp.concatenate([jnp.where(m, up, zero) for m in kinds], axis=0)
    grad_hidden = mm(wd_t[...], picked_g)
    grad_pre = (grad_hidden * sig * (1.0 + pre * (1.0 - sig))).astype(BF)
    grad_sub = mm_nt(grad_pre, source[...])
    grad_down = mm_nt(picked_g, hidden)
    picked_h = jnp.concatenate([jnp.where(m, hidden, zero) for m in kinds], axis=0)
    contrib = mm(wd_cat[...], picked_h)
    c_hi = contrib.astype(BF)
    c_lo = (contrib - c_hi.astype(F32)).astype(BF)
    split = jnp.concatenate([c_hi, c_lo], axis=0)
    own = mm_nt(split, pick_own)
    return own[:C] + own[C:], grad_pre, grad_sub, grad_down, split


def pick_edges(target):
    return pick((target - CROWS) == lax.broadcasted_iota(jnp.int32, (EDGE, VB), 0))


def scatter_work(remote, base, rows, frm, grad_pre, w_t, spread):
    high, low = table(remote, base, rows, frm)
    low_t = jnp.concatenate([low, jnp.zeros((32 - K, VB), F32)], axis=0).T.astype(BF)
    lane_ids = lax.broadcasted_iota(jnp.int32, (VB, L), 1).astype(F32).astype(BF)
    zero = jnp.zeros((), BF)
    for k in range(K):
        high_k = high[k:k + 1, :]
        count = 2 * H if (remote and DIRS[k] != 4) else H
        masked = jnp.concatenate([jnp.where(high_k == i, grad_pre, zero) for i in range(count)], axis=0)
        out = mm(masked, pick(low_t[:, k:k + 1] == lane_ids)).astype(BF)
        for i in range(count):
            spread[k * C:(k + 1) * C, i * L:(i + 1) * L] = out[i * C:(i + 1) * C, :]
    return mm(w_t[...], spread[:, 0:VB])


def prepare_sub(w_sub, w_cat, w_t):
    w_cat[...] = jnp.concatenate([w_sub[k] for k in range(K)], axis=1)
    w_t[...] = w_sub[...].reshape(KC, C).T


def prepare_down(w_down, wd_cat, wd_t):
    wd_cat[...] = jnp.concatenate([w_down[k] for k in range(8)], axis=1)
    wd_t[...] = w_down[...].reshape(8 * C, C).T


def live_rows(dmap):
    return jnp.sum((dmap[0:1, :] < NOWHERE).astype(F32)).astype(jnp.int32)


def one_local(block, live_count, feat, rows, frm, dmap, grad, w_cat, wd_cat, wd_t, outs, source):
    coarse_o, gpre_o, gsub_o, gdown_o = outs
    live = block * VB < live_count

    @pl.when(live)
    def _():
        coarse, gpre, gsub, gdown, _ = forward_work(
            False, block * VB, feat, rows, frm, dmap, grad, None, w_cat, wd_cat, wd_t, source)
        coarse_o[...] = coarse.astype(BF)
        gpre_o[...] = gpre
        gsub_o[...] += gsub
        gdown_o[...] += gdown

    @pl.when(jnp.logical_not(live))
    def _():
        coarse_o[...] = jnp.zeros_like(coarse_o)


def views(block, feat, rows, frm, dmap, grad):
    a, b = block * VB, (block + 1) * VB
    return feat.at[:, a:b], rows.at[:, :, a:b], frm.at[:, :, a:b], dmap.at[:, a:b], grad.at[:, a // 4:b // 4]


def first_kernel(feat_h, rows_h, frm_h, dmap_h, grad_h, w_sub_h, w_down_h,
                 coarse_o, gpre_o, gsub_o, gdown_o, w_cat, w_t, wd_cat, wd_t, feat, rows, frm, dmap, grad,
                 source, w_sub, w_down, sems):
    pairs = [(w_sub_h, w_sub), (w_down_h, w_down), (dmap_h, dmap), (rows_h, rows), (frm_h, frm), (feat_h, feat),
             (grad_h, grad)]
    copies = [pltpu.make_async_copy(a, b, sems.at[i]) for i, (a, b) in enumerate(pairs)]
    for copy in copies:
        copy.start()
    gsub_o[...] = jnp.zeros_like(gsub_o)
    gdown_o[...] = jnp.zeros_like(gdown_o)
    copies[0].wait()
    prepare_sub(w_sub, w_cat, w_t)
    copies[1].wait()
    prepare_down(w_down, wd_cat, wd_t)
    for copy in copies[2:]:
        copy.wait()
    one_local(1, live_rows(dmap), *views(1, feat, rows, frm, dmap, grad), w_cat, wd_cat, wd_t,
              (coarse_o.at[:, CQ:2 * CQ], gpre_o.at[:, VB:2 * VB], gsub_o, gdown_o), source)


def rest_kernel(feat, rows, frm, dmap, grad, w_cat, wd_cat, wd_t, gsub, gdown, coarse, gpre,
                coarse_o, gpre_o, gsub_o, gdown_o, source):
    live_count = live_rows(dmap)
    for i in (2, 3):
        one_local(i, live_count, *views(i, feat, rows, frm, dmap, grad), w_cat, wd_cat, wd_t,
                  (coarse_o.at[:, i * CQ:(i + 1) * CQ], gpre_o.at[:, i * VB:(i + 1) * VB], gsub_o, gdown_o), source)


def local_scatter_kernel(rows, frm, dmap, gpre, w_t, gfeat_o, spread):
    block = pl.program_id(0) + 1
    live = block * VB < live_rows(dmap)

    @pl.when(live)
    def _():
        here = pl.ds(pl.multiple_of(block * VB, VB), VB)
        gfeat_o[...] = scatter_work(
            False, block * VB, rows.at[:, :, here], frm.at[:, :, here], gpre[:, here], w_t, spread).astype(BF)

    @pl.when(jnp.logical_not(live))
    def _():
        gfeat_o[...] = jnp.zeros_like(gfeat_o)


WHOLE = pl.BlockSpec(memory_space=pltpu.VMEM)
SCALAR = pl.BlockSpec(memory_space=pltpu.SMEM)


def full(shape):
    return WHOLE


def piped(shape):
    return pl.BlockSpec(shape, lambda i: (0,) * len(shape))


def columns(shape, first):
    return pl.BlockSpec(shape, lambda i: (0, i + first))


def index_columns(first):
    return pl.BlockSpec((K, 1, VB), lambda i: (0, 0, i + first))


def table_specs(first):
    return [columns((C, VB), first), index_columns(first), index_columns(first),
            columns((2, VB), first), columns((C, CQ), first)]


LIMIT = pltpu.CompilerParams(vmem_limit_bytes=20 << 20)
SMALL = pltpu.CompilerParams(vmem_limit_bytes=8 << 20)
SOURCE = pltpu.VMEM((KC, VB), BF)


def sd(shape, dtype):
    return jax.ShapeDtypeStruct(shape, dtype)


def first_call(feat, rows, frm, dmap, grad, w_sub, w_down):
    weights = [(C, KC), (C, KC), (C, 8 * C), (C, 8 * C)]
    arrays = [feat, rows, frm, dmap, grad]
    return pl.pallas_call(
        first_kernel,
        in_specs=[pl.BlockSpec(memory_space=pltpu.HBM)] * 7,
        out_specs=[WHOLE] * 13,
        out_shape=[sd((C, CROWS), BF), sd((C, ROWS), BF), sd((C, KC), F32), sd((8 * C, C), F32)]
        + [sd(w, BF) for w in weights] + [sd(a.shape, a.dtype) for a in arrays],
        scratch_shapes=[SOURCE, pltpu.VMEM((K, C, C), BF), pltpu.VMEM((8, C, C), BF), pltpu.SemaphoreType.DMA((7,))],
        compiler_params=LIMIT,
        name="first_local_block",
    )(*[in_hbm(a) for a in arrays + [w_sub, w_down]])


def rest_call(feat, rows, frm, dmap, grad, w_cat, wd_cat, wd_t, gsub, gdown, coarse_all, gpre_all):
    return pl.pallas_call(
        rest_kernel,
        in_specs=[WHOLE] * 12,
        out_specs=[WHOLE] * 4,
        out_shape=[sd((C, CROWS), BF), sd((C, ROWS), BF), sd((C, KC), F32), sd((8 * C, C), F32)],
        scratch_shapes=[SOURCE],
        input_output_aliases={10: 0, 11: 1, 8: 2, 9: 3},
        compiler_params=LIMIT,
        name="other_local_blocks",
    )(feat, rows, frm, dmap, grad, w_cat, wd_cat, wd_t, gsub, gdown, coarse_all, gpre_all)


def local_scatter_call(rows, frm, dmap, gpre_all, w_t):
    return pl.pallas_call(
        local_scatter_kernel,
        grid=(3,),
        in_specs=[WHOLE] * 5,
        out_specs=columns((C, VB), 1),
        out_shape=sd((C, ROWS), BF),
        scratch_shapes=[SOURCE],
        compiler_params=LIMIT,
        name="local_scatter_blocks",
    )(rows, frm, dmap, gpre_all, w_t)


def in_hbm(array):
    return pltpu.with_memory_space_constraint(array, pltpu.HBM)


def border_pack_kernel(feat, grad, out, sems):
    a = pltpu.make_async_copy(feat.at[:, 0:VB], out.at[:, 0:VB], sems.at[0])
    b = pltpu.make_async_copy(grad.at[:, 0:CQ], out.at[:, VB:], sems.at[1])
    a.start()
    b.start()
    a.wait()
    b.wait()


def border_pack(feat, grad):
    return pl.pallas_call(
        border_pack_kernel,
        in_specs=[pl.BlockSpec(memory_space=pltpu.HBM)] * 2,
        out_specs=WHOLE,
        out_shape=sd((C, WIDE), BF),
        scratch_shapes=[pltpu.SemaphoreType.DMA((2,))],
        compiler_params=SMALL,
        name="pack_border",
    )(in_hbm(feat), in_hbm(grad))


def sum_kernel(pieces, out):
    rows = pieces.shape[0]
    span = 4 * PIECE
    total = jnp.sum(pieces[...].astype(F32).reshape(rows // span, span, 2 * C), axis=0)
    mine = total[0:PIECE]
    for i in range(1, 4):
        mine = mine + total[i * PIECE:(i + 1) * PIECE]
    tiled = jnp.concatenate([mine] * 8, axis=0).astype(BF)
    for i in range(rows // (8 * PIECE)):
        out[i * 8 * PIECE:(i + 1) * 8 * PIECE, :] = tiled


def sum_call(pieces):
    return pl.pallas_call(
        sum_kernel,
        grid=(1,),
        in_specs=[full(pieces.shape)],
        out_specs=piped(pieces.shape),
        out_shape=jax.ShapeDtypeStruct(pieces.shape, BF),
        compiler_params=SMALL,
        name="sum_pieces",
    )(pieces)


def border_kernel(side, feat, rows, frm, dmap, grad, near, column, far, w_cat, wd_cat, wd_t, gsub, gdown,
                  coarse_o, packed_o, gpre_o, split_o, source, below, above):
    feat, rows, frm, dmap, grad = views(0, feat, rows, frm, dmap, grad)
    even = side[0] == 1
    below[...] = jnp.where(even, far[...], near[...])
    above[...] = jnp.where(even, near[...], far[...])
    coarse, gpre, dsub, ddown, split = forward_work(
        True, 0, feat, rows, frm, dmap, grad, (below, column, above), w_cat, wd_cat, wd_t, source)
    coarse_o[...] = coarse
    gpre_o[...] = gpre
    split_o[...] = split
    total = gsub[...] + dsub
    for t in range(K // 2):
        packed_o[t * C:(t + 1) * C, :] = total[:, t * 2 * C:(t + 1) * 2 * C].astype(BF)
    last = jnp.concatenate([total[:, KC - C:], jnp.zeros((C, C), F32)], axis=1)
    packed_o[K // 2 * C:SUB_ROWS, :] = last.astype(BF)
    down = gdown[...] + ddown
    packed_o[SUB_ROWS:USED, :] = jnp.concatenate([down[:4 * C], down[4 * C:]], axis=1).astype(BF)
    packed_o[USED:, :] = jnp.zeros((packed_o.shape[0] - USED, 2 * C), BF)


def border_call(count, side, feat, rows, frm, dmap, grad, near, column, far, w_cat, wd_cat, wd_t, gsub, gdown):
    slab = full((3, C, WIDE))
    return pl.pallas_call(
        border_kernel,
        grid=(1,),
        in_specs=[SCALAR] + [WHOLE] * 5 + [slab, slab, slab, full((C, KC)), full((C, 8 * C)), full((C, 8 * C)),
                                   full((C, KC)), full((8 * C, C))],
        out_specs=[full((C, CQ)), piped((count * PIECE, 2 * C)), full((C, VB)), full((2 * C, VB))],
        out_shape=[sd((C, CQ), F32), sd((count * PIECE, 2 * C), BF), sd((C, VB), BF), sd((2 * C, VB), BF)],
        scratch_shapes=[SOURCE, pltpu.VMEM((3, C, WIDE), BF), pltpu.VMEM((3, C, WIDE), BF)],
        compiler_params=LIMIT,
        name="border_block",
    )(side, feat, rows, frm, dmap, grad, near, column, far, w_cat, wd_cat, wd_t, gsub, gdown)


def border_scatter_kernel(side, rows, frm, dmap, gpre, split, w_t, gfeat_o, mid_o, near_o, far_o, spread):
    gfeat_o[...] = scatter_work(True, 0, rows.at[:, :, 0:VB], frm.at[:, :, 0:VB], gpre[...], w_t, spread)
    both = mm_nt(split[...], pick_edges(dmap[0:1, 0:VB]))
    edge = both[:C] + both[C:]
    even = side[0] == 1

    def slab(d):
        a = 9 * (d // 3) + 3 * (d % 3)
        a, b = a * C, (a + 3) * C
        outward = jnp.zeros((C, VB), F32) if d == 4 else mm(w_t[:, a:b], spread[a:b, VB:2 * VB])
        return jnp.concatenate([outward, edge[:, d * CB:(d + 1) * CB], jnp.zeros((C, CB), F32)], axis=1)

    for x in range(3):
        down, up = slab(3 * x).astype(BF), slab(3 * x + 2).astype(BF)
        mid_o[x] = slab(3 * x + 1)
        near_o[x] = jnp.where(even, up, down)
        far_o[x] = jnp.where(even, down, up)


def border_scatter_call(side, rows, frm, dmap, gpre, split, w_t):
    slab = (3, C, WIDE)
    return pl.pallas_call(
        border_scatter_kernel,
        grid=(1,),
        in_specs=[SCALAR, WHOLE, WHOLE, WHOLE, full((C, VB)), full((2 * C, VB)),
                  full((C, KC))],
        out_specs=[full((C, VB)), full(slab), full(slab), full(slab)],
        out_shape=[sd((C, VB), F32), sd(slab, F32), sd(slab, BF), sd(slab, BF)],
        scratch_shapes=[pltpu.VMEM((KC, 2 * VB), BF)],
        compiler_params=LIMIT,
        name="border_scatter_block",
    )(side, rows, frm, dmap, gpre, split, w_t)


def finish_kernel(coarse_i, gfeat_i, coarse, gfeat, total, left, right, coarse_o, gfeat_o):
    inc = total[...] + left[...].astype(F32) + right[...].astype(F32)
    gfeat_o[...] = (gfeat[...] + inc[:, 0:VB]).astype(BF)
    coarse_o[:, 0:CB] = (coarse[:, 0:CB] + inc[:, VB:VB + CB]).astype(BF)
    coarse_o[:, CB:CQ] = coarse[:, CB:].astype(BF)
    coarse_o[:, CQ:] = coarse_i[:, CQ:]


def finish_call(coarse_all, gfeat_all, coarse, gfeat, total, left, right):
    return pl.pallas_call(
        finish_kernel,
        grid=(1,),
        in_specs=[
            WHOLE, pl.BlockSpec(memory_space=pl.ANY),
            full((C, CQ)), full((C, VB)), full((C, WIDE)), full((C, WIDE)), full((C, WIDE)),
        ],
        out_specs=[piped((C, CROWS)), pl.BlockSpec((C, VB), lambda i: (0, 0))],
        out_shape=[sd((C, CROWS), BF), sd((C, ROWS), BF)],
        input_output_aliases={1: 1},
        compiler_params=SMALL,
        name="add_incoming",
    )(coarse_all, gfeat_all, coarse, gfeat, total, left, right)


def weights_kernel(scale, packed, gsub_o, gdown_o):
    for k in range(K):
        r, c = k // 2 * C, k % 2 * C
        gsub_o[k] = packed[r:r + C, c:c + C].astype(F32) * scale
    for k in range(8):
        r, c = SUB_ROWS + k % 4 * C, k // 4 * C
        gdown_o[k] = packed[r:r + C, c:c + C].astype(F32) * scale


def weights_call(scale, packed):
    return pl.pallas_call(
        functools.partial(weights_kernel, scale),
        grid=(1,),
        in_specs=[full(packed.shape)],
        out_specs=[piped((K, C, C)), piped((8, C, C))],
        out_shape=[sd((K, C, C), F32), sd((8, C, C), F32)],
        compiler_params=SMALL,
        name="unpack_weights",
    )(packed)


def swapped(block, axis, first):
    n = lax.axis_size(axis)
    pairs = [(i, i + 1) for i in range(0 if first else 1, n - 1, 2)]
    return lax.ppermute(block, axis, pairs + [(b, a) for a, b in pairs])


def shards(features, counts, sub_rows, sub_from, down_map, w_sub, w_down, cotangent):
    feat = features[0, 0]
    grad = cotangent[0, 0]
    rows, frm, dmap = sub_rows.reshape(K, 1, ROWS), sub_from.reshape(K, 1, ROWS), down_map[0, 0]
    nx, ny = lax.axis_size("gx"), lax.axis_size("gy")
    count = nx * ny
    border = border_pack(feat, grad)
    even_x, even_y = lax.axis_index("gx") % 2 == 0, lax.axis_index("gy") % 2 == 0
    side = even_y.astype(jnp.int32).reshape(1)
    near, far = swapped(border, "gx", True), swapped(border, "gx", False)
    (coarse_all, gpre_all, gsub, gdown, w_cat, w_t, wd_cat, wd_t, feat, rows, frm, dmap, grad) = first_call(
        feat, rows, frm, dmap, grad, w_sub, w_down)
    near, far, gsub = lax.optimization_barrier((near, far, gsub))
    column = jnp.stack([jnp.where(even_x, far, near), border, jnp.where(even_x, near, far)])
    near, far = swapped(column, "gy", True), swapped(column, "gy", False)
    coarse_all, gpre_all, gsub, gdown = rest_call(
        feat, rows, frm, dmap, grad, w_cat, wd_cat, wd_t, gsub, gdown, coarse_all, gpre_all)
    coarse, packed, gpre, split = border_call(
        count, side, feat, rows, frm, dmap, grad, near, column, far, w_cat, wd_cat, wd_t, gsub, gdown)
    pieces = lax.all_to_all(packed.reshape(count, PAIRS, 2, 2 * C), ("gx", "gy"), 0, 0, tiled=True)
    gfeat, mid, out_near, out_far = border_scatter_call(side, rows, frm, dmap, gpre, split, w_t)
    near, far = swapped(out_near, "gy", True), swapped(out_far, "gy", False)
    shape = pieces.shape
    spread = sum_call(pieces.reshape(count * PIECE, 2 * C))
    spread, gpre_all, mid = lax.optimization_barrier((spread, gpre_all, mid))
    total = mid + near.astype(F32) + far.astype(F32)
    near = swapped(jnp.where(even_x, total[2], total[0]).astype(BF), "gx", True)
    far = swapped(jnp.where(even_x, total[0], total[2]).astype(BF), "gx", False)
    gathered = lax.all_to_all(spread.reshape(shape), ("gx", "gy"), 0, 0, tiled=True).reshape(-1, 2 * C)
    gfeat_all = local_scatter_call(rows, frm, dmap, gpre_all, w_t)
    coarse_out, grad_features = finish_call(coarse_all, gfeat_all, coarse, gfeat, total[1], near, far)
    grad_w_sub, grad_w_down = weights_call(float(ROWS * count) ** -0.5, gathered)
    return coarse_out[None, None], grad_features[None, None], grad_w_sub, grad_w_down


def solution(mesh):
    tile = P("gx", "gy", None, None)
    return jax.shard_map(
        shards,
        mesh=mesh,
        in_specs=(tile, P("gx", "gy"), tile, tile, tile, P(), P(), tile),
        out_specs=(tile, tile, P(), P()),
        check_vma=False,
    )
```

```python
import functools
import jax
import jax.numpy as jnp
from jax import lax
from jax.experimental import pallas as pl
from jax.sharding import PartitionSpec as P
from jax.experimental.pallas import tpu as pltpu

VB = 512
ROWS = 2048
CROWS = 512
CB = 64
NOWHERE = CROWS + 9 * CB
C = 64
K = 27
KC = K * C
L = 256
H = VB // L
CQ = 128
EDGE = 640
WIDE = VB + 2 * CB
SUB_ROWS = (K + 1) // 2 * C
USED = SUB_ROWS + 4 * C
PAIRS = 5
PIECE = 2 * PAIRS
BF = jnp.bfloat16
F32 = jnp.float32
DIRS = [3 * (k // 9) + k // 3 % 3 for k in range(K)]


def mm(a, b):
    return jnp.dot(a, b, preferred_element_type=F32)


def mm_nt(a, b):
    return lax.dot_general(a, b, (((1,), (1,)), ((), ())), preferred_element_type=F32)


def pick(cond):
    return jnp.where(cond, jnp.ones((), BF), jnp.zeros((), BF))


def table(remote, base, rows, frm):
    row_v = rows[:, 0, :]
    frm_v = frm[:, 0, :]
    if remote:
        joint = jnp.where(frm_v == 4, row_v, jnp.where(frm_v == 9, -1, row_v + VB))
    else:
        joint = jnp.where(frm_v == 4, row_v - base, -1)
    high = joint >> (L.bit_length() - 1)
    low = jnp.where(joint < 0, -1, joint & (L - 1)).astype(F32)
    return high, low


def forward_work(remote, base, feat, rows, frm, dmap, grad, halo, w_cat, wd_cat, wd_t, source):
    high, low = table(remote, base, rows, frm)
    low = low.astype(BF)
    low_ids = lax.broadcasted_iota(jnp.int32, (L, VB), 0).astype(F32).astype(BF)
    local = jnp.concatenate([feat[:, i * L:(i + 1) * L] for i in range(H)], axis=0)
    slabs = {}
    for k in range(K):
        one_hot = pick(low[k:k + 1, :] == low_ids)
        parts = [mm(local, one_hot)]
        if remote and DIRS[k] != 4:
            if DIRS[k] not in slabs:
                slab = halo[DIRS[k] % 3][DIRS[k] // 3, :, 0:VB]
                slabs[DIRS[k]] = jnp.concatenate([slab[:, i * L:(i + 1) * L] for i in range(H)], axis=0)
            parts.append(mm(slabs[DIRS[k]], one_hot))
        high_k = high[k:k + 1, :]
        pieces = [part[i * C:(i + 1) * C, :] for part in parts for i in range(H)]
        got = pieces[0]
        for i in range(1, len(pieces)):
            got = jnp.where(high_k == i, pieces[i], got)
        source[k * C:(k + 1) * C, :] = got.astype(BF)
    pre = mm(w_cat[...], source[...])
    sig = jax.nn.sigmoid(pre)
    hidden = (pre * sig).astype(BF)
    target = dmap[0:1, :]
    kind = dmap[1:2, :]
    coarse_rel = jnp.where(target < CROWS, target - base // 4, -1)
    pick_own = pick(coarse_rel == lax.broadcasted_iota(jnp.int32, (CQ, VB), 0))
    zero = jnp.zeros((), BF)
    kinds = [kind == i for i in range(8)]
    up = mm(grad[...], pick_own)
    if remote:
        edge_grad = [halo[d % 3][d // 3, :, VB:VB + CB] for d in range(9)] + [jnp.zeros((C, EDGE - 9 * CB), BF)]
        up = up + mm(jnp.concatenate(edge_grad, axis=1), pick_edges(target))
    up = up.astype(BF)
    picked_g = jnp.concatenate([jnp.where(m, up, zero) for m in kinds], axis=0)
    grad_hidden = mm(wd_t[...], picked_g)
    grad_pre = (grad_hidden * sig * (1.0 + pre * (1.0 - sig))).astype(BF)
    grad_sub = mm_nt(grad_pre, source[...])
    grad_down = mm_nt(picked_g, hidden)
    picked_h = jnp.concatenate([jnp.where(m, hidden, zero) for m in kinds], axis=0)
    contrib = mm(wd_cat[...], picked_h)
    c_hi = contrib.astype(BF)
    c_lo = (contrib - c_hi.astype(F32)).astype(BF)
    split = jnp.concatenate([c_hi, c_lo], axis=0)
    own = mm_nt(split, pick_own)
    return own[:C] + own[C:], grad_pre, grad_sub, grad_down, split


def pick_edges(target):
    return pick((target - CROWS) == lax.broadcasted_iota(jnp.int32, (EDGE, VB), 0))


def scatter_work(remote, base, rows, frm, grad_pre, w_t, spread):
    high, low = table(remote, base, rows, frm)
    low_t = jnp.concatenate([low, jnp.zeros((32 - K, VB), F32)], axis=0).T.astype(BF)
    lane_ids = lax.broadcasted_iota(jnp.int32, (VB, L), 1).astype(F32).astype(BF)
    zero = jnp.zeros((), BF)
    for k in range(K):
        high_k = high[k:k + 1, :]
        count = 2 * H if (remote and DIRS[k] != 4) else H
        masked = jnp.concatenate([jnp.where(high_k == i, grad_pre, zero) for i in range(count)], axis=0)
        out = mm(masked, pick(low_t[:, k:k + 1] == lane_ids)).astype(BF)
        for i in range(count):
            spread[k * C:(k + 1) * C, i * L:(i + 1) * L] = out[i * C:(i + 1) * C, :]
    return mm(w_t[...], spread[:, 0:VB])


def prepare_sub(w_sub, w_cat, w_t):
    w_cat[...] = jnp.concatenate([w_sub[k] for k in range(K)], axis=1)
    w_t[...] = w_sub[...].reshape(KC, C).T


def prepare_down(w_down, wd_cat, wd_t):
    wd_cat[...] = jnp.concatenate([w_down[k] for k in range(8)], axis=1)
    wd_t[...] = w_down[...].reshape(8 * C, C).T


def live_rows(dmap):
    return jnp.sum((dmap[0:1, :] < NOWHERE).astype(F32)).astype(jnp.int32)


def one_local(block, live_count, feat, rows, frm, dmap, grad, w_cat, wd_cat, wd_t, outs, source):
    coarse_o, gpre_o, gsub_o, gdown_o = outs
    live = block * VB < live_count

    @pl.when(live)
    def _():
        coarse, gpre, gsub, gdown, _ = forward_work(
            False, block * VB, feat, rows, frm, dmap, grad, None, w_cat, wd_cat, wd_t, source)
        coarse_o[...] = coarse.astype(BF)
        gpre_o[...] = gpre
        gsub_o[...] += gsub
        gdown_o[...] += gdown

    @pl.when(jnp.logical_not(live))
    def _():
        coarse_o[...] = jnp.zeros_like(coarse_o)


def views(block, feat, rows, frm, dmap, grad):
    a, b = block * VB, (block + 1) * VB
    return feat.at[:, a:b], rows.at[:, :, a:b], frm.at[:, :, a:b], dmap.at[:, a:b], grad.at[:, a // 4:b // 4]


def first_kernel(feat_h, rows_h, frm_h, dmap_h, grad_h, w_sub_h, w_down_h,
                 coarse_o, gpre_o, gsub_o, gdown_o, w_cat, w_t, wd_cat, wd_t, feat, rows, frm, dmap, grad,
                 source, w_sub, w_down, sems):
    pairs = [(w_sub_h, w_sub), (w_down_h, w_down), (dmap_h, dmap), (rows_h, rows), (frm_h, frm), (feat_h, feat),
             (grad_h, grad)]
    copies = [pltpu.make_async_copy(a, b, sems.at[i]) for i, (a, b) in enumerate(pairs)]
    for copy in copies:
        copy.start()
    gsub_o[...] = jnp.zeros_like(gsub_o)
    gdown_o[...] = jnp.zeros_like(gdown_o)
    copies[0].wait()
    prepare_sub(w_sub, w_cat, w_t)
    copies[1].wait()
    prepare_down(w_down, wd_cat, wd_t)
    for copy in copies[2:]:
        copy.wait()
    one_local(1, live_rows(dmap), *views(1, feat, rows, frm, dmap, grad), w_cat, wd_cat, wd_t,
              (coarse_o.at[:, CQ:2 * CQ], gpre_o.at[:, VB:2 * VB], gsub_o, gdown_o), source)


def rest_kernel(feat, rows, frm, dmap, grad, w_cat, wd_cat, wd_t, gsub, gdown, coarse, gpre,
                coarse_o, gpre_o, gsub_o, gdown_o, source):
    gsub_o[...] = gsub[...]
    gdown_o[...] = gdown[...]
    coarse_o[:, CQ:2 * CQ] = coarse[:, CQ:2 * CQ]
    gpre_o[:, VB:2 * VB] = gpre[:, VB:2 * VB]
    live_count = live_rows(dmap)
    for i in (2, 3):
        one_local(i, live_count, *views(i, feat, rows, frm, dmap, grad), w_cat, wd_cat, wd_t,
                  (coarse_o.at[:, i * CQ:(i + 1) * CQ], gpre_o.at[:, i * VB:(i + 1) * VB], gsub_o, gdown_o), source)


def local_scatter_kernel(rows, frm, dmap, gpre, w_t, gfeat_o, spread):
    block = pl.program_id(0) + 1
    live = block * VB < live_rows(dmap)

    @pl.when(live)
    def _():
        here = pl.ds(pl.multiple_of(block * VB, VB), VB)
        gfeat_o[...] = scatter_work(
            False, block * VB, rows.at[:, :, here], frm.at[:, :, here], gpre[:, here], w_t, spread).astype(BF)

    @pl.when(jnp.logical_not(live))
    def _():
        gfeat_o[...] = jnp.zeros_like(gfeat_o)


WHOLE = pl.BlockSpec(memory_space=pltpu.VMEM)
SCALAR = pl.BlockSpec(memory_space=pltpu.SMEM)


def full(shape):
    return WHOLE


def piped(shape):
    return pl.BlockSpec(shape, lambda i: (0,) * len(shape))


def columns(shape, first):
    return pl.BlockSpec(shape, lambda i: (0, i + first))


def index_columns(first):
    return pl.BlockSpec((K, 1, VB), lambda i: (0, 0, i + first))


def table_specs(first):
    return [columns((C, VB), first), index_columns(first), index_columns(first),
            columns((2, VB), first), columns((C, CQ), first)]


LIMIT = pltpu.CompilerParams(vmem_limit_bytes=20 << 20)
SMALL = pltpu.CompilerParams(vmem_limit_bytes=8 << 20)
SOURCE = pltpu.VMEM((KC, VB), BF)


def sd(shape, dtype):
    return jax.ShapeDtypeStruct(shape, dtype)


def first_call(feat, rows, frm, dmap, grad, w_sub, w_down):
    weights = [(C, KC), (C, KC), (C, 8 * C), (C, 8 * C)]
    arrays = [feat, rows, frm, dmap, grad]
    return pl.pallas_call(
        first_kernel,
        in_specs=[pl.BlockSpec(memory_space=pltpu.HBM)] * 7,
        out_specs=[WHOLE] * 13,
        out_shape=[sd((C, CROWS), BF), sd((C, ROWS), BF), sd((C, KC), F32), sd((8 * C, C), F32)]
        + [sd(w, BF) for w in weights] + [sd(a.shape, a.dtype) for a in arrays],
        scratch_shapes=[SOURCE, pltpu.VMEM((K, C, C), BF), pltpu.VMEM((8, C, C), BF), pltpu.SemaphoreType.DMA((7,))],
        compiler_params=LIMIT,
        name="first_local_block",
    )(*[in_hbm(a) for a in arrays + [w_sub, w_down]])


def rest_call(feat, rows, frm, dmap, grad, w_cat, wd_cat, wd_t, gsub, gdown, coarse_all, gpre_all):
    return pl.pallas_call(
        rest_kernel,
        in_specs=[WHOLE] * 12,
        out_specs=[WHOLE] * 4,
        out_shape=[sd((C, CROWS), BF), sd((C, ROWS), BF), sd((C, KC), F32), sd((8 * C, C), F32)],
        scratch_shapes=[SOURCE],
        input_output_aliases={10: 0, 11: 1, 8: 2, 9: 3},
        compiler_params=LIMIT,
        name="other_local_blocks",
    )(feat, rows, frm, dmap, grad, w_cat, wd_cat, wd_t, gsub, gdown, coarse_all, gpre_all)


def local_scatter_call(rows, frm, dmap, gpre_all, w_t):
    return pl.pallas_call(
        local_scatter_kernel,
        grid=(3,),
        in_specs=[WHOLE] * 5,
        out_specs=columns((C, VB), 1),
        out_shape=sd((C, ROWS), BF),
        scratch_shapes=[SOURCE],
        compiler_params=LIMIT,
        name="local_scatter_blocks",
    )(rows, frm, dmap, gpre_all, w_t)


def in_hbm(array):
    return pltpu.with_memory_space_constraint(array, pltpu.HBM)


def border_pack_kernel(feat, grad, out, sems):
    a = pltpu.make_async_copy(feat.at[:, 0:VB], out.at[:, 0:VB], sems.at[0])
    b = pltpu.make_async_copy(grad.at[:, 0:CQ], out.at[:, VB:], sems.at[1])
    a.start()
    b.start()
    a.wait()
    b.wait()


def border_pack(feat, grad):
    return pl.pallas_call(
        border_pack_kernel,
        in_specs=[pl.BlockSpec(memory_space=pltpu.HBM)] * 2,
        out_specs=WHOLE,
        out_shape=sd((C, WIDE), BF),
        scratch_shapes=[pltpu.SemaphoreType.DMA((2,))],
        compiler_params=SMALL,
        name="pack_border",
    )(in_hbm(feat), in_hbm(grad))


def sum_kernel(pieces, out):
    rows = pieces.shape[0]
    span = 4 * PIECE
    total = jnp.sum(pieces[...].astype(F32).reshape(rows // span, span, 2 * C), axis=0)
    mine = total[0:PIECE]
    for i in range(1, 4):
        mine = mine + total[i * PIECE:(i + 1) * PIECE]
    tiled = jnp.concatenate([mine] * 8, axis=0).astype(BF)
    for i in range(rows // (8 * PIECE)):
        out[i * 8 * PIECE:(i + 1) * 8 * PIECE, :] = tiled


def sum_call(pieces):
    return pl.pallas_call(
        sum_kernel,
        grid=(1,),
        in_specs=[full(pieces.shape)],
        out_specs=piped(pieces.shape),
        out_shape=jax.ShapeDtypeStruct(pieces.shape, BF),
        compiler_params=SMALL,
        name="sum_pieces",
    )(pieces)


def border_kernel(side, feat, rows, frm, dmap, grad, near, column, far, w_cat, wd_cat, wd_t, gsub, gdown,
                  coarse_o, packed_o, gpre_o, split_o, source, below, above):
    feat, rows, frm, dmap, grad = views(0, feat, rows, frm, dmap, grad)
    even = side[0] == 1
    below[...] = jnp.where(even, far[...], near[...])
    above[...] = jnp.where(even, near[...], far[...])
    coarse, gpre, dsub, ddown, split = forward_work(
        True, 0, feat, rows, frm, dmap, grad, (below, column, above), w_cat, wd_cat, wd_t, source)
    coarse_o[...] = coarse
    gpre_o[...] = gpre
    split_o[...] = split
    total = gsub[...] + dsub
    for t in range(K // 2):
        packed_o[t * C:(t + 1) * C, :] = total[:, t * 2 * C:(t + 1) * 2 * C].astype(BF)
    last = jnp.concatenate([total[:, KC - C:], jnp.zeros((C, C), F32)], axis=1)
    packed_o[K // 2 * C:SUB_ROWS, :] = last.astype(BF)
    down = gdown[...] + ddown
    packed_o[SUB_ROWS:USED, :] = jnp.concatenate([down[:4 * C], down[4 * C:]], axis=1).astype(BF)
    packed_o[USED:, :] = jnp.zeros((packed_o.shape[0] - USED, 2 * C), BF)


def border_call(count, side, feat, rows, frm, dmap, grad, near, column, far, w_cat, wd_cat, wd_t, gsub, gdown):
    slab = full((3, C, WIDE))
    return pl.pallas_call(
        border_kernel,
        grid=(1,),
        in_specs=[SCALAR] + [WHOLE] * 5 + [slab, slab, slab, full((C, KC)), full((C, 8 * C)), full((C, 8 * C)),
                                   full((C, KC)), full((8 * C, C))],
        out_specs=[full((C, CQ)), piped((count * PIECE, 2 * C)), full((C, VB)), full((2 * C, VB))],
        out_shape=[sd((C, CQ), F32), sd((count * PIECE, 2 * C), BF), sd((C, VB), BF), sd((2 * C, VB), BF)],
        scratch_shapes=[SOURCE, pltpu.VMEM((3, C, WIDE), BF), pltpu.VMEM((3, C, WIDE), BF)],
        compiler_params=LIMIT,
        name="border_block",
    )(side, feat, rows, frm, dmap, grad, near, column, far, w_cat, wd_cat, wd_t, gsub, gdown)


def border_scatter_kernel(side, rows, frm, dmap, gpre, split, w_t, gfeat_o, mid_o, near_o, far_o, spread):
    gfeat_o[...] = scatter_work(True, 0, rows.at[:, :, 0:VB], frm.at[:, :, 0:VB], gpre[...], w_t, spread)
    both = mm_nt(split[...], pick_edges(dmap[0:1, 0:VB]))
    edge = both[:C] + both[C:]
    even = side[0] == 1

    def slab(d):
        a = 9 * (d // 3) + 3 * (d % 3)
        a, b = a * C, (a + 3) * C
        outward = jnp.zeros((C, VB), F32) if d == 4 else mm(w_t[:, a:b], spread[a:b, VB:2 * VB])
        return jnp.concatenate([outward, edge[:, d * CB:(d + 1) * CB], jnp.zeros((C, CB), F32)], axis=1)

    for x in range(3):
        down, up = slab(3 * x).astype(BF), slab(3 * x + 2).astype(BF)
        mid_o[x] = slab(3 * x + 1)
        near_o[x] = jnp.where(even, up, down)
        far_o[x] = jnp.where(even, down, up)


def border_scatter_call(side, rows, frm, dmap, gpre, split, w_t):
    slab = (3, C, WIDE)
    return pl.pallas_call(
        border_scatter_kernel,
        grid=(1,),
        in_specs=[SCALAR, WHOLE, WHOLE, WHOLE, full((C, VB)), full((2 * C, VB)),
                  full((C, KC))],
        out_specs=[full((C, VB)), full(slab), full(slab), full(slab)],
        out_shape=[sd((C, VB), F32), sd(slab, F32), sd(slab, BF), sd(slab, BF)],
        scratch_shapes=[pltpu.VMEM((KC, 2 * VB), BF)],
        compiler_params=LIMIT,
        name="border_scatter_block",
    )(side, rows, frm, dmap, gpre, split, w_t)


def finish_kernel(coarse_i, gfeat_i, coarse, gfeat, total, left, right, coarse_o, gfeat_o):
    inc = total[...] + left[...].astype(F32) + right[...].astype(F32)
    gfeat_o[...] = (gfeat[...] + inc[:, 0:VB]).astype(BF)
    coarse_o[:, 0:CB] = (coarse[:, 0:CB] + inc[:, VB:VB + CB]).astype(BF)
    coarse_o[:, CB:CQ] = coarse[:, CB:].astype(BF)
    coarse_o[:, CQ:] = coarse_i[:, CQ:]


def finish_call(coarse_all, gfeat_all, coarse, gfeat, total, left, right):
    return pl.pallas_call(
        finish_kernel,
        grid=(1,),
        in_specs=[
            WHOLE, pl.BlockSpec(memory_space=pl.ANY),
            full((C, CQ)), full((C, VB)), full((C, WIDE)), full((C, WIDE)), full((C, WIDE)),
        ],
        out_specs=[piped((C, CROWS)), pl.BlockSpec((C, VB), lambda i: (0, 0))],
        out_shape=[sd((C, CROWS), BF), sd((C, ROWS), BF)],
        input_output_aliases={1: 1},
        compiler_params=SMALL,
        name="add_incoming",
    )(coarse_all, gfeat_all, coarse, gfeat, total, left, right)


def weights_kernel(scale, packed, gsub_o, gdown_o):
    for k in range(K):
        r, c = k // 2 * C, k % 2 * C
        gsub_o[k] = packed[r:r + C, c:c + C].astype(F32) * scale
    for k in range(8):
        r, c = SUB_ROWS + k % 4 * C, k // 4 * C
        gdown_o[k] = packed[r:r + C, c:c + C].astype(F32) * scale


def weights_call(scale, packed):
    return pl.pallas_call(
        functools.partial(weights_kernel, scale),
        grid=(1,),
        in_specs=[full(packed.shape)],
        out_specs=[piped((K, C, C)), piped((8, C, C))],
        out_shape=[sd((K, C, C), F32), sd((8, C, C), F32)],
        compiler_params=SMALL,
        name="unpack_weights",
    )(packed)


def swapped(block, axis, first):
    n = lax.axis_size(axis)
    pairs = [(i, i + 1) for i in range(0 if first else 1, n - 1, 2)]
    return lax.ppermute(block, axis, pairs + [(b, a) for a, b in pairs])


def shards(features, counts, sub_rows, sub_from, down_map, w_sub, w_down, cotangent):
    feat = features[0, 0]
    grad = cotangent[0, 0]
    rows, frm, dmap = sub_rows.reshape(K, 1, ROWS), sub_from.reshape(K, 1, ROWS), down_map[0, 0]
    nx, ny = lax.axis_size("gx"), lax.axis_size("gy")
    count = nx * ny
    border = border_pack(feat, grad)
    even_x, even_y = lax.axis_index("gx") % 2 == 0, lax.axis_index("gy") % 2 == 0
    side = even_y.astype(jnp.int32).reshape(1)
    near, far = swapped(border, "gx", True), swapped(border, "gx", False)
    (coarse_all, gpre_all, gsub, gdown, w_cat, w_t, wd_cat, wd_t, feat, rows, frm, dmap, grad) = first_call(
        feat, rows, frm, dmap, grad, w_sub, w_down)
    near, far, gsub = lax.optimization_barrier((near, far, gsub))
    column = jnp.stack([jnp.where(even_x, far, near), border, jnp.where(even_x, near, far)])
    near, far = swapped(column, "gy", True), swapped(column, "gy", False)
    coarse_all, gpre_all, gsub, gdown = rest_call(
        feat, rows, frm, dmap, grad, w_cat, wd_cat, wd_t, gsub, gdown, coarse_all, gpre_all)
    coarse, packed, gpre, split = border_call(
        count, side, feat, rows, frm, dmap, grad, near, column, far, w_cat, wd_cat, wd_t, gsub, gdown)
    pieces = lax.all_to_all(packed.reshape(count, PAIRS, 2, 2 * C), ("gx", "gy"), 0, 0, tiled=True)
    gfeat, mid, out_near, out_far = border_scatter_call(side, rows, frm, dmap, gpre, split, w_t)
    near, far = swapped(out_near, "gy", True), swapped(out_far, "gy", False)
    shape = pieces.shape
    spread = sum_call(pieces.reshape(count * PIECE, 2 * C))
    spread, gpre_all, mid = lax.optimization_barrier((spread, gpre_all, mid))
    total = mid + near.astype(F32) + far.astype(F32)
    near = swapped(jnp.where(even_x, total[2], total[0]).astype(BF), "gx", True)
    far = swapped(jnp.where(even_x, total[0], total[2]).astype(BF), "gx", False)
    gathered = lax.all_to_all(spread.reshape(shape), ("gx", "gy"), 0, 0, tiled=True).reshape(-1, 2 * C)
    gfeat_all = local_scatter_call(rows, frm, dmap, gpre_all, w_t)
    coarse_out, grad_features = finish_call(coarse_all, gfeat_all, coarse, gfeat, total[1], near, far)
    grad_w_sub, grad_w_down = weights_call(float(ROWS * count) ** -0.5, gathered)
    return coarse_out[None, None], grad_features[None, None], grad_w_sub, grad_w_down


def solution(mesh):
    tile = P("gx", "gy", None, None)
    return jax.shard_map(
        shards,
        mesh=mesh,
        in_specs=(tile, P("gx", "gy"), tile, tile, tile, P(), P(), tile),
        out_specs=(tile, tile, P(), P()),
        check_vma=False,
    )
```

```python
import functools
import jax
import jax.numpy as jnp
from jax import lax
from jax.experimental import pallas as pl
from jax.sharding import PartitionSpec as P
from jax.experimental.pallas import tpu as pltpu

VB = 512
ROWS = 2048
CROWS = 512
CB = 64
NOWHERE = CROWS + 9 * CB
C = 64
K = 27
KC = K * C
L = 256
H = VB // L
CQ = 128
EDGE = 640
WIDE = VB + 2 * CB
SUB_ROWS = (K + 1) // 2 * C
USED = SUB_ROWS + 4 * C
PAIRS = 5
PIECE = 2 * PAIRS
BF = jnp.bfloat16
F32 = jnp.float32
DIRS = [3 * (k // 9) + k // 3 % 3 for k in range(K)]


def mm(a, b):
    return jnp.dot(a, b, preferred_element_type=F32)


def mm_nt(a, b):
    return lax.dot_general(a, b, (((1,), (1,)), ((), ())), preferred_element_type=F32)


def pick(cond):
    return jnp.where(cond, jnp.ones((), BF), jnp.zeros((), BF))


def table(remote, base, rows, frm):
    row_v = rows[:, 0, :]
    frm_v = frm[:, 0, :]
    if remote:
        joint = jnp.where(frm_v == 4, row_v, jnp.where(frm_v == 9, -1, row_v + VB))
    else:
        joint = jnp.where(frm_v == 4, row_v - base, -1)
    high = joint >> (L.bit_length() - 1)
    low = jnp.where(joint < 0, -1, joint & (L - 1)).astype(F32)
    return high, low


def forward_work(remote, base, feat, rows, frm, dmap, grad, halo, w_cat, wd_cat, wd_t, source):
    high, low = table(remote, base, rows, frm)
    low = low.astype(BF)
    low_ids = lax.broadcasted_iota(jnp.int32, (L, VB), 0).astype(F32).astype(BF)
    local = jnp.concatenate([feat[:, i * L:(i + 1) * L] for i in range(H)], axis=0)
    slabs = {}
    for k in range(K):
        one_hot = pick(low[k:k + 1, :] == low_ids)
        parts = [mm(local, one_hot)]
        if remote and DIRS[k] != 4:
            if DIRS[k] not in slabs:
                slab = halo[DIRS[k] % 3][DIRS[k] // 3, :, 0:VB]
                slabs[DIRS[k]] = jnp.concatenate([slab[:, i * L:(i + 1) * L] for i in range(H)], axis=0)
            parts.append(mm(slabs[DIRS[k]], one_hot))
        high_k = high[k:k + 1, :]
        pieces = [part[i * C:(i + 1) * C, :] for part in parts for i in range(H)]
        got = pieces[0]
        for i in range(1, len(pieces)):
            got = jnp.where(high_k == i, pieces[i], got)
        source[k * C:(k + 1) * C, :] = got.astype(BF)
    pre = mm(w_cat[...], source[...])
    sig = jax.nn.sigmoid(pre)
    hidden = (pre * sig).astype(BF)
    target = dmap[0:1, :]
    kind = dmap[1:2, :]
    coarse_rel = jnp.where(target < CROWS, target - base // 4, -1)
    pick_own = pick(coarse_rel == lax.broadcasted_iota(jnp.int32, (CQ, VB), 0))
    zero = jnp.zeros((), BF)
    kinds = [kind == i for i in range(8)]
    up = mm(grad[...], pick_own)
    if remote:
        edge_grad = [halo[d % 3][d // 3, :, VB:VB + CB] for d in range(9)] + [jnp.zeros((C, EDGE - 9 * CB), BF)]
        up = up + mm(jnp.concatenate(edge_grad, axis=1), pick_edges(target))
    up = up.astype(BF)
    picked_g = jnp.concatenate([jnp.where(m, up, zero) for m in kinds], axis=0)
    grad_hidden = mm(wd_t[...], picked_g)
    grad_pre = (grad_hidden * sig * (1.0 + pre * (1.0 - sig))).astype(BF)
    grad_sub = mm_nt(grad_pre, source[...])
    grad_down = mm_nt(picked_g, hidden)
    if remote:
        return hidden, grad_pre, grad_sub, grad_down
    coarse, _ = down_convolution(hidden, kinds, pick_own, wd_cat)
    return coarse, grad_pre, grad_sub, grad_down


def down_convolution(hidden, kinds, pick_own, wd_cat):
    picked_h = jnp.concatenate([jnp.where(m, hidden, jnp.zeros((), BF)) for m in kinds], axis=0)
    contrib = mm(wd_cat[...], picked_h)
    c_hi = contrib.astype(BF)
    c_lo = (contrib - c_hi.astype(F32)).astype(BF)
    split = jnp.concatenate([c_hi, c_lo], axis=0)
    own = mm_nt(split, pick_own)
    return own[:C] + own[C:], split


def pick_edges(target):
    return pick((target - CROWS) == lax.broadcasted_iota(jnp.int32, (EDGE, VB), 0))


def scatter_work(remote, base, rows, frm, grad_pre, w_t, spread):
    high, low = table(remote, base, rows, frm)
    low_t = jnp.concatenate([low, jnp.zeros((32 - K, VB), F32)], axis=0).T.astype(BF)
    lane_ids = lax.broadcasted_iota(jnp.int32, (VB, L), 1).astype(F32).astype(BF)
    zero = jnp.zeros((), BF)
    for k in range(K):
        high_k = high[k:k + 1, :]
        count = 2 * H if (remote and DIRS[k] != 4) else H
        masked = jnp.concatenate([jnp.where(high_k == i, grad_pre, zero) for i in range(count)], axis=0)
        out = mm(masked, pick(low_t[:, k:k + 1] == lane_ids)).astype(BF)
        for i in range(count):
            spread[k * C:(k + 1) * C, i * L:(i + 1) * L] = out[i * C:(i + 1) * C, :]
    return mm(w_t[...], spread[:, 0:VB])


def prepare_sub(w_sub, w_cat, w_t):
    w_cat[...] = jnp.concatenate([w_sub[k] for k in range(K)], axis=1)
    w_t[...] = w_sub[...].reshape(KC, C).T


def prepare_down(w_down, wd_cat, wd_t):
    wd_cat[...] = jnp.concatenate([w_down[k] for k in range(8)], axis=1)
    wd_t[...] = w_down[...].reshape(8 * C, C).T


def live_rows(dmap):
    return jnp.sum((dmap[0:1, :] < NOWHERE).astype(F32)).astype(jnp.int32)


def one_local(block, live_count, feat, rows, frm, dmap, grad, w_cat, wd_cat, wd_t, outs, source):
    coarse_o, gpre_o, gsub_o, gdown_o = outs
    live = block * VB < live_count

    @pl.when(live)
    def _():
        coarse, gpre, gsub, gdown = forward_work(
            False, block * VB, feat, rows, frm, dmap, grad, None, w_cat, wd_cat, wd_t, source)
        coarse_o[...] = coarse.astype(BF)
        gpre_o[...] = gpre
        gsub_o[...] += gsub
        gdown_o[...] += gdown

    @pl.when(jnp.logical_not(live))
    def _():
        coarse_o[...] = jnp.zeros_like(coarse_o)


def views(block, feat, rows, frm, dmap, grad):
    a, b = block * VB, (block + 1) * VB
    return feat.at[:, a:b], rows.at[:, :, a:b], frm.at[:, :, a:b], dmap.at[:, a:b], grad.at[:, a // 4:b // 4]


def first_kernel(feat_h, rows_h, frm_h, dmap_h, grad_h, w_sub_h, w_down_h,
                 coarse_o, gpre_o, gsub_o, gdown_o, w_cat, w_t, wd_cat, wd_t, feat, rows, frm, dmap, grad,
                 source, w_sub, w_down, sems):
    pairs = [(w_sub_h, w_sub), (w_down_h, w_down), (dmap_h, dmap), (rows_h, rows), (frm_h, frm), (feat_h, feat),
             (grad_h, grad)]
    copies = [pltpu.make_async_copy(a, b, sems.at[i]) for i, (a, b) in enumerate(pairs)]
    for copy in copies:
        copy.start()
    gsub_o[...] = jnp.zeros_like(gsub_o)
    gdown_o[...] = jnp.zeros_like(gdown_o)
    copies[0].wait()
    prepare_sub(w_sub, w_cat, w_t)
    copies[1].wait()
    prepare_down(w_down, wd_cat, wd_t)
    for copy in copies[2:]:
        copy.wait()
    one_local(1, live_rows(dmap), *views(1, feat, rows, frm, dmap, grad), w_cat, wd_cat, wd_t,
              (coarse_o.at[:, CQ:2 * CQ], gpre_o.at[:, VB:2 * VB], gsub_o, gdown_o), source)


def rest_kernel(feat, rows, frm, dmap, grad, w_cat, wd_cat, wd_t, gsub, gdown, coarse, gpre,
                coarse_o, gpre_o, gsub_o, gdown_o, source):
    gsub_o[...] = gsub[...]
    gdown_o[...] = gdown[...]
    coarse_o[:, CQ:2 * CQ] = coarse[:, CQ:2 * CQ]
    gpre_o[:, VB:2 * VB] = gpre[:, VB:2 * VB]
    live_count = live_rows(dmap)
    for i in (2, 3):
        one_local(i, live_count, *views(i, feat, rows, frm, dmap, grad), w_cat, wd_cat, wd_t,
                  (coarse_o.at[:, i * CQ:(i + 1) * CQ], gpre_o.at[:, i * VB:(i + 1) * VB], gsub_o, gdown_o), source)


def local_scatter_kernel(rows, frm, dmap, gpre, w_t, gfeat_o, spread):
    block = pl.program_id(0) + 1
    live = block * VB < live_rows(dmap)

    @pl.when(live)
    def _():
        here = pl.ds(pl.multiple_of(block * VB, VB), VB)
        gfeat_o[...] = scatter_work(
            False, block * VB, rows.at[:, :, here], frm.at[:, :, here], gpre[:, here], w_t, spread).astype(BF)

    @pl.when(jnp.logical_not(live))
    def _():
        gfeat_o[...] = jnp.zeros_like(gfeat_o)


WHOLE = pl.BlockSpec(memory_space=pltpu.VMEM)
SCALAR = pl.BlockSpec(memory_space=pltpu.SMEM)


def full(shape):
    return WHOLE


def piped(shape):
    return pl.BlockSpec(shape, lambda i: (0,) * len(shape))


def columns(shape, first):
    return pl.BlockSpec(shape, lambda i: (0, i + first))


def index_columns(first):
    return pl.BlockSpec((K, 1, VB), lambda i: (0, 0, i + first))


def table_specs(first):
    return [columns((C, VB), first), index_columns(first), index_columns(first),
            columns((2, VB), first), columns((C, CQ), first)]


LIMIT = pltpu.CompilerParams(vmem_limit_bytes=20 << 20)
SMALL = pltpu.CompilerParams(vmem_limit_bytes=8 << 20)
SOURCE = pltpu.VMEM((KC, VB), BF)


def sd(shape, dtype):
    return jax.ShapeDtypeStruct(shape, dtype)


def first_call(feat, rows, frm, dmap, grad, w_sub, w_down):
    weights = [(C, KC), (C, KC), (C, 8 * C), (C, 8 * C)]
    arrays = [feat, rows, frm, dmap, grad]
    return pl.pallas_call(
        first_kernel,
        in_specs=[pl.BlockSpec(memory_space=pltpu.HBM)] * 7,
        out_specs=[WHOLE] * 13,
        out_shape=[sd((C, CROWS), BF), sd((C, ROWS), BF), sd((C, KC), F32), sd((8 * C, C), F32)]
        + [sd(w, BF) for w in weights] + [sd(a.shape, a.dtype) for a in arrays],
        scratch_shapes=[SOURCE, pltpu.VMEM((K, C, C), BF), pltpu.VMEM((8, C, C), BF), pltpu.SemaphoreType.DMA((7,))],
        compiler_params=LIMIT,
        name="first_local_block",
    )(*[in_hbm(a) for a in arrays + [w_sub, w_down]])


def rest_call(feat, rows, frm, dmap, grad, w_cat, wd_cat, wd_t, gsub, gdown, coarse_all, gpre_all):
    return pl.pallas_call(
        rest_kernel,
        in_specs=[WHOLE] * 12,
        out_specs=[WHOLE] * 4,
        out_shape=[sd((C, CROWS), BF), sd((C, ROWS), BF), sd((C, KC), F32), sd((8 * C, C), F32)],
        scratch_shapes=[SOURCE],
        input_output_aliases={10: 0, 11: 1, 8: 2, 9: 3},
        compiler_params=LIMIT,
        name="other_local_blocks",
    )(feat, rows, frm, dmap, grad, w_cat, wd_cat, wd_t, gsub, gdown, coarse_all, gpre_all)


def local_scatter_call(rows, frm, dmap, gpre_all, w_t):
    return pl.pallas_call(
        local_scatter_kernel,
        grid=(3,),
        in_specs=[WHOLE] * 5,
        out_specs=columns((C, VB), 1),
        out_shape=sd((C, ROWS), BF),
        scratch_shapes=[SOURCE],
        compiler_params=LIMIT,
        name="local_scatter_blocks",
    )(rows, frm, dmap, gpre_all, w_t)


def in_hbm(array):
    return pltpu.with_memory_space_constraint(array, pltpu.HBM)


def border_pack_kernel(feat, grad, out, sems):
    a = pltpu.make_async_copy(feat.at[:, 0:VB], out.at[:, 0:VB], sems.at[0])
    b = pltpu.make_async_copy(grad.at[:, 0:CQ], out.at[:, VB:], sems.at[1])
    a.start()
    b.start()
    a.wait()
    b.wait()


def border_pack(feat, grad):
    return pl.pallas_call(
        border_pack_kernel,
        in_specs=[pl.BlockSpec(memory_space=pltpu.HBM)] * 2,
        out_specs=WHOLE,
        out_shape=sd((C, WIDE), BF),
        scratch_shapes=[pltpu.SemaphoreType.DMA((2,))],
        compiler_params=SMALL,
        name="pack_border",
    )(in_hbm(feat), in_hbm(grad))


def sum_kernel(pieces, out):
    rows = pieces.shape[0]
    span = 4 * PIECE
    total = jnp.sum(pieces[...].astype(F32).reshape(rows // span, span, 2 * C), axis=0)
    mine = total[0:PIECE]
    for i in range(1, 4):
        mine = mine + total[i * PIECE:(i + 1) * PIECE]
    tiled = jnp.concatenate([mine] * 8, axis=0).astype(BF)
    for i in range(rows // (8 * PIECE)):
        out[i * 8 * PIECE:(i + 1) * 8 * PIECE, :] = tiled


def sum_call(pieces):
    return pl.pallas_call(
        sum_kernel,
        grid=(1,),
        in_specs=[full(pieces.shape)],
        out_specs=piped(pieces.shape),
        out_shape=jax.ShapeDtypeStruct(pieces.shape, BF),
        compiler_params=SMALL,
        name="sum_pieces",
    )(pieces)


def border_kernel(side, feat, rows, frm, dmap, grad, near, column, far, w_cat, wd_cat, wd_t, gsub, gdown,
                  packed_o, gpre_o, hidden_o, source, below, above):
    feat, rows, frm, dmap, grad = views(0, feat, rows, frm, dmap, grad)
    even = side[0] == 1
    below[...] = jnp.where(even, far[...], near[...])
    above[...] = jnp.where(even, near[...], far[...])
    hidden, gpre, dsub, ddown = forward_work(
        True, 0, feat, rows, frm, dmap, grad, (below, column, above), w_cat, wd_cat, wd_t, source)
    gpre_o[...] = gpre
    hidden_o[...] = hidden
    total = gsub[...] + dsub
    for t in range(K // 2):
        packed_o[t * C:(t + 1) * C, :] = total[:, t * 2 * C:(t + 1) * 2 * C].astype(BF)
    last = jnp.concatenate([total[:, KC - C:], jnp.zeros((C, C), F32)], axis=1)
    packed_o[K // 2 * C:SUB_ROWS, :] = last.astype(BF)
    down = gdown[...] + ddown
    packed_o[SUB_ROWS:USED, :] = jnp.concatenate([down[:4 * C], down[4 * C:]], axis=1).astype(BF)
    packed_o[USED:, :] = jnp.zeros((packed_o.shape[0] - USED, 2 * C), BF)


def border_call(count, side, feat, rows, frm, dmap, grad, near, column, far, w_cat, wd_cat, wd_t, gsub, gdown):
    slab = full((3, C, WIDE))
    return pl.pallas_call(
        border_kernel,
        grid=(1,),
        in_specs=[SCALAR] + [WHOLE] * 5 + [slab, slab, slab, full((C, KC)), full((C, 8 * C)), full((C, 8 * C)),
                                   full((C, KC)), full((8 * C, C))],
        out_specs=[piped((count * PIECE, 2 * C)), full((C, VB)), full((C, VB))],
        out_shape=[sd((count * PIECE, 2 * C), BF), sd((C, VB), BF), sd((C, VB), BF)],
        scratch_shapes=[SOURCE, pltpu.VMEM((3, C, WIDE), BF), pltpu.VMEM((3, C, WIDE), BF)],
        compiler_params=LIMIT,
        name="border_block",
    )(side, feat, rows, frm, dmap, grad, near, column, far, w_cat, wd_cat, wd_t, gsub, gdown)


def border_scatter_kernel(side, rows, frm, dmap, gpre, hidden, w_t, wd_cat, coarse_o, gfeat_o, mid_o, near_o, far_o, spread):
    gfeat_o[...] = scatter_work(True, 0, rows.at[:, :, 0:VB], frm.at[:, :, 0:VB], gpre[...], w_t, spread)
    target = dmap[0:1, 0:VB]
    kinds = [dmap[1:2, 0:VB] == i for i in range(8)]
    pick_own = pick(target == lax.broadcasted_iota(jnp.int32, (CQ, VB), 0))
    coarse_o[...], split = down_convolution(hidden[...], kinds, pick_own, wd_cat)
    both = mm_nt(split, pick_edges(target))
    edge = both[:C] + both[C:]
    even = side[0] == 1

    def slab(d):
        a = 9 * (d // 3) + 3 * (d % 3)
        a, b = a * C, (a + 3) * C
        outward = jnp.zeros((C, VB), F32) if d == 4 else mm(w_t[:, a:b], spread[a:b, VB:2 * VB])
        return jnp.concatenate([outward, edge[:, d * CB:(d + 1) * CB], jnp.zeros((C, CB), F32)], axis=1)

    for x in range(3):
        down, up = slab(3 * x).astype(BF), slab(3 * x + 2).astype(BF)
        mid_o[x] = slab(3 * x + 1)
        near_o[x] = jnp.where(even, up, down)
        far_o[x] = jnp.where(even, down, up)


def border_scatter_call(side, rows, frm, dmap, gpre, hidden, w_t, wd_cat):
    slab = (3, C, WIDE)
    return pl.pallas_call(
        border_scatter_kernel,
        grid=(1,),
        in_specs=[SCALAR] + [WHOLE] * 7,
        out_specs=[WHOLE] * 5,
        out_shape=[sd((C, CQ), F32), sd((C, VB), F32), sd(slab, F32), sd(slab, BF), sd(slab, BF)],
        scratch_shapes=[pltpu.VMEM((KC, 2 * VB), BF)],
        compiler_params=LIMIT,
        name="border_scatter_block",
    )(side, rows, frm, dmap, gpre, hidden, w_t, wd_cat)


def finish_kernel(coarse_i, gfeat_i, coarse, gfeat, total, left, right, coarse_o, gfeat_o):
    inc = total[...] + left[...].astype(F32) + right[...].astype(F32)
    gfeat_o[...] = (gfeat[...] + inc[:, 0:VB]).astype(BF)
    coarse_o[:, 0:CB] = (coarse[:, 0:CB] + inc[:, VB:VB + CB]).astype(BF)
    coarse_o[:, CB:CQ] = coarse[:, CB:].astype(BF)
    coarse_o[:, CQ:] = coarse_i[:, CQ:]


def finish_call(coarse_all, gfeat_all, coarse, gfeat, total, left, right):
    return pl.pallas_call(
        finish_kernel,
        grid=(1,),
        in_specs=[
            WHOLE, pl.BlockSpec(memory_space=pl.ANY),
            full((C, CQ)), full((C, VB)), full((C, WIDE)), full((C, WIDE)), full((C, WIDE)),
        ],
        out_specs=[piped((C, CROWS)), pl.BlockSpec((C, VB), lambda i: (0, 0))],
        out_shape=[sd((C, CROWS), BF), sd((C, ROWS), BF)],
        input_output_aliases={1: 1},
        compiler_params=SMALL,
        name="add_incoming",
    )(coarse_all, gfeat_all, coarse, gfeat, total, left, right)


def weights_kernel(scale, packed, gsub_o, gdown_o):
    for k in range(K):
        r, c = k // 2 * C, k % 2 * C
        gsub_o[k] = packed[r:r + C, c:c + C].astype(F32) * scale
    for k in range(8):
        r, c = SUB_ROWS + k % 4 * C, k // 4 * C
        gdown_o[k] = packed[r:r + C, c:c + C].astype(F32) * scale


def weights_call(scale, packed):
    return pl.pallas_call(
        functools.partial(weights_kernel, scale),
        grid=(1,),
        in_specs=[full(packed.shape)],
        out_specs=[piped((K, C, C)), piped((8, C, C))],
        out_shape=[sd((K, C, C), F32), sd((8, C, C), F32)],
        compiler_params=SMALL,
        name="unpack_weights",
    )(packed)


def swapped(block, axis, first):
    n = lax.axis_size(axis)
    pairs = [(i, i + 1) for i in range(0 if first else 1, n - 1, 2)]
    return lax.ppermute(block, axis, pairs + [(b, a) for a, b in pairs])


def shards(features, counts, sub_rows, sub_from, down_map, w_sub, w_down, cotangent):
    feat = features[0, 0]
    grad = cotangent[0, 0]
    rows, frm, dmap = sub_rows.reshape(K, 1, ROWS), sub_from.reshape(K, 1, ROWS), down_map[0, 0]
    nx, ny = lax.axis_size("gx"), lax.axis_size("gy")
    count = nx * ny
    border = border_pack(feat, grad)
    even_x, even_y = lax.axis_index("gx") % 2 == 0, lax.axis_index("gy") % 2 == 0
    side = even_y.astype(jnp.int32).reshape(1)
    near, far = swapped(border, "gx", True), swapped(border, "gx", False)
    (coarse_all, gpre_all, gsub, gdown, w_cat, w_t, wd_cat, wd_t, feat, rows, frm, dmap, grad) = first_call(
        feat, rows, frm, dmap, grad, w_sub, w_down)
    near, far, gsub = lax.optimization_barrier((near, far, gsub))
    column = jnp.stack([jnp.where(even_x, far, near), border, jnp.where(even_x, near, far)])
    near, far = swapped(column, "gy", True), swapped(column, "gy", False)
    coarse_all, gpre_all, gsub, gdown = rest_call(
        feat, rows, frm, dmap, grad, w_cat, wd_cat, wd_t, gsub, gdown, coarse_all, gpre_all)
    packed, gpre, hidden = border_call(
        count, side, feat, rows, frm, dmap, grad, near, column, far, w_cat, wd_cat, wd_t, gsub, gdown)
    pieces = lax.all_to_all(packed.reshape(count, PAIRS, 2, 2 * C), ("gx", "gy"), 0, 0, tiled=True)
    coarse, gfeat, mid, out_near, out_far = border_scatter_call(
        side, rows, frm, dmap, gpre, hidden, w_t, wd_cat)
    near, far = swapped(out_near, "gy", True), swapped(out_far, "gy", False)
    shape = pieces.shape
    spread = sum_call(pieces.reshape(count * PIECE, 2 * C))
    spread, gpre_all, mid = lax.optimization_barrier((spread, gpre_all, mid))
    total = mid + near.astype(F32) + far.astype(F32)
    near = swapped(jnp.where(even_x, total[2], total[0]).astype(BF), "gx", True)
    far = swapped(jnp.where(even_x, total[0], total[2]).astype(BF), "gx", False)
    gathered = lax.all_to_all(spread.reshape(shape), ("gx", "gy"), 0, 0, tiled=True).reshape(-1, 2 * C)
    gfeat_all = local_scatter_call(rows, frm, dmap, gpre_all, w_t)
    coarse_out, grad_features = finish_call(coarse_all, gfeat_all, coarse, gfeat, total[1], near, far)
    grad_w_sub, grad_w_down = weights_call(float(ROWS * count) ** -0.5, gathered)
    return coarse_out[None, None], grad_features[None, None], grad_w_sub, grad_w_down


def solution(mesh):
    tile = P("gx", "gy", None, None)
    return jax.shard_map(
        shards,
        mesh=mesh,
        in_specs=(tile, P("gx", "gy"), tile, tile, tile, P(), P(), tile),
        out_specs=(tile, tile, P(), P()),
        check_vma=False,
    )
```
